32 devices in a mesh: rows: 2 (over y), dp: 16 (over z, x, core).
Axes of the slice: x: 2, y: 2, z: 4, core: 2. Of those that a mesh axis runs over, the one named last changes fastest.
Arguments:
- images: bfloat16 [48, 14, 14, 512], P('dp', 'rows'), may hold values from -6 to 6
- cotangent: bfloat16 [48, 14, 14, 512], P('dp', 'rows'), may hold values from -6 to 6
- attn_in_weight: bfloat16 [2, 512, 1536], P(None, 'dp'), may hold values from -0.25 to 0.25
- attn_out_weight: bfloat16 [2, 512, 512], P(None, 'dp'), may hold values from -0.75 to 0.75
- mlp_in_weight: bfloat16 [2, 512, 2048], P(None, 'dp'), may hold values from -0.25 to 0.25
- mlp_out_weight: bfloat16 [2, 2048, 512], P(None, 'dp'), may hold values from -0.125 to 0.125
- norm1_gain: bfloat16 [2, 512], P(None, 'dp'), may hold values from 0.5 to 1.5
- norm1_bias: bfloat16 [2, 512], P(None, 'dp'), may hold values from -1.5 to 1.5
- attn_in_bias: bfloat16 [2, 1024], P(None, 'dp'), may hold values from -1.5 to 1.5
- attn_out_bias: bfloat16 [2, 512], P(None, 'dp'), may hold values from -1.5 to 1.5
- norm2_gain: bfloat16 [2, 512], P(None, 'dp'), may hold values from 0.5 to 1.5
- norm2_bias: bfloat16 [2, 512], P(None, 'dp'), may hold values from -1.5 to 1.5
- mlp_in_bias: bfloat16 [2, 2048], P(None, 'dp'), may hold values from -1.5 to 1.5
- mlp_out_bias: bfloat16 [2, 512], P(None, 'dp'), may hold values from -1.5 to 1.5
- bias_table: float32 [2, 169, 16], replicated, may hold values from -5 to 303
- region_labels: int32 [14, 14], replicated, may hold values from 0 to 2
- table_index: int32 [49, 49], replicated, may hold values from 0 to 168
Outputs:
- final_out: bfloat16 [48, 14, 14, 512], P('dp', 'rows')
- input_grad: float32 [48, 14, 14, 512], P('dp', 'rows')
- grad_attn_in_weight: float32 [2, 512, 1536], P(None, 'dp')
- grad_attn_out_weight: float32 [2, 512, 512], P(None, 'dp')
- grad_mlp_in_weight: float32 [2, 512, 2048], P(None, 'dp')
- grad_mlp_out_weight: float32 [2, 2048, 512], P(None, 'dp')
- grad_norm1_gain: float32 [2, 512], P(None, 'dp')
- grad_norm1_bias: float32 [2, 512], P(None, 'dp')
- grad_attn_in_bias: float32 [2, 1024], P(None, 'dp')
- grad_attn_out_bias: float32 [2, 512], P(None, 'dp')
- grad_norm2_gain: float32 [2, 512], P(None, 'dp')
- grad_norm2_bias: float32 [2, 512], P(None, 'dp')
- grad_mlp_in_bias: float32 [2, 2048], P(None, 'dp')
- grad_mlp_out_bias: float32 [2, 512], P(None, 'dp')
- grad_bias_table: float32 [2, 169, 16], replicated
The draws below stay inside these ranges and needn't reach their ends.
All inputs are finite; a program needn't handle non-finite values.
Results may differ from the reference program's by a relative error of at most 0.015.
Values may be sent and summed in bfloat16 or wider, within the bound.
A program may use at most 192 MiB of HBM per device.

```python
import jax
import jax.numpy as jnp
from jax import lax

C = 512
HEADS = 16
HEAD_DIM = 32
FF = 2048
WIN = 7
GRID = 14
SHIFT = 3
LAYERS = 2
IMG_DEV = 3
IMAGES = 48
REL = 169


def draw_bias_table(key, part):
    shape = (LAYERS, REL, HEADS)
    normal_part = jax.random.truncated_normal(jax.random.fold_in(key, 11), -2.5, 2.5, shape, jnp.float32) * 2.0
    return normal_part


def set_ends(entries, own_key, least, high):
    extent = entries.shape
    spot = [jax.random.randint(jax.random.fold_in(own_key, axis), (), 0, extent[axis]) for axis in range(len(extent))]
    entries = entries.at[tuple(spot)].set(least)
    longest = extent.index(max(extent))
    spot[longest] = (spot[longest] + 1) % extent[longest]
    return entries.at[tuple(spot)].set(high)


def levels(key, shape, cuts, low, top_value):
    def one(dim, shards_of):
        draws = jax.random.uniform(jax.random.fold_in(jax.random.fold_in(key, 6), dim), (shards_of,), jnp.float32, low / len(cuts), top_value / len(cuts))
        return jnp.repeat(jnp.exp(draws), shape[dim] // shards_of).reshape((-1,) + (1,) * (len(shape) - dim - 1))

    level = one(*cuts[0])
    for cut in cuts[1:]:
        level = level * one(*cut)
    return level


def centred(stream_key, dims, scale, limit, pieces=(), kind=jnp.bfloat16):
    entries = jax.random.normal(stream_key, dims, jnp.float32) * scale
    if len(pieces) > 0:
        entries = levels(stream_key, dims, pieces, -0.22, 0.18) * entries
    return jnp.clip(entries, min=-limit, max=limit).astype(kind)


def setup_inputs(seed: int = 0) -> dict:
    key_of = jax.random.split(jax.random.key(seed), 18)
    images = centred(key_of[0], (IMAGES, GRID, GRID, C), 1.0, 6.0, ((0, 16), (1, 2)))
    cotangent = centred(key_of[1], (IMAGES, GRID, GRID, C), 1.0, 6.0, ((0, 16), (1, 2)))
    attn_in_weight = centred(key_of[2], (LAYERS, C, 3 * C), C ** -0.5, 0.25, ((1, 16),))
    attn_out_weight = centred(key_of[3], (LAYERS, C, C), (C // 8) ** -0.5, 0.75, ((1, 16),))
    mlp_in_weight = centred(key_of[4], (LAYERS, C, FF), C ** -0.5, 0.25, ((1, 16),))
    mlp_out_weight = centred(key_of[5], (LAYERS, FF, C), FF ** -0.5, 0.125, ((1, 16),))
    norm1_gain = jnp.clip(1.0 + 0.1 * jax.random.normal(key_of[6], (LAYERS, C), jnp.float32), 0.5, 1.5).astype(jnp.bfloat16)
    norm1_bias = centred(key_of[7], (LAYERS, C), 0.3, 1.5, ((1, 16),))
    attn_in_bias = centred(key_of[8], (LAYERS, 2 * C), 0.3, 1.5, ((1, 16),))
    attn_out_bias = centred(key_of[9], (LAYERS, C), 0.3, 1.5, ((1, 16),))
    norm2_gain = jnp.clip(1.0 + 0.1 * jax.random.normal(key_of[10], (LAYERS, C), jnp.float32), 0.5, 1.5).astype(jnp.bfloat16)
    norm2_bias = centred(key_of[11], (LAYERS, C), 0.3, 1.5, ((1, 16),))
    mlp_in_bias = centred(key_of[12], (LAYERS, FF), 0.3, 1.5, ((1, 16),))
    mlp_out_bias = centred(key_of[13], (LAYERS, C), 0.3, 1.5, ((1, 16),))
    bias_table = draw_bias_table(jax.random.fold_in(key_of[17], 71), 0)
    region_labels = set_ends(jax.random.randint(key_of[15], (GRID, GRID), 0, 3), jax.random.fold_in(key_of[15], 1), 0, 2).astype(jnp.int32)
    table_index = set_ends(jax.random.randint(key_of[16], (WIN * WIN, WIN * WIN), 0, REL), jax.random.fold_in(key_of[16], 1), 0, REL - 1).astype(jnp.int32)
    return {"images": images, "cotangent": cotangent, "attn_in_weight": attn_in_weight, "attn_out_weight": attn_out_weight, "mlp_in_weight": mlp_in_weight, "mlp_out_weight": mlp_out_weight, "norm1_gain": norm1_gain, "norm1_bias": norm1_bias, "attn_in_bias": attn_in_bias, "attn_out_bias": attn_out_bias, "norm2_gain": norm2_gain, "norm2_bias": norm2_bias, "mlp_in_bias": mlp_in_bias, "mlp_out_bias": mlp_out_bias, "bias_table": bias_table, "region_labels": region_labels, "table_index": table_index}


EPS = 1e-05
NEG = -1e+30
SQRT_HALF = 0.7071067811865476
INV_ROOT_TAU = 0.3989422804014327

def product(spec, left, right):
    return jnp.einsum(spec, left.astype(jnp.float32), right.astype(jnp.float32))

def outer(left, right):
    left_flat = left.reshape(-1, left.shape[-1])
    right_flat = right.reshape(-1, right.shape[-1])
    return jnp.dot(left_flat.T, right_flat, preferred_element_type=jnp.float32)

def back_product(grad_rows, weight):
    return jnp.dot(grad_rows, weight.T, preferred_element_type=jnp.float32)

def token_total(values):
    return lax.optimization_barrier(jnp.sum(values.reshape(-1, values.shape[-1]), axis=0))

def to_windows(grid):
    num_images, grid_rows, grid_cols, channels = grid.shape
    split = grid.reshape(num_images, grid_rows // WIN, WIN, grid_cols // WIN, WIN, channels)
    return split.transpose(0, 1, 3, 2, 4, 5).reshape(num_images, grid_rows // WIN * (grid_cols // WIN), WIN * WIN, channels)

def from_windows(window_rows, grid_rows, grid_cols):
    num_images = window_rows.shape[0]
    channels = window_rows.shape[-1]
    split = window_rows.reshape(num_images, grid_rows // WIN, grid_cols // WIN, WIN, WIN, channels)
    return split.transpose(0, 1, 3, 2, 4, 5).reshape(num_images, grid_rows, grid_cols, channels)

def layernorm_apply(values, gain_vector, offset_vector):
    average = lax.optimization_barrier(jnp.mean(values, axis=-1, keepdims=True))
    centered_input = values - average
    variance = lax.optimization_barrier(jnp.mean(centered_input * centered_input, axis=-1, keepdims=True))
    inverse_deviation = lax.rsqrt(variance + EPS)
    standardized = centered_input * inverse_deviation
    return (standardized * gain_vector + offset_vector, standardized, inverse_deviation)

def layernorm_reverse(output_gradient, standardized, inverse_deviation, gain_vector):
    standardized_gradient = output_gradient * gain_vector
    input_gradient_rows = inverse_deviation * (standardized_gradient - lax.optimization_barrier(jnp.mean(standardized_gradient, axis=-1, keepdims=True)) - standardized * lax.optimization_barrier(jnp.mean(standardized_gradient * standardized, axis=-1, keepdims=True)))
    return (input_gradient_rows, token_total(output_gradient * standardized), token_total(output_gradient))

def gelu_value(preactivation):
    return preactivation * 0.5 * (1.0 + lax.erf(preactivation * SQRT_HALF))

def gelu_slope(preactivation):
    return 0.5 * (1.0 + lax.erf(preactivation * SQRT_HALF)) + preactivation * jnp.exp(-0.5 * preactivation * preactivation) * INV_ROOT_TAU

def split_heads(rows):
    return rows.reshape(rows.shape[:-1] + (HEADS, HEAD_DIM))

def masked_scores(window_queries, window_keys, pos_bias, allowed):
    scores = product('bwqhd,bwkhd->bwhqk', split_heads(window_queries), split_heads(window_keys)) + pos_bias[None, None]
    return jnp.where(allowed[None, :, None], scores, NEG)

def attend(window_queries, window_keys, window_values, pos_bias, allowed):
    scores = masked_scores(window_queries, window_keys, pos_bias, allowed)
    row_max = lax.optimization_barrier(jnp.max(scores, axis=-1, keepdims=True))
    log_partition = row_max + jnp.log(lax.optimization_barrier(jnp.sum(jnp.exp(scores - row_max), axis=-1, keepdims=True)))
    attn_probs = jnp.exp(scores - log_partition).astype(jnp.bfloat16)
    context = product('bwhqk,bwkhd->bwqhd', attn_probs, split_heads(window_values))
    return (context.reshape(window_queries.shape).astype(jnp.bfloat16), log_partition)

def attend_back(window_queries, window_keys, window_values, pos_bias, allowed, log_partition, grad_context):
    scores = masked_scores(window_queries, window_keys, pos_bias, allowed)
    attn_probs = jnp.exp(scores - log_partition)
    grad_heads = split_heads(grad_context)
    grad_probs = product('bwqhd,bwkhd->bwhqk', grad_heads, split_heads(window_values))
    grad_values = product('bwhqk,bwqhd->bwkhd', attn_probs.astype(jnp.bfloat16), grad_heads)
    grad_scores = attn_probs * (grad_probs - lax.optimization_barrier(jnp.sum(attn_probs * grad_probs, axis=-1, keepdims=True)))
    table_term = lax.optimization_barrier(jnp.sum(grad_scores, axis=(0, 1)))
    scores_bf = grad_scores.astype(jnp.bfloat16)
    grad_query = product('bwhqk,bwkhd->bwqhd', scores_bf, split_heads(window_keys))
    grad_keys = product('bwhqk,bwqhd->bwkhd', scores_bf, split_heads(window_queries))
    shape = window_queries.shape
    return (grad_query.reshape(shape), grad_keys.reshape(shape), grad_values.reshape(shape), table_term)

def lookup(table_part, table_index):
    picked = jnp.take(table_part, table_index.reshape(-1), axis=0)
    return picked.T.reshape(HEADS, WIN * WIN, WIN * WIN)

def layer_forward(residual_tokens, params, table_part, table_index, allowed, shifted):
    in_weight, out_weight, up_weight, down_weight, first_gain, first_offset, in_bias, out_bias, second_gain, second_offset, up_bias, down_bias = params
    normalized_tokens, first_standardized, first_scale = layernorm_apply(residual_tokens, first_gain, first_offset)
    normalized_tokens = normalized_tokens.astype(jnp.bfloat16)
    if shifted:
        normalized_tokens = jnp.roll(normalized_tokens, (-SHIFT, -SHIFT), axis=(1, 2))
    window_input = to_windows(normalized_tokens)
    packed = jnp.dot(window_input, in_weight, preferred_element_type=jnp.float32)
    window_queries = ((packed[..., :C] + in_bias[:C]) * HEAD_DIM ** (-0.5)).astype(jnp.bfloat16)
    window_keys = packed[..., C:2 * C].astype(jnp.bfloat16)
    window_values = (packed[..., 2 * C:] + in_bias[C:]).astype(jnp.bfloat16)
    pos_bias = lookup(table_part, table_index)
    context, log_partition = attend(window_queries, window_keys, window_values, pos_bias, allowed)
    local_context = from_windows(context, GRID, GRID)
    if shifted:
        local_context = jnp.roll(local_context, (SHIFT, SHIFT), axis=(1, 2))
    attended_residual = residual_tokens + jnp.dot(local_context, out_weight, preferred_element_type=jnp.float32) + out_bias
    second_normalized, second_standardized, second_scale = layernorm_apply(attended_residual, second_gain, second_offset)
    hidden_units = second_normalized.astype(jnp.bfloat16)
    preactivation = jnp.dot(hidden_units, up_weight, preferred_element_type=jnp.float32) + up_bias
    activated_units = gelu_value(preactivation).astype(jnp.bfloat16)
    result = attended_residual + jnp.dot(activated_units, down_weight, preferred_element_type=jnp.float32) + down_bias
    retained_state = (first_standardized, first_scale, window_input, window_queries, window_keys, window_values, log_partition, local_context, second_standardized, second_scale, hidden_units, preactivation, activated_units)
    return (result, retained_state)

def layer_backward(grad_flow, params, table_part, table_index, allowed, onehot, shifted, retained_state):
    in_weight, out_weight, up_weight, down_weight, first_gain, first_offset, in_bias, out_bias, second_gain, second_offset, up_bias, down_bias = params
    first_standardized, first_scale, window_input, window_queries, window_keys, window_values, log_partition, local_context, second_standardized, second_scale, hidden_units, preactivation, activated_units = retained_state
    grad_bf = grad_flow.astype(jnp.bfloat16)
    grad_down = outer(activated_units, grad_bf)
    grad_down_bias = token_total(grad_flow)
    grad_active = back_product(grad_bf, down_weight)
    grad_pre = grad_active * gelu_slope(preactivation)
    grad_pre_bf = grad_pre.astype(jnp.bfloat16)
    grad_upw = outer(hidden_units, grad_pre_bf)
    grad_up_bias = token_total(grad_pre)
    hidden_gradient = back_product(grad_pre_bf, up_weight)
    attention_share, second_gain_gradient, second_offset_gradient = layernorm_reverse(hidden_gradient, second_standardized, second_scale, second_gain)
    grad_mixed = grad_flow + attention_share
    mixed_bf = grad_mixed.astype(jnp.bfloat16)
    grad_outw = outer(local_context, mixed_bf)
    grad_out_bias = token_total(grad_mixed)
    grad_context = back_product(mixed_bf, out_weight).astype(jnp.bfloat16)
    if shifted:
        grad_context = jnp.roll(grad_context, (-SHIFT, -SHIFT), axis=(1, 2))
    grad_context_win = to_windows(grad_context)
    pos_bias = lookup(table_part, table_index)
    grad_query, grad_keys, grad_values, table_term = attend_back(window_queries, window_keys, window_values, pos_bias, allowed, log_partition, grad_context_win)
    grad_query = grad_query * HEAD_DIM ** (-0.5)
    grad_packed = jnp.concatenate([grad_query, grad_keys, grad_values], axis=-1).astype(jnp.bfloat16)
    grad_inw = outer(window_input, grad_packed)
    grad_in_bias = jnp.concatenate([token_total(grad_query), token_total(grad_values)])
    normalized_gradient = from_windows(back_product(grad_packed, in_weight), GRID, GRID)
    if shifted:
        normalized_gradient = jnp.roll(normalized_gradient, (SHIFT, SHIFT), axis=(1, 2))
    residual_share, first_gain_gradient, first_offset_gradient = layernorm_reverse(normalized_gradient, first_standardized, first_scale, first_gain)
    grad_stream = grad_mixed + residual_share
    grad_table = lax.dot_general(onehot, table_term.reshape(HEADS, -1), (((0,), (1,)), ((), ())), precision=lax.Precision.HIGHEST)
    grads = (grad_inw, grad_outw, grad_upw, grad_down, first_gain_gradient, first_offset_gradient, grad_in_bias, grad_out_bias, second_gain_gradient, second_offset_gradient, grad_up_bias, grad_down_bias)
    return (grad_stream, grads, grad_table)

def layer_params(weights, layer_no):
    return tuple((member[layer_no] if position < 4 else member[layer_no].astype(jnp.float32) for position, member in enumerate(weights)))

def two_layers(image_part, cot_part, weights, bias_table, table_index, allowed_pair, onehot):
    residual_tokens = image_part.astype(jnp.float32)
    saved_all = []
    for layer_no in range(LAYERS):
        params = layer_params(weights, layer_no)
        residual_tokens, retained_state = layer_forward(residual_tokens, params, bias_table[layer_no], table_index, allowed_pair[layer_no % 2], layer_no % 2 == 1)
        saved_all.append(retained_state)
    final_out = residual_tokens.astype(jnp.bfloat16)
    grad_flow = cot_part.astype(jnp.float32)
    grads_all = [None] * LAYERS
    tables_all = [None] * LAYERS
    for layer_no in reversed(range(LAYERS)):
        params = layer_params(weights, layer_no)
        grad_flow, grads_all[layer_no], tables_all[layer_no] = layer_backward(grad_flow, params, bias_table[layer_no], table_index, allowed_pair[layer_no % 2], onehot, layer_no % 2 == 1, saved_all[layer_no])
    return (final_out, grad_flow, grads_all, tables_all)

def reference(images, cotangent, attn_in_weight, attn_out_weight, mlp_in_weight, mlp_out_weight, norm1_gain, norm1_bias, attn_in_bias, attn_out_bias, norm2_gain, norm2_bias, mlp_in_bias, mlp_out_bias, bias_table, region_labels, table_index):
    weights = (attn_in_weight, attn_out_weight, mlp_in_weight, mlp_out_weight, norm1_gain, norm1_bias, attn_in_bias, attn_out_bias, norm2_gain, norm2_bias, mlp_in_bias, mlp_out_bias)
    label_tiles = to_windows(region_labels[None, :, :, None])[0, :, :, 0]
    shifted_allowed = label_tiles[:, :, None] == label_tiles[:, None, :]
    allowed_pair = (jnp.ones_like(shifted_allowed), shifted_allowed)
    onehot = (table_index.reshape(-1)[:, None] == jnp.arange(REL, dtype=jnp.int32)[None, :]).astype(jnp.float32)
    block_count = IMAGES // IMG_DEV
    image_blocks = images.reshape(block_count, IMG_DEV, GRID, GRID, C)
    cot_blocks = cotangent.reshape(block_count, IMG_DEV, GRID, GRID, C)
    zero_grads = tuple((jnp.zeros(member.shape, jnp.float32) for member in weights))
    zero_table = jnp.zeros(bias_table.shape, jnp.float32)

    def run_block(carry, inputs):
        grad_sums, table_total = carry
        image_part, cot_part = inputs
        final_out, grad_flow, grads_all, tables_all = two_layers(image_part, cot_part, weights, bias_table, table_index, allowed_pair, onehot)
        new_sums = tuple((grad_sums[position] + jnp.stack([grads_all[layer_no][position] for layer_no in range(LAYERS)]) for position in range(12)))
        return ((new_sums, table_total + jnp.stack(tables_all)), (final_out, grad_flow))
    (grad_sums, table_total), (finals, flows) = lax.scan(run_block, (zero_grads, zero_table), (image_blocks, cot_blocks))
    final_out = finals.reshape(IMAGES, GRID, GRID, C)
    input_grad = flows.reshape(IMAGES, GRID, GRID, C)
    return (final_out, input_grad, grad_sums[0], grad_sums[1], grad_sums[2], grad_sums[3], grad_sums[4], grad_sums[5], grad_sums[6], grad_sums[7], grad_sums[8], grad_sums[9], grad_sums[10], grad_sums[11], table_total)
```

```python
import jax
import jax.numpy as jnp
import numpy as np
from jax import lax
from jax.experimental import pallas as pl
from jax.experimental.pallas import tpu as pltpu
from jax.sharding import PartitionSpec as P

C = 512
HEADS = 16
HEAD_DIM = 32
WIN = 7
GRID = 14
SHIFT = 3
LAYERS = 2
REL = 169
SIDE = 8
PAD = SIDE * SIDE
LANES = 128
GROUP = LANES // HEAD_DIM
GROUPS = HEADS // GROUP


EPS = 1e-05
NEG = -1e30
SQRT_HALF = 0.7071067811865476
INV_ROOT_TAU = 0.3989422804014327


def swapped(array, axis, distance):
    return lax.ppermute(array, axis, [(i, i ^ 1 << distance) for i in range(lax.axis_size(axis))])


def product(spec, left, right):
    return jnp.einsum(spec, left, right, preferred_element_type=jnp.float32)


def outer(left, right):
    left_flat = left.reshape(-1, left.shape[-1])
    right_flat = right.reshape(-1, right.shape[-1])
    return lax.dot_general(
        left_flat, right_flat, (((0,), (0,)), ((), ())), preferred_element_type=jnp.float32
    )


def back_product(grad_rows, weight):
    return lax.dot_general(
        grad_rows,
        weight,
        (((grad_rows.ndim - 1,), (1,)), ((), ())),
        preferred_element_type=jnp.float32,
    )


def token_total(values):
    return jnp.sum(values.reshape(-1, values.shape[-1]), axis=0)


def to_padded(grid):
    images, _, cols, channels = grid.shape
    split = grid.reshape(images, WIN, cols // WIN, WIN, channels).transpose(0, 2, 1, 3, 4)
    padded = jnp.pad(split, ((0, 0), (0, 0), (0, SIDE - WIN), (0, SIDE - WIN), (0, 0)))
    return padded.reshape(-1, channels)


def from_padded(rows):
    channels = rows.shape[-1]
    split = rows.reshape(-1, GRID // WIN, SIDE, SIDE, channels)[:, :, :WIN, :WIN]
    return split.transpose(0, 2, 1, 3, 4).reshape(-1, WIN, GRID, channels)


def layernorm_apply(values, gain_vector, offset_vector):
    average = jnp.mean(values, axis=-1, keepdims=True)
    centered_input = values - average
    variance = jnp.mean(centered_input * centered_input, axis=-1, keepdims=True)
    inverse_deviation = lax.rsqrt(variance + EPS)
    standardized = centered_input * inverse_deviation
    return (standardized * gain_vector + offset_vector, standardized, inverse_deviation)


def layernorm_reverse(output_gradient, standardized, inverse_deviation, gain_vector):
    standardized_gradient = output_gradient * gain_vector
    input_gradient_rows = inverse_deviation * (
        standardized_gradient
        - jnp.mean(standardized_gradient, axis=-1, keepdims=True)
        - standardized * jnp.mean(standardized_gradient * standardized, axis=-1, keepdims=True)
    )
    return (
        input_gradient_rows,
        token_total(output_gradient * standardized),
        token_total(output_gradient),
    )


def gelu_value(preactivation):
    return preactivation * 0.5 * (1.0 + lax.erf(preactivation * SQRT_HALF))


def gelu_slope(preactivation):
    return (
        0.5 * (1.0 + lax.erf(preactivation * SQRT_HALF))
        + preactivation * jnp.exp(-0.5 * preactivation * preactivation) * INV_ROOT_TAU
    )


def head_lanes(dtype):
    shape = (GROUP, 1, LANES)
    head = lax.broadcasted_iota(jnp.int32, shape, 0)
    lane = lax.broadcasted_iota(jnp.int32, shape, 2)
    return (lane // HEAD_DIM == head).astype(jnp.float32).astype(dtype)


def spread(rows, lanes):
    return (rows[None] * lanes).reshape(GROUP * PAD, LANES)


def gather_heads(wide, lanes):
    return jnp.sum(wide.reshape(GROUP, PAD, LANES) * lanes, axis=0)


def dot_nt(left, right):
    return lax.dot_general(left, right, (((1,), (1,)), ((), ())), preferred_element_type=jnp.float32)


def dot_tn(left, right):
    return lax.dot_general(left, right, (((0,), (0,)), ((), ())), preferred_element_type=jnp.float32)


def window_probs(wide_query, keys, scores_bias):
    scores = dot_nt(wide_query, keys) + scores_bias
    weights = jnp.exp(scores - jnp.max(scores, axis=-1, keepdims=True))
    return weights / jnp.sum(weights, axis=-1, keepdims=True)


def attend_kernel(kinds, x_ref, w_ref, b_ref, sb_ref, packed_ref, context_ref):
    rows = x_ref[...]
    bias = b_ref[...]
    queries = jnp.dot(rows, w_ref[:, :C], preferred_element_type=jnp.float32) + bias[:, :C]
    packed_ref[:, :C] = (queries * HEAD_DIM ** (-0.5)).astype(jnp.bfloat16)
    keys = jnp.dot(rows, w_ref[:, C : 2 * C], preferred_element_type=jnp.float32)
    packed_ref[:, C : 2 * C] = keys.astype(jnp.bfloat16)
    values = jnp.dot(rows, w_ref[:, 2 * C :], preferred_element_type=jnp.float32) + bias[:, C:]
    packed_ref[:, 2 * C :] = values.astype(jnp.bfloat16)
    lanes = head_lanes(jnp.bfloat16)
    lanes_f32 = head_lanes(jnp.float32)

    def window(step, carry):
        rows = pl.ds(pl.multiple_of(step * PAD, PAD), PAD)
        kind = lax.rem(step, kinds)
        for group in range(GROUPS):
            low = group * LANES
            wide_query = spread(packed_ref[rows, low : low + LANES], lanes)
            keys = packed_ref[rows, C + low : C + low + LANES]
            values = packed_ref[rows, 2 * C + low : 2 * C + low + LANES]
            probs = window_probs(wide_query, keys, sb_ref[kind, group])
            wide = jnp.dot(
                probs.astype(jnp.bfloat16), values, preferred_element_type=jnp.float32
            )
            context_ref[rows, low : low + LANES] = gather_heads(wide, lanes_f32).astype(
                jnp.bfloat16
            )
        return carry

    lax.fori_loop(0, x_ref.shape[0] // PAD, window, 0)


def attend_back_kernel(kinds, packed_ref, dc_ref, sb_ref, dp_ref, db_ref, table_ref):
    lanes = head_lanes(jnp.bfloat16)
    lanes_f32 = head_lanes(jnp.float32)
    db_ref[...] = jnp.zeros_like(db_ref)
    table_ref[...] = jnp.zeros_like(table_ref)
    scale = HEAD_DIM ** (-0.5)

    def window(step, carry):
        rows = pl.ds(pl.multiple_of(step * PAD, PAD), PAD)
        kind = lax.rem(step, kinds)
        for group in range(GROUPS):
            low = group * LANES
            wide_query = spread(packed_ref[rows, low : low + LANES], lanes)
            keys = packed_ref[rows, C + low : C + low + LANES]
            values = packed_ref[rows, 2 * C + low : 2 * C + low + LANES]
            probs = window_probs(wide_query, keys, sb_ref[kind, group])
            wide_grad = spread(dc_ref[rows, low : low + LANES], lanes)
            grad_probs = dot_nt(wide_grad, values)
            grad_values = dot_tn(probs.astype(jnp.bfloat16), wide_grad)
            grad_scores = probs * (
                grad_probs - jnp.sum(probs * grad_probs, axis=-1, keepdims=True)
            )
            table_ref[group] += grad_scores
            scores_bf = grad_scores.astype(jnp.bfloat16)
            wide = jnp.dot(scores_bf, keys, preferred_element_type=jnp.float32)
            grad_query = gather_heads(wide, lanes_f32) * scale
            grad_keys = dot_tn(scores_bf, wide_query)
            dp_ref[rows, low : low + LANES] = grad_query.astype(jnp.bfloat16)
            dp_ref[rows, C + low : C + low + LANES] = grad_keys.astype(jnp.bfloat16)
            dp_ref[rows, 2 * C + low : 2 * C + low + LANES] = grad_values.astype(jnp.bfloat16)
            db_ref[:, low : low + LANES] += jnp.sum(grad_query, axis=0, keepdims=True)
            db_ref[:, C + low : C + low + LANES] += jnp.sum(grad_values, axis=0, keepdims=True)
        return carry

    lax.fori_loop(0, dc_ref.shape[0] // PAD, window, 0)


def in_vmem(count):
    return [pl.BlockSpec(memory_space=pltpu.VMEM)] * count


def attend(window_input, in_weight, in_bias, scores_bias):
    tokens = window_input.shape[0]
    kinds = scores_bias.shape[0]
    return pl.pallas_call(
        lambda *refs: attend_kernel(kinds, *refs),
        out_shape=(
            jax.ShapeDtypeStruct((tokens, 3 * C), jnp.bfloat16),
            jax.ShapeDtypeStruct((tokens, C), jnp.bfloat16),
        ),
        in_specs=in_vmem(4),
        out_specs=tuple(in_vmem(2)),
        cost_estimate=pl.CostEstimate(
            flops=8 * tokens * C * C, bytes_accessed=20 * 2**20, transcendentals=0
        ),
    )(window_input, in_weight, in_bias[None], scores_bias)


def attend_back(packed, grad_context, scores_bias):
    tokens = packed.shape[0]
    kinds = scores_bias.shape[0]
    return pl.pallas_call(
        lambda *refs: attend_back_kernel(kinds, *refs),
        out_shape=(
            jax.ShapeDtypeStruct((tokens, 3 * C), jnp.bfloat16),
            jax.ShapeDtypeStruct((1, 2 * C), jnp.float32),
            jax.ShapeDtypeStruct((GROUPS, GROUP * PAD, PAD), jnp.float32),
        ),
        in_specs=in_vmem(3),
        out_specs=tuple(in_vmem(3)),
        cost_estimate=pl.CostEstimate(
            flops=8 * tokens * C * C, bytes_accessed=40 * 2**20, transcendentals=0
        ),
    )(packed, grad_context, scores_bias)


def enter_grid(rows, shifted):
    if not shifted:
        return rows
    grid = from_padded(rows)
    incoming = swapped(grid[:, :SHIFT], "rows", 0)
    grid = jnp.concatenate([grid[:, SHIFT:], incoming], axis=1)
    return to_padded(jnp.roll(grid, -SHIFT, axis=2))


def leave_grid(rows, shifted):
    if not shifted:
        return rows
    grid = jnp.roll(from_padded(rows), SHIFT, axis=2)
    incoming = swapped(grid[:, WIN - SHIFT :].astype(jnp.bfloat16), "rows", 0).astype(grid.dtype)
    return to_padded(jnp.concatenate([incoming, grid[:, : WIN - SHIFT]], axis=1))


def layer_forward(stream, attn_weights, take_mlp, vectors, scores_bias, shifted, weave):
    in_weight, out_weight = attn_weights
    first_gain, first_offset, in_bias, out_bias = vectors[:4]
    second_gain, second_offset, up_bias, down_bias = vectors[4:]
    normalized, first_standardized, first_scale = layernorm_apply(stream, first_gain, first_offset)
    window_input = enter_grid(weave(normalized.astype(jnp.bfloat16)), shifted)
    window_input = weave(window_input)
    packed, context = attend(window_input, in_weight, in_bias, scores_bias)
    local_context = weave(leave_grid(weave(context), shifted))
    attended = (
        stream
        + jnp.dot(local_context, out_weight, preferred_element_type=jnp.float32)
        + out_bias
    )
    second_normalized, second_standardized, second_scale = layernorm_apply(
        attended, second_gain, second_offset
    )
    hidden = weave(second_normalized.astype(jnp.bfloat16))
    up_weight, down_weight = take_mlp()
    preactivation = jnp.dot(hidden, up_weight, preferred_element_type=jnp.float32) + up_bias
    activated = weave(gelu_value(preactivation).astype(jnp.bfloat16))
    result = (
        attended + jnp.dot(activated, down_weight, preferred_element_type=jnp.float32) + down_bias
    )
    kept = (
        first_standardized,
        first_scale,
        window_input,
        packed,
        local_context,
        second_standardized,
        second_scale,
        hidden,
        preactivation,
        activated,
    )
    return result, kept


def layer_backward(
    grad_flow, weights, vectors, scores_bias, onehot, shifted, kept, weave
):
    in_weight, out_weight, up_weight, down_weight = weights
    first_gain, second_gain = vectors[0], vectors[4]
    (
        first_standardized,
        first_scale,
        window_input,
        packed,
        local_context,
        second_standardized,
        second_scale,
        hidden,
        preactivation,
        activated,
    ) = kept
    grad_bf = grad_flow.astype(jnp.bfloat16)
    grad_down = outer(activated, grad_bf)
    grad_down_bias = token_total(grad_flow)
    grad_pre = back_product(grad_bf, down_weight) * gelu_slope(preactivation)
    grad_pre_bf = weave(grad_pre.astype(jnp.bfloat16))
    grad_up = outer(hidden, grad_pre_bf)
    grad_up_bias = token_total(grad_pre)
    attention_share, second_gain_gradient, second_offset_gradient = layernorm_reverse(
        back_product(grad_pre_bf, up_weight), second_standardized, second_scale, second_gain
    )
    attention_share = weave(attention_share)
    mlp_shards = weave.add(scatter_steps(owner_blocks((grad_up, grad_down))))
    grad_mixed = grad_flow + attention_share
    mixed_bf = grad_mixed.astype(jnp.bfloat16)
    grad_out = outer(local_context, mixed_bf)
    grad_out_bias = token_total(grad_mixed)
    grad_context = weave(back_product(mixed_bf, out_weight).astype(jnp.bfloat16))
    grad_packed, grad_in_bias, table_term = attend_back(
        packed, weave(enter_grid(grad_context, shifted)), scores_bias
    )
    grad_packed = weave(grad_packed)
    grad_in = outer(window_input, grad_packed)
    attn_shards = weave.add(scatter_steps(owner_blocks((grad_in, grad_out))))
    normalized_gradient = weave(leave_grid(weave(back_product(grad_packed, in_weight)), shifted))
    residual_share, first_gain_gradient, first_offset_gradient = layernorm_reverse(
        normalized_gradient, first_standardized, first_scale, first_gain
    )
    grad_table = lax.dot_general(
        onehot,
        table_term.reshape(HEADS, -1),
        (((0,), (1,)), ((), ())),
        precision=lax.Precision.HIGHEST,
    )
    vector_grads = (
        first_gain_gradient,
        first_offset_gradient,
        grad_in_bias.reshape(-1),
        grad_out_bias,
        second_gain_gradient,
        second_offset_gradient,
        grad_up_bias,
        grad_down_bias,
    )
    return grad_mixed + residual_share, mlp_shards, attn_shards, vector_grads, grad_table


class Chain:
    def __init__(self, steps):
        self.steps = steps
        self.state = next(steps)
        self.done = False

    def advance(self):
        following = next(self.steps, None)
        if following is None:
            self.done = True
        else:
            self.state = following

    def finish(self):
        while not self.done:
            self.advance()
        return self.state


class Weave:
    def __init__(self):
        self.chains = []

    def add(self, steps):
        chain = Chain(steps)
        self.chains.append(chain)
        return chain

    def __call__(self, value):
        live = [chain for chain in self.chains if not chain.done]
        for chain in live:
            chain.advance()
        if live:
            value, states = lax.optimization_barrier((value, [chain.state for chain in live]))
            for chain, state in zip(live, states):
                chain.state = state
        return value


def owner_blocks(grads):
    owners = lax.axis_size("dp")
    parts = []
    for grad in grads:
        grad = grad.astype(jnp.bfloat16)
        for low in range(0, grad.shape[1], C):
            parts.append(grad[:, low : low + C].reshape(owners, -1, C))
    return jnp.concatenate(parts, axis=1)


def merge(array, axis_name, bit):
    other = swapped(array, axis_name, bit)
    upper = ((lax.axis_index(axis_name) >> bit) & 1) == 1
    return jnp.where(upper, other, array), jnp.where(upper, array, other)


def double_owner(blocks, bit):
    owners, rows, _ = blocks.shape
    return jnp.stack(merge(blocks, "dp", bit), axis=1).reshape(2 * owners, rows, C)


def double_rows(blocks):
    return jnp.concatenate(merge(blocks, "rows", 0), axis=1)


def gather_steps(piece):
    bits = (lax.axis_size("dp") - 1).bit_length()
    quarters = piece.reshape(2, 2, -1, C)
    blocks = lax.dynamic_index_in_dim(quarters, lax.axis_index("rows"), 1, keepdims=False)
    blocks = blocks.reshape(1, -1, C)
    yield blocks
    for bit in range(bits - 1, 1, -1):
        blocks = double_owner(blocks, bit)
        yield blocks
    half = blocks.shape[1] // 2
    first, second = blocks[:, :half], blocks[:, half:]
    first, second = double_owner(first, 1), double_rows(second)
    yield first, second
    blocks = jnp.concatenate([double_rows(first), double_owner(second, 1)], axis=1)
    yield blocks
    yield double_owner(blocks, 0)


def piece_blocks(pieces):
    parts = []
    for piece in pieces:
        parts.extend(piece[:, low : low + C] for low in range(0, piece.shape[1], C))
    return jnp.concatenate(parts, axis=0)


def columns_of(blocks, count):
    depth = blocks.shape[1] // count
    parts = [
        blocks[:, step * depth : (step + 1) * depth].reshape(-1, C) for step in range(count)
    ]
    return jnp.concatenate(parts, axis=1)


def all_sum(values):
    for axis_name in ("dp", "rows"):
        for bit in range((lax.axis_size(axis_name) - 1).bit_length()):
            values = values + swapped(values, axis_name, bit)
    return values


def from_blocks(block, depth):
    return block.reshape(-1, depth, C).transpose(1, 0, 2).reshape(depth, -1)


def halve(array, axis_name, bit, dim):
    mine = (lax.axis_index(axis_name) >> bit) & 1
    keep = lax.dynamic_index_in_dim(array, mine, dim, keepdims=False)
    away = lax.dynamic_index_in_dim(array, 1 - mine, dim, keepdims=False)
    return add_bf(keep, swapped(away, axis_name, bit))


def add_bf(left, right):
    return (left.astype(jnp.float32) + right.astype(jnp.float32)).astype(jnp.bfloat16)


def halve_owner(blocks, bit):
    owners, rows, _ = blocks.shape
    return halve(blocks.reshape(owners // 2, 2, rows, C), "dp", bit, 1)


def halve_rows(blocks):
    owners, rows, _ = blocks.shape
    return halve(blocks.reshape(owners, 2, rows // 2, C), "rows", 0, 1)


def scatter_steps(blocks):
    bits = (lax.axis_size("dp") - 1).bit_length()
    yield blocks
    blocks = halve_owner(blocks, 0)
    yield blocks
    half = blocks.shape[1] // 2
    first, second = blocks[:, :half], blocks[:, half:]
    first, second = halve_owner(first, 1), halve_rows(second)
    yield first, second
    first, second = halve_rows(first), halve_owner(second, 1)
    both = jnp.concatenate([first, second], axis=1)
    yield both
    for bit in range(2, bits):
        both = halve_owner(both, bit)
        yield both
    low, high = merge(both[0].reshape(2, -1, C), "rows", 0)
    yield jnp.stack([low, high], axis=1).reshape(-1, C).astype(jnp.float32)


def per_device_general(
    images,
    cotangent,
    attn_in_weight,
    attn_out_weight,
    mlp_in_weight,
    mlp_out_weight,
    norm1_gain,
    norm1_bias,
    attn_in_bias,
    attn_out_bias,
    norm2_gain,
    norm2_bias,
    mlp_in_bias,
    mlp_out_bias,
    bias_table,
    region_labels,
    table_index,
):
    owners = lax.axis_size("dp")
    vector_shards = (
        norm1_gain,
        norm1_bias,
        attn_in_bias,
        attn_out_bias,
        norm2_gain,
        norm2_bias,
        mlp_in_bias,
        mlp_out_bias,
    )
    widths = [member.shape[1] for member in vector_shards]
    vector_piece = jnp.concatenate(vector_shards, axis=1).reshape(-1)
    vector_size = vector_piece.shape[0]
    vector_piece = jnp.pad(vector_piece, (0, -vector_size % (32 * C))).reshape(-1, C)
    depth = attn_in_weight.shape[1]
    up_blocks = mlp_in_weight.shape[2] // C

    def attn_piece(layer_no):
        return piece_blocks([attn_in_weight[layer_no], attn_out_weight[layer_no]])

    def mlp_piece(layer_no):
        return piece_blocks([mlp_in_weight[layer_no], mlp_out_weight[layer_no]])

    def attn_split(blocks):
        blocks = blocks[:, : 4 * depth]
        return columns_of(blocks[:, : 3 * depth], 3), blocks[:, 3 * depth :].reshape(-1, C)

    def mlp_split(blocks):
        up, down = blocks[:, : up_blocks * depth], blocks[:, up_blocks * depth :]
        return columns_of(up, up_blocks), down.reshape(-1, C)

    lead = Chain(gather_steps(jnp.concatenate([attn_piece(0), vector_piece], axis=0)))
    lead.advance()
    lead.advance()
    lead.state, first_mlp = lax.optimization_barrier((lead.state, mlp_piece(0)))
    weave = Weave()
    mlp_chains = [weave.add(gather_steps(first_mlp))]
    lead.advance()
    lead.state = weave(lead.state)
    lead.advance()
    lead.state = weave(lead.state)
    lead_blocks = lead.finish()
    vector_all = lead_blocks[:, 4 * depth :].reshape(owners, -1)[:, :vector_size]
    vector_all = vector_all.reshape(owners, LAYERS, -1).astype(jnp.float32)

    def layer_vectors(layer_no):
        start, result = 0, []
        for width in widths:
            result.append(vector_all[:, layer_no, start : start + width].reshape(-1))
            start += width
        return tuple(result)

    def pad_window(values, fill):
        grid = values.reshape(values.shape[:-1] + (WIN, WIN))
        pads = [(0, 0)] * (values.ndim - 1) + [(0, SIDE - WIN)] * 2
        return jnp.pad(grid, pads, constant_values=fill).reshape(values.shape[:-1] + (PAD,))

    def pad_pair(values, fill):
        both = pad_window(jnp.swapaxes(pad_window(values, fill), -1, -2), fill)
        return jnp.swapaxes(both, -1, -2)

    half_index = lax.axis_index("rows")
    local_labels = lax.dynamic_slice_in_dim(region_labels, half_index * WIN, WIN, 0)
    label_tiles = (
        local_labels.reshape(WIN, GRID // WIN, WIN).transpose(1, 0, 2).reshape(GRID // WIN, -1)
    )
    same = label_tiles[:, :, None] == label_tiles[:, None, :]
    real_key = pad_window(jnp.ones((WIN * WIN,), jnp.int32), 0) == 1
    allowed_pair = (
        jnp.broadcast_to(real_key[None, None, :], (1, PAD, PAD)),
        (pad_pair(same.astype(jnp.int32), 1) == 1) & real_key[None, None, :],
    )
    index_pad = pad_pair(table_index, 0)
    onehot = (index_pad.reshape(-1)[:, None] == jnp.arange(REL, dtype=jnp.int32)[None, :]).astype(
        jnp.float32
    )

    def scores_bias_of(layer_no):
        picked = lax.dot_general(
            bias_table[layer_no],
            onehot,
            (((0,), (1,)), ((), ())),
            precision=lax.Precision.HIGHEST,
            preferred_element_type=jnp.float32,
        ).reshape(HEADS, PAD, PAD)
        allowed = allowed_pair[layer_no % 2]
        masked = jnp.where(allowed[:, None], picked[None], NEG)
        return masked.reshape(-1, GROUPS, GROUP * PAD, PAD)

    stream = to_padded(images).astype(jnp.float32)
    vectors = [layer_vectors(layer_no) for layer_no in range(LAYERS)]
    score_biases = [scores_bias_of(layer_no) for layer_no in range(LAYERS)]
    kept_all = []
    attn_chains = [lead]
    weights = []
    for layer_no in range(LAYERS):
        if layer_no + 1 < LAYERS:
            attn_chains.append(weave.add(gather_steps(attn_piece(layer_no + 1))))
        attn_weights = attn_split(attn_chains[layer_no].finish())
        taken = []

        def take_mlp():
            taken.extend(mlp_split(mlp_chains[layer_no].finish()))
            if layer_no + 1 < LAYERS:
                mlp_chains.append(weave.add(gather_steps(mlp_piece(layer_no + 1))))
            return taken

        stream, kept = layer_forward(
            stream,
            attn_weights,
            take_mlp,
            vectors[layer_no],
            score_biases[layer_no],
            layer_no % 2 == 1,
            weave,
        )
        weights.append((*attn_weights, *taken))
        kept_all.append(kept)
    final_out = from_padded(stream.astype(jnp.bfloat16))
    grad_flow = to_padded(cotangent).astype(jnp.float32)
    mlp_all, attn_all, vectors_all, tables_all = ([None] * LAYERS for _ in range(4))
    for layer_no in reversed(range(LAYERS)):
        grad_flow, mlp_all[layer_no], attn_all[layer_no], grads, tables_all[layer_no] = (
            layer_backward(
                grad_flow,
                weights[layer_no],
                vectors[layer_no],
                score_biases[layer_no],
                onehot,
                layer_no % 2 == 1,
                kept_all[layer_no],
                weave,
            )
        )
        vectors_all[layer_no] = jnp.concatenate(grads)
    lengths = [width * owners for width in widths]
    small = jnp.concatenate(vectors_all + [jnp.stack(tables_all).reshape(-1)])
    total = small.shape[0]
    small = jnp.pad(small, (0, -total % (8 * LANES))).reshape(-1, LANES)
    small = all_sum(small).reshape(-1)[:total]
    mlp_all = [chain.finish() for chain in mlp_all]
    attn_all = [chain.finish() for chain in attn_all]
    vector_total = small[: LAYERS * sum(lengths)].reshape(LAYERS, -1)
    table_total = small[LAYERS * sum(lengths) :].reshape(bias_table.shape)
    vector_outs, start = [], 0
    owner = lax.axis_index("dp")
    for width, length in zip(widths, lengths):
        part = vector_total[:, start : start + length]
        vector_outs.append(lax.dynamic_slice_in_dim(part, owner * width, width, 1))
        start += length
    def stacked(blocks, low, high, rows):
        return jnp.stack([from_blocks(block[low * depth : high * depth], rows) for block in blocks])

    down_depth = mlp_out_weight.shape[1]
    grad_up = stacked(mlp_all, 0, up_blocks, depth)
    grad_down = jnp.stack([block[up_blocks * depth :].reshape(down_depth, C) for block in mlp_all])
    grad_in = stacked(attn_all, 0, 3, depth)
    grad_out = stacked(attn_all, 3, 4, depth)
    return (
        final_out,
        from_padded(grad_flow),
        grad_in,
        grad_out,
        grad_up,
        grad_down,
        *vector_outs,
        table_total,
    )


HALF_SEND = PAD // 2
KEYS = WIN * SIDE
WIDE = GROUP * PAD
VEC_ROWS = 32
SUM_ROWS = 40
TABLE_COLS = 256
MESH = pl.DeviceIdType.MESH
VMEM_BYTES = 63 * 2**20
F32 = jnp.float32
BF16 = jnp.bfloat16


class Links:
    def __init__(self, depth_z, send_sems, recv_sems):
        owner = lax.axis_index("dp")
        self.zs = depth_z
        self.r = lax.axis_index("rows")
        self.z = owner // 4
        self.x = lax.rem(owner // 2, 2)
        self.c = lax.rem(owner, 2)
        self.send_sems = send_sems
        self.recv_sems = recv_sems
        self.used = 0

    def place(self, kind, step=0):
        z, x, c, r = self.z, self.x, self.c, self.r
        if kind == "z":
            z = lax.rem(z + step, self.zs)
        elif kind == "x":
            x = 1 - x
        elif kind == "c":
            c = 1 - c
        else:
            r = 1 - r
        return (r, z * 4 + x * 2 + c)

    def greet(self):
        barrier = pltpu.get_barrier_semaphore()
        partners = [self.place("z", step) for step in range(1, self.zs)]
        partners += [self.place(kind) for kind in ("x", "c", "y")]
        for partner in partners:
            pl.semaphore_signal(barrier, inc=1, device_id=partner, device_id_type=MESH)
        pl.semaphore_wait(barrier, len(partners))

    def send(self, src, dst, kind, step=0):
        spot = self.used
        self.used += 1
        copy = pltpu.make_async_remote_copy(
            src_ref=src,
            dst_ref=dst,
            send_sem=self.send_sems.at[spot],
            recv_sem=self.recv_sems.at[spot],
            device_id=self.place(kind, step),
            device_id_type=MESH,
        )
        copy.start()
        return copy


class Gather:
    def __init__(self, links, parts):
        self.links = links
        self.parts = parts
        self.flying = []
        self.sent = []

    def wait(self):
        for copy in self.flying:
            copy.wait_recv()
        self.sent += self.flying
        self.flying = []

    def go(self, kind, pick, step=0):
        for ref, cols, route in self.parts:
            spot = pick(route)
            if spot is not None:
                view = ref.at[spot + (slice(None), cols)]
                self.flying.append(self.links.send(view, view, kind, step))

    def start(self):
        k = self.links
        for step in range(1, k.zs):
            self.go("z", lambda route: (k.z, k.x, k.c, k.r), step)

    def first(self):
        k = self.links
        self.wait()
        every = slice(None)
        self.go("x", lambda route: (every, k.x, k.c, k.r) if route == 0 else None)
        self.go("y", lambda route: (every, k.x, k.c, k.r) if route == 1 else None)

    def second(self):
        k = self.links
        self.wait()
        every = slice(None)
        self.go("y", lambda route: (every, every, k.c, k.r) if route == 0 else None)
        self.go("x", lambda route: (every, k.x, k.c, every) if route == 1 else None)

    def cores(self):
        k = self.links
        self.wait()
        every = slice(None)
        self.go("c", lambda route: (every, every, k.c, every))

    def finish(self):
        self.wait()
        for copy in self.sent:
            copy.wait_send()


def add_rows(left, right):
    return (left.astype(F32) + right.astype(F32)).astype(BF16)


class ScatterPart:
    def __init__(self, grad, low, high, route, buffers, out, layer_no):
        self.grad, self.low, self.high, self.route = grad, low, high, route
        self.core_in, self.first_in, self.second_in, self.z_in, self.mine, self.other = buffers
        self.out, self.layer_no = out, layer_no


class Scatter:
    def __init__(self, links, parts):
        self.links = links
        self.parts = parts
        self.flying = []
        self.sent = []

    def wait(self):
        for copy in self.flying:
            copy.wait_recv()
        self.sent += self.flying
        self.flying = []

    def go(self, part, spot, into, kind, step=0):
        view = part.grad.at[spot + (slice(None), pl.ds(part.low, part.high - part.low))]
        self.flying.append(self.links.send(view, into, kind, step))

    def start(self):
        k = self.links
        every = slice(None)
        for part in self.parts:
            self.go(part, (every, every, 1 - k.c, every), part.core_in, "c")

    def first(self):
        k = self.links
        every = slice(None)
        self.wait()

        def one(zi, carry):
            for part in self.parts:
                spot = (zi, every, k.c, every, every, slice(part.low, part.high))
                part.grad[spot] = add_rows(part.grad[spot], part.core_in[zi])
            return carry

        lax.fori_loop(0, k.zs, one, 0)
        for part in self.parts:
            if part.route == 0:
                self.go(part, (every, 1 - k.x, k.c, every), part.first_in, "x")
            else:
                self.go(part, (every, every, k.c, 1 - k.r), part.first_in, "y")

    def second(self):
        k = self.links
        every = slice(None)
        self.wait()

        def one(zi, carry):
            for part in self.parts:
                cols = slice(part.low, part.high)
                if part.route == 0:
                    spot = (zi, k.x, k.c, every, every, cols)
                else:
                    spot = (zi, every, k.c, k.r, every, cols)
                part.grad[spot] = add_rows(part.grad[spot], part.first_in[zi])
            return carry

        lax.fori_loop(0, k.zs, one, 0)
        for part in self.parts:
            if part.route == 0:
                self.go(part, (every, k.x, k.c, 1 - k.r), part.second_in, "y")
            else:
                self.go(part, (every, 1 - k.x, k.c, k.r), part.second_in, "x")

    def third(self):
        k = self.links
        every = slice(None)
        self.wait()

        def one(zi, carry):
            for part in self.parts:
                spot = (zi, k.x, k.c, k.r, every, slice(part.low, part.high))
                part.grad[spot] = add_rows(part.grad[spot], part.second_in[zi])
            return carry

        lax.fori_loop(0, k.zs, one, 0)
        for part in self.parts:
            for step in range(1, k.zs):
                far = lax.rem(k.z + step, k.zs)
                self.go(part, (far, k.x, k.c, k.r), part.z_in.at[step - 1], "z", step)

    def fourth(self):
        k = self.links
        self.wait()
        for part in self.parts:
            spot = (k.z, k.x, k.c, k.r, slice(None), slice(part.low, part.high))
            total = part.grad[spot].astype(F32)
            for step in range(1, k.zs):
                total = total + part.z_in[step - 1].astype(F32)
            part.mine[...] = total.astype(BF16)
            self.flying.append(k.send(part.mine, part.other, "y"))

    def finish(self):
        k = self.links
        self.wait()
        for part in self.parts:
            cols = slice(part.low, part.high)
            part.out[part.layer_no, k.r, :, cols] = part.mine[...].astype(F32)
            part.out[part.layer_no, 1 - k.r, :, cols] = part.other[...].astype(F32)
        for copy in self.sent:
            copy.wait_send()


def pad_keys(values):
    return jnp.concatenate([values, jnp.zeros((PAD - KEYS, values.shape[1]), values.dtype)], axis=0)


def attend_windows(packed, bias_of, probs, context):
    lanes = head_lanes(BF16)
    lanes_f32 = head_lanes(F32)

    def window(w, carry):
        for group in range(GROUPS):
            low = group * LANES
            wide_query = spread(packed[w, :, low : low + LANES], lanes)
            keys = packed[w, :, C + low : C + low + LANES]
            values = packed[w, :, 2 * C + low : 2 * C + low + LANES]
            scores = dot_nt(keys, wide_query)[:KEYS] + bias_of(w, group)
            weights = jnp.exp(scores - jnp.max(scores, axis=0, keepdims=True))
            part = weights * (1.0 / jnp.sum(weights, axis=0, keepdims=True))
            probs[w * GROUPS + group] = part
            wide = dot_tn(pad_keys(part).astype(BF16), values)
            context[w, :, low : low + LANES] = gather_heads(wide, lanes_f32).astype(BF16)
        return carry

    lax.fori_loop(0, packed.shape[0], window, 0)


def attend_windows_back(packed, probs, grad_context, grad_packed, table, sums, row):
    lanes = head_lanes(BF16)
    lanes_f32 = head_lanes(F32)
    scale = HEAD_DIM ** (-0.5)
    sums[row : row + 2, :] = jnp.zeros((2, C), F32)
    table[...] = jnp.zeros(table.shape, F32)

    def window(w, carry):
        for group in range(GROUPS):
            low = group * LANES
            wide_query = spread(packed[w, :, low : low + LANES], lanes)
            keys = packed[w, :, C + low : C + low + LANES]
            values = packed[w, :, 2 * C + low : 2 * C + low + LANES]
            wide_grad = spread(grad_context[w, :, low : low + LANES], lanes)
            part = probs[w * GROUPS + group]
            grad_probs = dot_nt(values, wide_grad)[:KEYS]
            product_sum = jnp.sum(part * grad_probs, axis=0, keepdims=True)
            grad_scores = part * (grad_probs - product_sum)
            table[2 * group] += grad_scores[:, :LANES]
            table[2 * group + 1] += grad_scores[:, LANES:]
            part_bf = pad_keys(part).astype(BF16)
            scores_bf = pad_keys(grad_scores).astype(BF16)
            grad_values = jnp.dot(part_bf, wide_grad, preferred_element_type=F32)
            grad_keys = jnp.dot(scores_bf, wide_query, preferred_element_type=F32)
            grad_query = gather_heads(dot_tn(scores_bf, keys), lanes_f32) * scale
            grad_packed[w, :, low : low + LANES] = grad_query.astype(BF16)
            grad_packed[w, :, C + low : C + low + LANES] = grad_keys.astype(BF16)
            grad_packed[w, :, 2 * C + low : 2 * C + low + LANES] = grad_values.astype(BF16)
            sums[row : row + 1, low : low + LANES] += jnp.sum(grad_query, axis=0, keepdims=True)
            sums[row + 1 : row + 2, low : low + LANES] += jnp.sum(
                grad_values, axis=0, keepdims=True
            )
        return carry

    lax.fori_loop(0, packed.shape[0], window, 0)


def table_sums(tables, index, sums, row):
    entry = lax.broadcasted_iota(jnp.int32, (TABLE_COLS, LANES), 0)
    lane = lax.broadcasted_iota(jnp.int32, (8, LANES), 1)
    first = (lane < PAD).astype(F32)

    def eight(block, total):
        low = pl.multiple_of(block * 8, 8)
        tiles = [table[:, pl.ds(low, 8), :] for table in tables]
        spots = index[pl.ds(low, 8), :]
        for j in range(8):
            rows = []
            for tile in tiles:
                one = tile[:, j, :]
                rows += [one * first, one * (1.0 - first)]
            rows = jnp.concatenate(rows, axis=0)
            high = rows.astype(BF16)
            rest = (rows - high.astype(F32)).astype(BF16)
            onehot = (entry == spots[j : j + 1, :]).astype(F32).astype(BF16)
            total = total + dot_nt(jnp.concatenate([high, rest], axis=0), onehot)
        return total

    count = len(tables) * 16
    total = lax.fori_loop(0, KEYS // 8, eight, jnp.zeros((2 * count, TABLE_COLS), F32))
    total = total[:count] + total[count:]
    sums[row : row + 16, :TABLE_COLS] = total[:16]
    sums[row : row + 16, TABLE_COLS:] = total[16:]


def token_rows(ref):
    value = ref[...]
    return value.reshape(-1, value.shape[-1])


def whole(ref, low, high):
    value = ref[:, :, :, :, :, low:high]
    return value.reshape(-1, high - low)


def training_kernel(depth_z, *refs):
    refs = iter(refs)

    def take(count):
        return [next(refs) for _ in range(count)]

    x_ref, cot_ref = take(2)
    shards = take(4)
    vec_ref, bias_ref, index_ref, perm_ref = take(4)
    final_ref, input_grad_ref = take(2)
    grad_outs = take(4)
    sums_out = next(refs)
    weights = [take(4) for _ in range(LAYERS)]
    top_grads = take(4)
    xhat1, xhat2, scale1, scale2, inputs, packed, probs, context, hidden, slope, active = (
        take(2) for _ in range(11)
    )
    stream, grad_flow, grad_rows, rows_bf, more_bf, halo = take(6)
    grad_packed, grad_bf, tables = take(3)
    scatter_buffers = [[take(6) for _ in range(5)] for _ in range(LAYERS)]
    vecs, vec_core, vec_one, vec_x, vec_two, vec_z = take(6)
    sums, sum_c, sum_one, sum_x, sum_two, sum_y, sum_three, sum_z = take(8)
    send_sems, recv_sems = take(2)

    windows = x_ref.shape[0]
    images = windows // 2
    tokens = windows * PAD
    ff = shards[2].shape[-1]
    links = Links(depth_z, send_sems, recv_sems)
    every = slice(None)
    mine = (links.z, links.x, links.c, links.r)

    for layer_no in range(LAYERS):
        for shard, weight in zip(shards, weights[layer_no]):
            weight[mine + (every, every)] = shard[layer_no, links.r]
    links.greet()
    vec_c = links.send(vec_ref, vec_core, "c")
    attn_parts = [(0, 0, 2 * C, 0), (0, 2 * C, 3 * C, 1), (1, 0, C, 1)]
    mlp_parts = [(2, 0, ff, 0), (3, 0, C, 1)]

    def gather_of(layer_no, parts):
        return Gather(
            links,
            [
                (weights[layer_no][which], pl.ds(low, high - low), route)
                for which, low, high, route in parts
            ],
        )

    attn = [gather_of(layer_no, attn_parts) for layer_no in range(LAYERS)]
    mlp = [gather_of(layer_no, mlp_parts) for layer_no in range(LAYERS)]
    attn[0].start()
    mlp[0].start()
    attn[1].start()
    mlp[1].start()

    def load_stream(w, carry):
        stream[w] = x_ref[w].astype(F32)
        return carry

    lax.fori_loop(0, windows, load_stream, 0)
    vec_sent = [vec_c]
    vec_c.wait_recv()
    vec_one[...] = vec_ref[...] + vec_core[...]
    step = links.send(vec_one, vec_x, "x")
    vec_sent.append(step)
    step.wait_recv()
    vec_two[...] = vec_one[...] + vec_x[...]
    vec_z[links.z] = vec_two[...]
    steps = [links.send(vec_two, vec_z.at[links.z], "z", far) for far in range(1, depth_z)]
    for step in steps:
        step.wait_recv()
    vec_sent += steps
    total = vec_z[0].astype(F32)
    for zi in range(1, depth_z):
        total = total + vec_z[zi].astype(F32)
    vecs[...] = total
    for step in vec_sent:
        step.wait_send()
    attn[0].first()

    def vec(layer_no, row):
        spot = layer_no * 12 + row
        return vecs[spot : spot + 1, :]

    def normalize(source, gain, offset, xhat, scale, target):
        def one(w, carry):
            values = source[w]
            average = jnp.mean(values, axis=-1, keepdims=True)
            centered = values - average
            variance = jnp.mean(centered * centered, axis=-1, keepdims=True)
            inverse = lax.rsqrt(variance + EPS)
            standard = centered * inverse
            xhat[w] = standard
            scale[w] = inverse
            target[w] = (standard * gain + offset).astype(BF16)
            return carry

        lax.fori_loop(0, windows, one, 0)

    def normalize_back(source, gain, xhat, scale, row_gain):
        def one(w, carry):
            by_gain, by_offset, flow_sum = carry
            values = source[w]
            standard = xhat[w]
            scaled = values * gain
            first = jnp.mean(scaled, axis=-1, keepdims=True)
            second = jnp.mean(scaled * standard, axis=-1, keepdims=True)
            flow = grad_flow[w] + scale[w] * (scaled - first - standard * second)
            grad_flow[w] = flow
            rows_bf[w] = flow.astype(BF16)
            return (
                by_gain + jnp.sum(values * standard, axis=0, keepdims=True),
                by_offset + jnp.sum(values, axis=0, keepdims=True),
                flow_sum + jnp.sum(flow, axis=0, keepdims=True),
            )

        zero = jnp.zeros((1, C), F32)
        by_gain, by_offset, flow_sum = lax.fori_loop(0, windows, one, (zero, zero, zero))
        sums[row_gain : row_gain + 1, :] = by_gain
        sums[row_gain + 1 : row_gain + 2, :] = by_offset
        return flow_sum

    def enter_start(source, slot):
        return links.send(source.at[:, pl.ds(0, HALF_SEND), :], halo.at[slot], "y")

    def leave_start(source, slot):
        return links.send(source.at[:, pl.ds(HALF_SEND, HALF_SEND), :], halo.at[slot], "y")

    def moved(source, slot, kind, image):
        own = source[2 * image : 2 * image + 2].reshape(2 * PAD, C)
        away = halo[slot, 2 * image : 2 * image + 2].reshape(PAD, C)
        return jnp.dot(perm_ref[2 * kind], own, preferred_element_type=F32) + jnp.dot(
            perm_ref[2 * kind + 1][:, :PAD], away, preferred_element_type=F32
        )

    def move(source, slot, kind, target):
        for image in range(images):
            target[2 * image : 2 * image + 2] = (
                moved(source, slot, kind, image).astype(BF16).reshape(2, PAD, C)
            )

    def project(layer_no):
        rows = token_rows(inputs[layer_no])
        weight = weights[layer_no][0]
        query = jnp.dot(rows, whole(weight, 0, C), preferred_element_type=F32) + vec(layer_no, 2)
        query = query * HEAD_DIM ** (-0.5)
        packed[layer_no][:, :, :C] = query.astype(BF16).reshape(windows, PAD, C)
        keys = jnp.dot(rows, whole(weight, C, 2 * C), preferred_element_type=F32)
        packed[layer_no][:, :, C : 2 * C] = keys.astype(BF16).reshape(windows, PAD, C)
        values = jnp.dot(rows, whole(weight, 2 * C, 3 * C), preferred_element_type=F32)
        values = values + vec(layer_no, 3)
        packed[layer_no][:, :, 2 * C :] = values.astype(BF16).reshape(windows, PAD, C)

    def mix(layer_no):
        rows = token_rows(context[layer_no])
        out = jnp.dot(rows, whole(weights[layer_no][1], 0, C), preferred_element_type=F32)
        stream[...] = stream[...] + (out + vec(layer_no, 4)).reshape(windows, PAD, C)

    def up_columns(layer_no, j):
        cols = pl.ds(pl.multiple_of(j * C, C), C)
        return weights[layer_no][2][:, :, :, :, :, cols].reshape(C, C), cols

    def feed(layer_no):
        rows = token_rows(hidden[layer_no])
        base = layer_no * 12
        stream[...] = stream[...] + vec(layer_no, 11).reshape(1, 1, C)

        def one(j, carry):
            up, cols = up_columns(layer_no, j)
            pre = jnp.dot(rows, up, preferred_element_type=F32) + vecs[pl.ds(base + 7 + j, 1), :]
            half = 0.5 * (1.0 + lax.erf(pre * SQRT_HALF))
            value = (pre * half).astype(BF16)
            steep = half + pre * jnp.exp(-0.5 * pre * pre) * INV_ROOT_TAU
            active[layer_no][:, :, cols] = value.reshape(windows, PAD, C)
            slope[layer_no][:, :, cols] = steep.astype(BF16).reshape(windows, PAD, C)
            down = weights[layer_no][3][j].reshape(C, C)
            out = jnp.dot(value, down, preferred_element_type=F32)
            stream[...] = stream[...] + out.reshape(windows, PAD, C)
            return carry

        lax.fori_loop(0, depth_z, one, 0)

    halo_sent = []
    normalize(stream, vec(0, 0), vec(0, 1), xhat1[0], scale1[0], inputs[0])
    attn[0].second()
    mlp[0].first()
    attn[0].cores()
    attn[0].finish()
    project(0)
    mlp[0].second()
    attn[1].first()
    attend_windows(packed[0], lambda w, g: bias_ref[0, g], probs[0], context[0])
    mlp[0].cores()
    attn[1].second()
    mlp[1].first()
    mix(0)
    normalize(stream, vec(0, 5), vec(0, 6), xhat2[0], scale2[0], hidden[0])
    mlp[0].finish()
    feed(0)
    attn[1].cores()
    mlp[1].second()
    normalize(stream, vec(1, 0), vec(1, 1), xhat1[1], scale1[1], rows_bf)
    halo_sent.append(enter_start(rows_bf, 0))
    attn[1].finish()
    halo_sent[-1].wait_recv()
    move(rows_bf, 0, 0, inputs[1])
    halo_sent[-1].wait_send()
    project(1)
    attend_windows(
        packed[1], lambda w, g: bias_ref[1 + lax.rem(w, 2), g], probs[1], more_bf
    )
    halo_sent.append(leave_start(more_bf, 1))
    mlp[1].cores()
    halo_sent[-1].wait_recv()
    move(more_bf, 1, 1, context[1])
    halo_sent[-1].wait_send()
    mix(1)
    normalize(stream, vec(1, 5), vec(1, 6), xhat2[1], scale2[1], hidden[1])
    mlp[1].finish()
    feed(1)

    def turn(w, carry):
        final_ref[w] = stream[w].astype(BF16)
        grad_flow[w] = cot_ref[w].astype(F32)
        rows_bf[w] = cot_ref[w]
        return carry + jnp.sum(cot_ref[w].astype(F32), axis=0, keepdims=True)

    flow_sum = lax.fori_loop(0, windows, turn, jnp.zeros((1, C), F32))

    grads = [weights[1], top_grads]

    def scatter_of(layer_no, parts, first_buffer):
        return Scatter(
            links,
            [
                ScatterPart(
                    grads[layer_no][which],
                    low,
                    high,
                    route,
                    scatter_buffers[layer_no][first_buffer + number],
                    grad_outs[which],
                    layer_no,
                )
                for number, (which, low, high, route) in enumerate(parts)
            ],
        )

    attn_back = [scatter_of(layer_no, attn_parts, 0) for layer_no in range(LAYERS)]
    mlp_back = [scatter_of(layer_no, mlp_parts, 3) for layer_no in range(LAYERS)]

    def feed_back(layer_no):
        base = layer_no * 12
        grad_up, grad_down = grads[layer_no][2], grads[layer_no][3]
        grad_rows[...] = jnp.zeros(grad_rows.shape, F32)

        def one(j, carry):
            flow = token_rows(rows_bf)
            up, cols = up_columns(layer_no, j)
            down = weights[layer_no][3][j].reshape(C, C)
            steep = slope[layer_no][:, :, cols].reshape(tokens, C).astype(F32)
            grad_pre = dot_nt(flow, down) * steep
            sums[pl.ds(base + 7 + j, 1), :] = jnp.sum(grad_pre, axis=0, keepdims=True)
            grad_pre_bf = grad_pre.astype(BF16)
            grad_bf[...] = grad_pre_bf
            value = active[layer_no][:, :, cols].reshape(tokens, C)
            down_part = dot_tn(value, flow).astype(BF16)
            grad_down[j] = down_part.reshape(grad_down.shape[1:])
            up_part = dot_tn(token_rows(hidden[layer_no]), grad_bf[...]).astype(BF16)
            grad_up[:, :, :, :, :, cols] = up_part.reshape(grad_up.shape[:-1] + (C,))
            back = dot_nt(grad_bf[...], up)
            grad_rows[...] = grad_rows[...] + back.reshape(windows, PAD, C)
            return carry

        lax.fori_loop(0, depth_z, one, 0)

    def mix_back(layer_no):
        flow = token_rows(rows_bf)
        part = dot_tn(token_rows(context[layer_no]), flow).astype(BF16)
        grad_out = grads[layer_no][1]
        grad_out[...] = part.reshape(grad_out.shape)
        back = dot_nt(flow, whole(weights[layer_no][1], 0, C)).astype(BF16)
        more_bf[...] = back.reshape(windows, PAD, C)

    def project_back(layer_no):
        rows = token_rows(inputs[layer_no])
        grad_in = grads[layer_no][0]
        for low in range(0, 3 * C, C):
            part = grad_packed[:, :, low : low + C].reshape(tokens, C)
            weight_part = dot_tn(rows, part).astype(BF16)
            grad_in[:, :, :, :, :, low : low + C] = weight_part.reshape(
                grad_in.shape[:-1] + (C,)
            )

    def project_rows_back(layer_no):
        total = None
        for low in range(0, 3 * C, C):
            part = grad_packed[:, :, low : low + C].reshape(tokens, C)
            back = dot_nt(part, whole(weights[layer_no][0], low, low + C))
            total = back if total is None else total + back
        grad_rows[...] = total.reshape(windows, PAD, C)

    sums[23:24, :] = flow_sum
    feed_back(1)
    mlp_back[1].start()
    sums[16:17, :] = normalize_back(grad_rows, vec(1, 5), xhat2[1], scale2[1], 17)
    mix_back(1)
    halo_sent.append(enter_start(more_bf, 2))
    mlp_back[1].first()
    halo_sent[-1].wait_recv()
    move(more_bf, 2, 0, rows_bf)
    halo_sent[-1].wait_send()
    attend_windows_back(packed[1], probs[1], rows_bf, grad_packed, tables.at[1], sums, 14)
    mlp_back[1].second()
    project_back(1)
    attn_back[1].start()
    project_rows_back(1)

    def split(w, carry):
        high = grad_rows[w].astype(BF16)
        rows_bf[w] = high
        more_bf[w] = (grad_rows[w] - high.astype(F32)).astype(BF16)
        return carry

    lax.fori_loop(0, windows, split, 0)
    halo_sent.append(leave_start(rows_bf, 3))
    mlp_back[1].third()
    attn_back[1].first()
    halo_sent[-1].wait_recv()
    for image in range(images):
        rest = more_bf[2 * image : 2 * image + 2].reshape(2 * PAD, C)
        value = moved(rows_bf, 3, 1, image) + jnp.dot(
            perm_ref[2], rest, preferred_element_type=F32
        )
        grad_rows[2 * image : 2 * image + 2] = value.reshape(2, PAD, C)
    halo_sent[-1].wait_send()
    flow_sum = normalize_back(grad_rows, vec(1, 0), xhat1[1], scale1[1], 12)

    sums[11:12, :] = flow_sum
    mlp_back[1].fourth()
    attn_back[1].second()
    feed_back(0)
    mlp_back[0].start()
    mlp_back[1].finish()
    attn_back[1].third()
    sums[4:5, :] = normalize_back(grad_rows, vec(0, 5), xhat2[0], scale2[0], 5)
    mix_back(0)
    mlp_back[0].first()
    attn_back[1].fourth()
    attend_windows_back(packed[0], probs[0], more_bf, grad_packed, tables.at[0], sums, 2)
    mlp_back[0].second()
    project_back(0)
    attn_back[0].start()
    attn_back[1].finish()
    project_rows_back(0)
    normalize_back(grad_rows, vec(0, 0), xhat1[0], scale1[0], 0)
    attn_back[0].first()
    table_sums([tables.at[0], tables.at[1]], index_ref, sums, 24)
    sum_sent = [links.send(sums, sum_c, "c")]
    mlp_back[0].third()
    sum_sent[-1].wait_recv()
    sum_one[...] = sums[...] + sum_c[...]
    sum_sent.append(links.send(sum_one, sum_x, "x"))
    attn_back[0].second()

    def result(w, carry):
        input_grad_ref[w] = grad_flow[w]
        return carry

    lax.fori_loop(0, windows, result, 0)
    sum_sent[-1].wait_recv()
    sum_two[...] = sum_one[...] + sum_x[...]
    sum_sent.append(links.send(sum_two, sum_y, "y"))
    mlp_back[0].fourth()
    attn_back[0].third()
    sum_sent[-1].wait_recv()
    sum_three[...] = sum_two[...] + sum_y[...]
    sum_z[links.z] = sum_three[...]
    last = [links.send(sum_three, sum_z.at[links.z], "z", far) for far in range(1, depth_z)]
    mlp_back[0].finish()
    attn_back[0].fourth()
    for step in last:
        step.wait_recv()
    total = sum_z[0]
    for zi in range(1, depth_z):
        total = total + sum_z[zi]
    sums_out[...] = total
    attn_back[0].finish()
    for step in sum_sent + last:
        step.wait_send()


def shift_matrices():
    spots = 2 * PAD
    kinds = np.zeros((4, spots, spots), np.float32)
    for w in range(2):
        for row in range(WIN):
            for col in range(WIN):
                here = w * PAD + row * SIDE + col
                keep = WIN - SHIFT
                from_w, from_col = (w, col + SHIFT) if col < keep else (1 - w, col - keep)
                if row < keep:
                    there = from_w * PAD + (row + SHIFT) * SIDE + from_col
                    kinds[0, here, there] = 1
                    kinds[2, there, here] = 1
                else:
                    there = from_w * HALF_SEND + (row - keep) * SIDE + from_col
                    kinds[1, here, there] = 1
                    source = w * HALF_SEND + (row - keep) * SIDE + col
                    kinds[3, from_w * PAD + (row - keep) * SIDE + from_col, source] = 1
    return kinds


def one_kernel_fits(owners, depth, down_depth, ff):
    return owners % 4 == 0 and depth % 32 == 0 and down_depth % 32 == 0 and ff == owners // 4 * C


def per_device(*args):
    attn_in_weight, mlp_in_weight, mlp_out_weight = args[2], args[4], args[5]
    sizes = (attn_in_weight.shape[1], mlp_out_weight.shape[1], mlp_in_weight.shape[2])
    if one_kernel_fits(lax.axis_size("dp"), *sizes) and lax.axis_size("rows") == 2:
        return per_device_one_kernel(*args)
    return per_device_general(*args)


def per_device_one_kernel(images, cotangent, *rest):
    shards, vectors = rest[:4], rest[4:12]
    bias_table, region_labels, table_index = rest[12:]
    owners = lax.axis_size("dp")
    depth_z = owners // 4
    owner = lax.axis_index("dp")
    widths = [member.shape[1] for member in vectors]

    placed = []
    for member, width in zip(vectors, widths):
        length = owners * width
        spot = lax.broadcasted_iota(jnp.int32, (LAYERS, length), 1)
        tiled = jnp.tile(member, (1, owners))
        placed.append(jnp.where(spot // width == owner, tiled, jnp.zeros((), member.dtype)))
    placed = jnp.concatenate(placed, axis=1).reshape(-1, C)
    vec_rows = jnp.pad(placed, ((0, VEC_ROWS - placed.shape[0]), (0, 0)))

    def pad_window(values, fill):
        grid = values.reshape(values.shape[:-1] + (WIN, WIN))
        pads = [(0, 0)] * (values.ndim - 1) + [(0, SIDE - WIN)] * 2
        return jnp.pad(grid, pads, constant_values=fill).reshape(values.shape[:-1] + (PAD,))

    def pad_pair(values, fill):
        both = pad_window(jnp.swapaxes(pad_window(values, fill), -1, -2), fill)
        return jnp.swapaxes(both, -1, -2)

    half_index = lax.axis_index("rows")
    local_labels = lax.dynamic_slice_in_dim(region_labels, half_index * WIN, WIN, 0)
    label_tiles = (
        local_labels.reshape(WIN, GRID // WIN, WIN).transpose(1, 0, 2).reshape(GRID // WIN, -1)
    )
    same = label_tiles[:, :, None] == label_tiles[:, None, :]
    real_key = pad_window(jnp.ones((WIN * WIN,), jnp.int32), 0) == 1
    same_pad = (pad_pair(same.astype(jnp.int32), 1) == 1) & real_key[None, None, :]
    same_keys = jnp.swapaxes(same_pad, 1, 2)[:, :KEYS]
    index_keys = pad_pair(table_index, 0).T[:KEYS]
    onehot = (
        index_keys.reshape(-1)[:, None] == jnp.arange(REL, dtype=jnp.int32)[None, :]
    ).astype(F32)
    picked = lax.dot_general(
        bias_table.transpose(0, 2, 1).reshape(LAYERS * HEADS, REL),
        onehot,
        (((1,), (1,)), ((), ())),
        precision=lax.Precision.HIGHEST,
        preferred_element_type=F32,
    ).reshape(LAYERS, GROUPS, GROUP, KEYS, PAD)
    picked = picked.transpose(0, 1, 3, 2, 4)
    allowed = jnp.concatenate(
        [jnp.broadcast_to(real_key[None, :KEYS, None], (1, KEYS, PAD)), same_keys], axis=0
    )
    layers = jnp.stack([picked[0], picked[1], picked[1]])
    bias = jnp.where(allowed[:, None, :, None, :], layers, NEG)
    bias = bias.reshape(3, GROUPS, KEYS, WIDE)
    index_wide = jnp.concatenate([index_keys, index_keys], axis=1)
    perms = jnp.asarray(shift_matrices(), BF16)

    x = to_padded(images).reshape(-1, PAD, C)
    cot = to_padded(cotangent).reshape(-1, PAD, C)
    windows = x.shape[0]
    tokens = windows * PAD
    split_shards = [shard.reshape(LAYERS, 2, shard.shape[1] // 2, -1) for shard in shards]
    shapes = [(depth_z, 2, 2, 2) + shard.shape[2:] for shard in split_shards]
    ff = shapes[2][-1]

    def rows_of(width, dtype):
        return pltpu.VMEM((windows, PAD, width), dtype)

    scratch = []
    for _ in range(LAYERS):
        scratch += [pltpu.VMEM(shape, BF16) for shape in shapes]
    scratch += [pltpu.VMEM(shape, BF16) for shape in shapes]
    scratch += [rows_of(C, F32)] * 4 + [rows_of(1, F32)] * 4
    scratch += [rows_of(C, BF16)] * 2 + [rows_of(3 * C, BF16)] * 2
    scratch += [pltpu.VMEM((windows * GROUPS, KEYS, WIDE), F32)] * 2
    scratch += [rows_of(C, BF16)] * 4 + [rows_of(ff, BF16)] * 4
    scratch += [rows_of(C, F32)] * 3 + [rows_of(C, BF16)] * 2
    scratch += [pltpu.VMEM((4, windows, HALF_SEND, C), BF16)]
    scratch += [rows_of(3 * C, BF16), pltpu.VMEM((tokens, C), BF16)]
    scratch += [pltpu.VMEM((LAYERS, 2 * GROUPS, KEYS, LANES), F32)]
    for _ in range(LAYERS):
        for which, width in ((0, 2 * C), (0, C), (1, C), (2, ff), (3, C)):
            tail = (shapes[which][-2], width)
            for lead in ((depth_z, 2, 2), (depth_z, 2), (depth_z,), (depth_z - 1,), (), ()):
                scratch.append(pltpu.VMEM(lead + tail, BF16))
    scratch += [pltpu.VMEM((VEC_ROWS, C), F32)] + [pltpu.VMEM((VEC_ROWS, C), BF16)] * 4
    scratch += [pltpu.VMEM((depth_z, VEC_ROWS, C), BF16)]
    scratch += [pltpu.VMEM((SUM_ROWS, C), F32)] * 7 + [pltpu.VMEM((depth_z, SUM_ROWS, C), F32)]
    sems = 2 * 5 * (2 * (depth_z + 2) + 1) + 2 * (depth_z + 2) + 8
    scratch += [pltpu.SemaphoreType.DMA((sems,))] * 2

    out_shape = [
        jax.ShapeDtypeStruct(x.shape, BF16),
        jax.ShapeDtypeStruct(x.shape, F32),
        *(jax.ShapeDtypeStruct(shard.shape, F32) for shard in split_shards),
        jax.ShapeDtypeStruct((SUM_ROWS, C), F32),
    ]
    final, input_grad, *weight_grads, sums = pl.pallas_call(
        lambda *refs: training_kernel(depth_z, *refs),
        out_shape=out_shape,
        in_specs=in_vmem(10),
        out_specs=in_vmem(7),
        scratch_shapes=scratch,
        compiler_params=pltpu.CompilerParams(
            collective_id=0, has_side_effects=True, vmem_limit_bytes=VMEM_BYTES
        ),
    )(x, cot, *split_shards, vec_rows, bias, index_wide, perms)

    vector_total = sums[: LAYERS * 12].reshape(LAYERS, -1)
    vector_outs, start = [], 0
    for width in widths:
        length = width * owners
        part = vector_total[:, start : start + length]
        vector_outs.append(lax.dynamic_slice_in_dim(part, owner * width, width, 1))
        start += length
    table = sums[24:40].reshape(2, 2 * GROUPS, LAYERS, TABLE_COLS)
    table = table.transpose(2, 3, 1, 0).reshape(LAYERS, TABLE_COLS, HEADS)[:, :REL]
    return (
        from_padded(final.reshape(-1, C)),
        from_padded(input_grad.reshape(-1, C)),
        *(grad.reshape(shard.shape) for grad, shard in zip(weight_grads, shards)),
        *vector_outs,
        table,
    )


def solution(mesh):
    return jax.shard_map(
        per_device,
        mesh=mesh,
        in_specs=(
            P("dp", "rows", None, None),
            P("dp", "rows", None, None),
            P(None, "dp", None),
            P(None, "dp", None),
            P(None, "dp", None),
            P(None, "dp", None),
            P(None, "dp"),
            P(None, "dp"),
            P(None, "dp"),
            P(None, "dp"),
            P(None, "dp"),
            P(None, "dp"),
            P(None, "dp"),
            P(None, "dp"),
            P(),
            P(),
            P(),
        ),
        out_specs=(
            P("dp", "rows", None, None),
            P("dp", "rows", None, None),
            P(None, "dp", None),
            P(None, "dp", None),
            P(None, "dp", None),
            P(None, "dp", None),
            P(None, "dp"),
            P(None, "dp"),
            P(None, "dp"),
            P(None, "dp"),
            P(None, "dp"),
            P(None, "dp"),
            P(None, "dp"),
            P(None, "dp"),
            P(),
        ),
        check_vma=False,
    )
```

```python
import jax
import jax.numpy as jnp
import numpy as np
from jax import lax
from jax.experimental import pallas as pl
from jax.experimental.pallas import tpu as pltpu
from jax.sharding import PartitionSpec as P

C = 512
HEADS = 16
HEAD_DIM = 32
WIN = 7
GRID = 14
SHIFT = 3
LAYERS = 2
REL = 169
SIDE = 8
PAD = SIDE * SIDE
LANES = 128
GROUP = LANES // HEAD_DIM
GROUPS = HEADS // GROUP


EPS = 1e-05
NEG = -1e30
SQRT_HALF = 0.7071067811865476
INV_ROOT_TAU = 0.3989422804014327


def swapped(array, axis, distance):
    return lax.ppermute(array, axis, [(i, i ^ 1 << distance) for i in range(lax.axis_size(axis))])


def product(spec, left, right):
    return jnp.einsum(spec, left, right, preferred_element_type=jnp.float32)


def outer(left, right):
    left_flat = left.reshape(-1, left.shape[-1])
    right_flat = right.reshape(-1, right.shape[-1])
    return lax.dot_general(
        left_flat, right_flat, (((0,), (0,)), ((), ())), preferred_element_type=jnp.float32
    )


def back_product(grad_rows, weight):
    return lax.dot_general(
        grad_rows,
        weight,
        (((grad_rows.ndim - 1,), (1,)), ((), ())),
        preferred_element_type=jnp.float32,
    )


def token_total(values):
    return jnp.sum(values.reshape(-1, values.shape[-1]), axis=0)


def to_padded(grid):
    images, _, cols, channels = grid.shape
    split = grid.reshape(images, WIN, cols // WIN, WIN, channels).transpose(0, 2, 1, 3, 4)
    padded = jnp.pad(split, ((0, 0), (0, 0), (0, SIDE - WIN), (0, SIDE - WIN), (0, 0)))
    return padded.reshape(-1, channels)


def from_padded(rows):
    channels = rows.shape[-1]
    split = rows.reshape(-1, GRID // WIN, SIDE, SIDE, channels)[:, :, :WIN, :WIN]
    return split.transpose(0, 2, 1, 3, 4).reshape(-1, WIN, GRID, channels)


def layernorm_apply(values, gain_vector, offset_vector):
    average = jnp.mean(values, axis=-1, keepdims=True)
    centered_input = values - average
    variance = jnp.mean(centered_input * centered_input, axis=-1, keepdims=True)
    inverse_deviation = lax.rsqrt(variance + EPS)
    standardized = centered_input * inverse_deviation
    return (standardized * gain_vector + offset_vector, standardized, inverse_deviation)


def layernorm_reverse(output_gradient, standardized, inverse_deviation, gain_vector):
    standardized_gradient = output_gradient * gain_vector
    input_gradient_rows = inverse_deviation * (
        standardized_gradient
        - jnp.mean(standardized_gradient, axis=-1, keepdims=True)
        - standardized * jnp.mean(standardized_gradient * standardized, axis=-1, keepdims=True)
    )
    return (
        input_gradient_rows,
        token_total(output_gradient * standardized),
        token_total(output_gradient),
    )


def gelu_value(preactivation):
    return preactivation * 0.5 * (1.0 + lax.erf(preactivation * SQRT_HALF))


def gelu_slope(preactivation):
    return (
        0.5 * (1.0 + lax.erf(preactivation * SQRT_HALF))
        + preactivation * jnp.exp(-0.5 * preactivation * preactivation) * INV_ROOT_TAU
    )


def head_lanes(dtype):
    shape = (GROUP, 1, LANES)
    head = lax.broadcasted_iota(jnp.int32, shape, 0)
    lane = lax.broadcasted_iota(jnp.int32, shape, 2)
    return (lane // HEAD_DIM == head).astype(jnp.float32).astype(dtype)


def spread(rows, lanes):
    return (rows[None] * lanes).reshape(GROUP * PAD, LANES)


def gather_heads(wide, lanes):
    return jnp.sum(wide.reshape(GROUP, PAD, LANES) * lanes, axis=0)


def dot_nt(left, right):
    return lax.dot_general(left, right, (((1,), (1,)), ((), ())), preferred_element_type=jnp.float32)


def dot_tn(left, right):
    return lax.dot_general(left, right, (((0,), (0,)), ((), ())), preferred_element_type=jnp.float32)


def window_probs(wide_query, keys, scores_bias):
    scores = dot_nt(wide_query, keys) + scores_bias
    weights = jnp.exp(scores - jnp.max(scores, axis=-1, keepdims=True))
    return weights / jnp.sum(weights, axis=-1, keepdims=True)


def attend_kernel(kinds, x_ref, w_ref, b_ref, sb_ref, packed_ref, context_ref):
    rows = x_ref[...]
    bias = b_ref[...]
    queries = jnp.dot(rows, w_ref[:, :C], preferred_element_type=jnp.float32) + bias[:, :C]
    packed_ref[:, :C] = (queries * HEAD_DIM ** (-0.5)).astype(jnp.bfloat16)
    keys = jnp.dot(rows, w_ref[:, C : 2 * C], preferred_element_type=jnp.float32)
    packed_ref[:, C : 2 * C] = keys.astype(jnp.bfloat16)
    values = jnp.dot(rows, w_ref[:, 2 * C :], preferred_element_type=jnp.float32) + bias[:, C:]
    packed_ref[:, 2 * C :] = values.astype(jnp.bfloat16)
    lanes = head_lanes(jnp.bfloat16)
    lanes_f32 = head_lanes(jnp.float32)

    def window(step, carry):
        rows = pl.ds(pl.multiple_of(step * PAD, PAD), PAD)
        kind = lax.rem(step, kinds)
        for group in range(GROUPS):
            low = group * LANES
            wide_query = spread(packed_ref[rows, low : low + LANES], lanes)
            keys = packed_ref[rows, C + low : C + low + LANES]
            values = packed_ref[rows, 2 * C + low : 2 * C + low + LANES]
            probs = window_probs(wide_query, keys, sb_ref[kind, group])
            wide = jnp.dot(
                probs.astype(jnp.bfloat16), values, preferred_element_type=jnp.float32
            )
            context_ref[rows, low : low + LANES] = gather_heads(wide, lanes_f32).astype(
                jnp.bfloat16
            )
        return carry

    lax.fori_loop(0, x_ref.shape[0] // PAD, window, 0)


def attend_back_kernel(kinds, packed_ref, dc_ref, sb_ref, dp_ref, db_ref, table_ref):
    lanes = head_lanes(jnp.bfloat16)
    lanes_f32 = head_lanes(jnp.float32)
    db_ref[...] = jnp.zeros_like(db_ref)
    table_ref[...] = jnp.zeros_like(table_ref)
    scale = HEAD_DIM ** (-0.5)

    def window(step, carry):
        rows = pl.ds(pl.multiple_of(step * PAD, PAD), PAD)
        kind = lax.rem(step, kinds)
        for group in range(GROUPS):
            low = group * LANES
            wide_query = spread(packed_ref[rows, low : low + LANES], lanes)
            keys = packed_ref[rows, C + low : C + low + LANES]
            values = packed_ref[rows, 2 * C + low : 2 * C + low + LANES]
            probs = window_probs(wide_query, keys, sb_ref[kind, group])
            wide_grad = spread(dc_ref[rows, low : low + LANES], lanes)
            grad_probs = dot_nt(wide_grad, values)
            grad_values = dot_tn(probs.astype(jnp.bfloat16), wide_grad)
            grad_scores = probs * (
                grad_probs - jnp.sum(probs * grad_probs, axis=-1, keepdims=True)
            )
            table_ref[group] += grad_scores
            scores_bf = grad_scores.astype(jnp.bfloat16)
            wide = jnp.dot(scores_bf, keys, preferred_element_type=jnp.float32)
            grad_query = gather_heads(wide, lanes_f32) * scale
            grad_keys = dot_tn(scores_bf, wide_query)
            dp_ref[rows, low : low + LANES] = grad_query.astype(jnp.bfloat16)
            dp_ref[rows, C + low : C + low + LANES] = grad_keys.astype(jnp.bfloat16)
            dp_ref[rows, 2 * C + low : 2 * C + low + LANES] = grad_values.astype(jnp.bfloat16)
            db_ref[:, low : low + LANES] += jnp.sum(grad_query, axis=0, keepdims=True)
            db_ref[:, C + low : C + low + LANES] += jnp.sum(grad_values, axis=0, keepdims=True)
        return carry

    lax.fori_loop(0, dc_ref.shape[0] // PAD, window, 0)


def in_vmem(count):
    return [pl.BlockSpec(memory_space=pltpu.VMEM)] * count


def attend(window_input, in_weight, in_bias, scores_bias):
    tokens = window_input.shape[0]
    kinds = scores_bias.shape[0]
    return pl.pallas_call(
        lambda *refs: attend_kernel(kinds, *refs),
        out_shape=(
            jax.ShapeDtypeStruct((tokens, 3 * C), jnp.bfloat16),
            jax.ShapeDtypeStruct((tokens, C), jnp.bfloat16),
        ),
        in_specs=in_vmem(4),
        out_specs=tuple(in_vmem(2)),
        cost_estimate=pl.CostEstimate(
            flops=8 * tokens * C * C, bytes_accessed=20 * 2**20, transcendentals=0
        ),
    )(window_input, in_weight, in_bias[None], scores_bias)


def attend_back(packed, grad_context, scores_bias):
    tokens = packed.shape[0]
    kinds = scores_bias.shape[0]
    return pl.pallas_call(
        lambda *refs: attend_back_kernel(kinds, *refs),
        out_shape=(
            jax.ShapeDtypeStruct((tokens, 3 * C), jnp.bfloat16),
            jax.ShapeDtypeStruct((1, 2 * C), jnp.float32),
            jax.ShapeDtypeStruct((GROUPS, GROUP * PAD, PAD), jnp.float32),
        ),
        in_specs=in_vmem(3),
        out_specs=tuple(in_vmem(3)),
        cost_estimate=pl.CostEstimate(
            flops=8 * tokens * C * C, bytes_accessed=40 * 2**20, transcendentals=0
        ),
    )(packed, grad_context, scores_bias)


def enter_grid(rows, shifted):
    if not shifted:
        return rows
    grid = from_padded(rows)
    incoming = swapped(grid[:, :SHIFT], "rows", 0)
    grid = jnp.concatenate([grid[:, SHIFT:], incoming], axis=1)
    return to_padded(jnp.roll(grid, -SHIFT, axis=2))


def leave_grid(rows, shifted):
    if not shifted:
        return rows
    grid = jnp.roll(from_padded(rows), SHIFT, axis=2)
    incoming = swapped(grid[:, WIN - SHIFT :].astype(jnp.bfloat16), "rows", 0).astype(grid.dtype)
    return to_padded(jnp.concatenate([incoming, grid[:, : WIN - SHIFT]], axis=1))


def layer_forward(stream, attn_weights, take_mlp, vectors, scores_bias, shifted, weave):
    in_weight, out_weight = attn_weights
    first_gain, first_offset, in_bias, out_bias = vectors[:4]
    second_gain, second_offset, up_bias, down_bias = vectors[4:]
    normalized, first_standardized, first_scale = layernorm_apply(stream, first_gain, first_offset)
    window_input = enter_grid(weave(normalized.astype(jnp.bfloat16)), shifted)
    window_input = weave(window_input)
    packed, context = attend(window_input, in_weight, in_bias, scores_bias)
    local_context = weave(leave_grid(weave(context), shifted))
    attended = (
        stream
        + jnp.dot(local_context, out_weight, preferred_element_type=jnp.float32)
        + out_bias
    )
    second_normalized, second_standardized, second_scale = layernorm_apply(
        attended, second_gain, second_offset
    )
    hidden = weave(second_normalized.astype(jnp.bfloat16))
    up_weight, down_weight = take_mlp()
    preactivation = jnp.dot(hidden, up_weight, preferred_element_type=jnp.float32) + up_bias
    activated = weave(gelu_value(preactivation).astype(jnp.bfloat16))
    result = (
        attended + jnp.dot(activated, down_weight, preferred_element_type=jnp.float32) + down_bias
    )
    kept = (
        first_standardized,
        first_scale,
        window_input,
        packed,
        local_context,
        second_standardized,
        second_scale,
        hidden,
        preactivation,
        activated,
    )
    return result, kept


def layer_backward(
    grad_flow, weights, vectors, scores_bias, onehot, shifted, kept, weave
):
    in_weight, out_weight, up_weight, down_weight = weights
    first_gain, second_gain = vectors[0], vectors[4]
    (
        first_standardized,
        first_scale,
        window_input,
        packed,
        local_context,
        second_standardized,
        second_scale,
        hidden,
        preactivation,
        activated,
    ) = kept
    grad_bf = grad_flow.astype(jnp.bfloat16)
    grad_down = outer(activated, grad_bf)
    grad_down_bias = token_total(grad_flow)
    grad_pre = back_product(grad_bf, down_weight) * gelu_slope(preactivation)
    grad_pre_bf = weave(grad_pre.astype(jnp.bfloat16))
    grad_up = outer(hidden, grad_pre_bf)
    grad_up_bias = token_total(grad_pre)
    attention_share, second_gain_gradient, second_offset_gradient = layernorm_reverse(
        back_product(grad_pre_bf, up_weight), second_standardized, second_scale, second_gain
    )
    attention_share = weave(attention_share)
    mlp_shards = weave.add(scatter_steps(owner_blocks((grad_up, grad_down))))
    grad_mixed = grad_flow + attention_share
    mixed_bf = grad_mixed.astype(jnp.bfloat16)
    grad_out = outer(local_context, mixed_bf)
    grad_out_bias = token_total(grad_mixed)
    grad_context = weave(back_product(mixed_bf, out_weight).astype(jnp.bfloat16))
    grad_packed, grad_in_bias, table_term = attend_back(
        packed, weave(enter_grid(grad_context, shifted)), scores_bias
    )
    grad_packed = weave(grad_packed)
    grad_in = outer(window_input, grad_packed)
    attn_shards = weave.add(scatter_steps(owner_blocks((grad_in, grad_out))))
    normalized_gradient = weave(leave_grid(weave(back_product(grad_packed, in_weight)), shifted))
    residual_share, first_gain_gradient, first_offset_gradient = layernorm_reverse(
        normalized_gradient, first_standardized, first_scale, first_gain
    )
    grad_table = lax.dot_general(
        onehot,
        table_term.reshape(HEADS, -1),
        (((0,), (1,)), ((), ())),
        precision=lax.Precision.HIGHEST,
    )
    vector_grads = (
        first_gain_gradient,
        first_offset_gradient,
        grad_in_bias.reshape(-1),
        grad_out_bias,
        second_gain_gradient,
        second_offset_gradient,
        grad_up_bias,
        grad_down_bias,
    )
    return grad_mixed + residual_share, mlp_shards, attn_shards, vector_grads, grad_table


class Chain:
    def __init__(self, steps):
        self.steps = steps
        self.state = next(steps)
        self.done = False

    def advance(self):
        following = next(self.steps, None)
        if following is None:
            self.done = True
        else:
            self.state = following

    def finish(self):
        while not self.done:
            self.advance()
        return self.state


class Weave:
    def __init__(self):
        self.chains = []

    def add(self, steps):
        chain = Chain(steps)
        self.chains.append(chain)
        return chain

    def __call__(self, value):
        live = [chain for chain in self.chains if not chain.done]
        for chain in live:
            chain.advance()
        if live:
            value, states = lax.optimization_barrier((value, [chain.state for chain in live]))
            for chain, state in zip(live, states):
                chain.state = state
        return value


def owner_blocks(grads):
    owners = lax.axis_size("dp")
    parts = []
    for grad in grads:
        grad = grad.astype(jnp.bfloat16)
        for low in range(0, grad.shape[1], C):
            parts.append(grad[:, low : low + C].reshape(owners, -1, C))
    return jnp.concatenate(parts, axis=1)


def merge(array, axis_name, bit):
    other = swapped(array, axis_name, bit)
    upper = ((lax.axis_index(axis_name) >> bit) & 1) == 1
    return jnp.where(upper, other, array), jnp.where(upper, array, other)


def double_owner(blocks, bit):
    owners, rows, _ = blocks.shape
    return jnp.stack(merge(blocks, "dp", bit), axis=1).reshape(2 * owners, rows, C)


def double_rows(blocks):
    return jnp.concatenate(merge(blocks, "rows", 0), axis=1)


def gather_steps(piece):
    bits = (lax.axis_size("dp") - 1).bit_length()
    quarters = piece.reshape(2, 2, -1, C)
    blocks = lax.dynamic_index_in_dim(quarters, lax.axis_index("rows"), 1, keepdims=False)
    blocks = blocks.reshape(1, -1, C)
    yield blocks
    for bit in range(bits - 1, 1, -1):
        blocks = double_owner(blocks, bit)
        yield blocks
    half = blocks.shape[1] // 2
    first, second = blocks[:, :half], blocks[:, half:]
    first, second = double_owner(first, 1), double_rows(second)
    yield first, second
    blocks = jnp.concatenate([double_rows(first), double_owner(second, 1)], axis=1)
    yield blocks
    yield double_owner(blocks, 0)


def piece_blocks(pieces):
    parts = []
    for piece in pieces:
        parts.extend(piece[:, low : low + C] for low in range(0, piece.shape[1], C))
    return jnp.concatenate(parts, axis=0)


def columns_of(blocks, count):
    depth = blocks.shape[1] // count
    parts = [
        blocks[:, step * depth : (step + 1) * depth].reshape(-1, C) for step in range(count)
    ]
    return jnp.concatenate(parts, axis=1)


def all_sum(values):
    for axis_name in ("dp", "rows"):
        for bit in range((lax.axis_size(axis_name) - 1).bit_length()):
            values = values + swapped(values, axis_name, bit)
    return values


def from_blocks(block, depth):
    return block.reshape(-1, depth, C).transpose(1, 0, 2).reshape(depth, -1)


def halve(array, axis_name, bit, dim):
    mine = (lax.axis_index(axis_name) >> bit) & 1
    keep = lax.dynamic_index_in_dim(array, mine, dim, keepdims=False)
    away = lax.dynamic_index_in_dim(array, 1 - mine, dim, keepdims=False)
    return add_bf(keep, swapped(away, axis_name, bit))


def add_bf(left, right):
    return (left.astype(jnp.float32) + right.astype(jnp.float32)).astype(jnp.bfloat16)


def halve_owner(blocks, bit):
    owners, rows, _ = blocks.shape
    return halve(blocks.reshape(owners // 2, 2, rows, C), "dp", bit, 1)


def halve_rows(blocks):
    owners, rows, _ = blocks.shape
    return halve(blocks.reshape(owners, 2, rows // 2, C), "rows", 0, 1)


def scatter_steps(blocks):
    bits = (lax.axis_size("dp") - 1).bit_length()
    yield blocks
    blocks = halve_owner(blocks, 0)
    yield blocks
    half = blocks.shape[1] // 2
    first, second = blocks[:, :half], blocks[:, half:]
    first, second = halve_owner(first, 1), halve_rows(second)
    yield first, second
    first, second = halve_rows(first), halve_owner(second, 1)
    both = jnp.concatenate([first, second], axis=1)
    yield both
    for bit in range(2, bits):
        both = halve_owner(both, bit)
        yield both
    low, high = merge(both[0].reshape(2, -1, C), "rows", 0)
    yield jnp.stack([low, high], axis=1).reshape(-1, C).astype(jnp.float32)


def per_device_general(
    images,
    cotangent,
    attn_in_weight,
    attn_out_weight,
    mlp_in_weight,
    mlp_out_weight,
    norm1_gain,
    norm1_bias,
    attn_in_bias,
    attn_out_bias,
    norm2_gain,
    norm2_bias,
    mlp_in_bias,
    mlp_out_bias,
    bias_table,
    region_labels,
    table_index,
):
    owners = lax.axis_size("dp")
    vector_shards = (
        norm1_gain,
        norm1_bias,
        attn_in_bias,
        attn_out_bias,
        norm2_gain,
        norm2_bias,
        mlp_in_bias,
        mlp_out_bias,
    )
    widths = [member.shape[1] for member in vector_shards]
    vector_piece = jnp.concatenate(vector_shards, axis=1).reshape(-1)
    vector_size = vector_piece.shape[0]
    vector_piece = jnp.pad(vector_piece, (0, -vector_size % (32 * C))).reshape(-1, C)
    depth = attn_in_weight.shape[1]
    up_blocks = mlp_in_weight.shape[2] // C

    def attn_piece(layer_no):
        return piece_blocks([attn_in_weight[layer_no], attn_out_weight[layer_no]])

    def mlp_piece(layer_no):
        return piece_blocks([mlp_in_weight[layer_no], mlp_out_weight[layer_no]])

    def attn_split(blocks):
        blocks = blocks[:, : 4 * depth]
        return columns_of(blocks[:, : 3 * depth], 3), blocks[:, 3 * depth :].reshape(-1, C)

    def mlp_split(blocks):
        up, down = blocks[:, : up_blocks * depth], blocks[:, up_blocks * depth :]
        return columns_of(up, up_blocks), down.reshape(-1, C)

    lead = Chain(gather_steps(jnp.concatenate([attn_piece(0), vector_piece], axis=0)))
    lead.advance()
    lead.advance()
    lead.state, first_mlp = lax.optimization_barrier((lead.state, mlp_piece(0)))
    weave = Weave()
    mlp_chains = [weave.add(gather_steps(first_mlp))]
    lead.advance()
    lead.state = weave(lead.state)
    lead.advance()
    lead.state = weave(lead.state)
    lead_blocks = lead.finish()
    vector_all = lead_blocks[:, 4 * depth :].reshape(owners, -1)[:, :vector_size]
    vector_all = vector_all.reshape(owners, LAYERS, -1).astype(jnp.float32)

    def layer_vectors(layer_no):
        start, result = 0, []
        for width in widths:
            result.append(vector_all[:, layer_no, start : start + width].reshape(-1))
            start += width
        return tuple(result)

    def pad_window(values, fill):
        grid = values.reshape(values.shape[:-1] + (WIN, WIN))
        pads = [(0, 0)] * (values.ndim - 1) + [(0, SIDE - WIN)] * 2
        return jnp.pad(grid, pads, constant_values=fill).reshape(values.shape[:-1] + (PAD,))

    def pad_pair(values, fill):
        both = pad_window(jnp.swapaxes(pad_window(values, fill), -1, -2), fill)
        return jnp.swapaxes(both, -1, -2)

    half_index = lax.axis_index("rows")
    local_labels = lax.dynamic_slice_in_dim(region_labels, half_index * WIN, WIN, 0)
    label_tiles = (
        local_labels.reshape(WIN, GRID // WIN, WIN).transpose(1, 0, 2).reshape(GRID // WIN, -1)
    )
    same = label_tiles[:, :, None] == label_tiles[:, None, :]
    real_key = pad_window(jnp.ones((WIN * WIN,), jnp.int32), 0) == 1
    allowed_pair = (
        jnp.broadcast_to(real_key[None, None, :], (1, PAD, PAD)),
        (pad_pair(same.astype(jnp.int32), 1) == 1) & real_key[None, None, :],
    )
    index_pad = pad_pair(table_index, 0)
    onehot = (index_pad.reshape(-1)[:, None] == jnp.arange(REL, dtype=jnp.int32)[None, :]).astype(
        jnp.float32
    )

    def scores_bias_of(layer_no):
        picked = lax.dot_general(
            bias_table[layer_no],
            onehot,
            (((0,), (1,)), ((), ())),
            precision=lax.Precision.HIGHEST,
            preferred_element_type=jnp.float32,
        ).reshape(HEADS, PAD, PAD)
        allowed = allowed_pair[layer_no % 2]
        masked = jnp.where(allowed[:, None], picked[None], NEG)
        return masked.reshape(-1, GROUPS, GROUP * PAD, PAD)

    stream = to_padded(images).astype(jnp.float32)
    vectors = [layer_vectors(layer_no) for layer_no in range(LAYERS)]
    score_biases = [scores_bias_of(layer_no) for layer_no in range(LAYERS)]
    kept_all = []
    attn_chains = [lead]
    weights = []
    for layer_no in range(LAYERS):
        if layer_no + 1 < LAYERS:
            attn_chains.append(weave.add(gather_steps(attn_piece(layer_no + 1))))
        attn_weights = attn_split(attn_chains[layer_no].finish())
        taken = []

        def take_mlp():
            taken.extend(mlp_split(mlp_chains[layer_no].finish()))
            if layer_no + 1 < LAYERS:
                mlp_chains.append(weave.add(gather_steps(mlp_piece(layer_no + 1))))
            return taken

        stream, kept = layer_forward(
            stream,
            attn_weights,
            take_mlp,
            vectors[layer_no],
            score_biases[layer_no],
            layer_no % 2 == 1,
            weave,
        )
        weights.append((*attn_weights, *taken))
        kept_all.append(kept)
    final_out = from_padded(stream.astype(jnp.bfloat16))
    grad_flow = to_padded(cotangent).astype(jnp.float32)
    mlp_all, attn_all, vectors_all, tables_all = ([None] * LAYERS for _ in range(4))
    for layer_no in reversed(range(LAYERS)):
        grad_flow, mlp_all[layer_no], attn_all[layer_no], grads, tables_all[layer_no] = (
            layer_backward(
                grad_flow,
                weights[layer_no],
                vectors[layer_no],
                score_biases[layer_no],
                onehot,
                layer_no % 2 == 1,
                kept_all[layer_no],
                weave,
            )
        )
        vectors_all[layer_no] = jnp.concatenate(grads)
    lengths = [width * owners for width in widths]
    small = jnp.concatenate(vectors_all + [jnp.stack(tables_all).reshape(-1)])
    total = small.shape[0]
    small = jnp.pad(small, (0, -total % (8 * LANES))).reshape(-1, LANES)
    small = all_sum(small).reshape(-1)[:total]
    mlp_all = [chain.finish() for chain in mlp_all]
    attn_all = [chain.finish() for chain in attn_all]
    vector_total = small[: LAYERS * sum(lengths)].reshape(LAYERS, -1)
    table_total = small[LAYERS * sum(lengths) :].reshape(bias_table.shape)
    vector_outs, start = [], 0
    owner = lax.axis_index("dp")
    for width, length in zip(widths, lengths):
        part = vector_total[:, start : start + length]
        vector_outs.append(lax.dynamic_slice_in_dim(part, owner * width, width, 1))
        start += length
    def stacked(blocks, low, high, rows):
        return jnp.stack([from_blocks(block[low * depth : high * depth], rows) for block in blocks])

    down_depth = mlp_out_weight.shape[1]
    grad_up = stacked(mlp_all, 0, up_blocks, depth)
    grad_down = jnp.stack([block[up_blocks * depth :].reshape(down_depth, C) for block in mlp_all])
    grad_in = stacked(attn_all, 0, 3, depth)
    grad_out = stacked(attn_all, 3, 4, depth)
    return (
        final_out,
        from_padded(grad_flow),
        grad_in,
        grad_out,
        grad_up,
        grad_down,
        *vector_outs,
        table_total,
    )


HALF_SEND = PAD // 2
KEYS = WIN * SIDE
WIDE = GROUP * PAD
VEC_ROWS = 32
SUM_ROWS = 24
TABLE_ROW = 16
TABLE_COLS = 256
MESH = pl.DeviceIdType.MESH
VMEM_BYTES = 63 * 2**20
F32 = jnp.float32
BF16 = jnp.bfloat16


class Links:
    def __init__(self, depth_z, send_sems, recv_sems):
        owner = lax.axis_index("dp")
        self.zs = depth_z
        self.r = lax.axis_index("rows")
        self.z = owner // 4
        self.x = lax.rem(owner // 2, 2)
        self.c = lax.rem(owner, 2)
        self.send_sems = send_sems
        self.recv_sems = recv_sems
        self.used = 0

    def place(self, kind, step=0):
        z, x, c, r = self.z, self.x, self.c, self.r
        if kind == "z":
            z = lax.rem(z + step, self.zs)
        elif kind == "x":
            x = 1 - x
        elif kind == "c":
            c = 1 - c
        else:
            r = 1 - r
        return (r, z * 4 + x * 2 + c)

    def greet(self):
        barrier = pltpu.get_barrier_semaphore()
        partners = [self.place("z", step) for step in range(1, self.zs)]
        partners += [self.place(kind) for kind in ("x", "c", "y")]
        for partner in partners:
            pl.semaphore_signal(barrier, inc=1, device_id=partner, device_id_type=MESH)
        pl.semaphore_wait(barrier, len(partners))

    def send(self, src, dst, kind, step=0):
        spot = self.used
        self.used += 1
        copy = pltpu.make_async_remote_copy(
            src_ref=src,
            dst_ref=dst,
            send_sem=self.send_sems.at[spot],
            recv_sem=self.recv_sems.at[spot],
            device_id=self.place(kind, step),
            device_id_type=MESH,
        )
        copy.start()
        return copy


class Gather:
    def __init__(self, links, parts):
        self.links = links
        self.parts = parts
        self.flying = []
        self.sent = []

    def wait(self):
        for copy in self.flying:
            copy.wait_recv()
        self.sent += self.flying
        self.flying = []

    def go(self, kind, pick, step=0):
        for ref, cols, route in self.parts:
            spot = pick(route)
            if spot is not None:
                view = ref.at[spot + (slice(None), cols)]
                self.flying.append(self.links.send(view, view, kind, step))

    def start(self):
        k = self.links
        for step in range(1, k.zs):
            self.go("z", lambda route: (k.z, k.x, k.c, k.r), step)

    def first(self):
        k = self.links
        self.wait()
        every = slice(None)
        self.go("x", lambda route: (every, k.x, k.c, k.r) if route == 0 else None)
        self.go("y", lambda route: (every, k.x, k.c, k.r) if route == 1 else None)

    def second(self):
        k = self.links
        self.wait()
        every = slice(None)
        self.go("y", lambda route: (every, every, k.c, k.r) if route == 0 else None)
        self.go("x", lambda route: (every, k.x, k.c, every) if route == 1 else None)

    def cores(self):
        k = self.links
        self.wait()
        every = slice(None)
        self.go("c", lambda route: (every, every, k.c, every))

    def finish(self):
        self.wait()

    def drain(self):
        for copy in self.sent:
            copy.wait_send()


def add_rows(left, right):
    return (left.astype(F32) + right.astype(F32)).astype(BF16)


class ScatterPart:
    def __init__(self, grad, low, high, route, buffers, out, layer_no):
        self.grad, self.low, self.high, self.route = grad, low, high, route
        self.core_in, self.first_in, self.second_in, self.z_in, self.mine, self.other = buffers
        self.out, self.layer_no = out, layer_no


class Scatter:
    def __init__(self, links, parts):
        self.links = links
        self.parts = parts
        self.flying = []
        self.sent = []

    def wait(self):
        for copy in self.flying:
            copy.wait_recv()
        self.sent += self.flying
        self.flying = []

    def go(self, part, spot, into, kind, step=0):
        view = part.grad.at[spot + (slice(None), pl.ds(part.low, part.high - part.low))]
        self.flying.append(self.links.send(view, into, kind, step))

    def start(self):
        k = self.links
        every = slice(None)
        for part in self.parts:
            self.go(part, (every, every, 1 - k.c, every), part.core_in, "c")

    def first(self):
        k = self.links
        every = slice(None)
        self.wait()

        def one(zi, carry):
            for part in self.parts:
                spot = (zi, every, k.c, every, every, slice(part.low, part.high))
                part.grad[spot] = add_rows(part.grad[spot], part.core_in[zi])
            return carry

        lax.fori_loop(0, k.zs, one, 0)
        for part in self.parts:
            if part.route == 0:
                self.go(part, (every, 1 - k.x, k.c, every), part.first_in, "x")
            else:
                self.go(part, (every, every, k.c, 1 - k.r), part.first_in, "y")

    def second(self):
        k = self.links
        every = slice(None)
        self.wait()

        def one(zi, carry):
            for part in self.parts:
                cols = slice(part.low, part.high)
                if part.route == 0:
                    spot = (zi, k.x, k.c, every, every, cols)
                else:
                    spot = (zi, every, k.c, k.r, every, cols)
                part.grad[spot] = add_rows(part.grad[spot], part.first_in[zi])
            return carry

        lax.fori_loop(0, k.zs, one, 0)
        for part in self.parts:
            if part.route == 0:
                self.go(part, (every, k.x, k.c, 1 - k.r), part.second_in, "y")
            else:
                self.go(part, (every, 1 - k.x, k.c, k.r), part.second_in, "x")

    def third(self):
        k = self.links
        every = slice(None)
        self.wait()

        def one(zi, carry):
            for part in self.parts:
                spot = (zi, k.x, k.c, k.r, every, slice(part.low, part.high))
                part.grad[spot] = add_rows(part.grad[spot], part.second_in[zi])
            return carry

        lax.fori_loop(0, k.zs, one, 0)
        for part in self.parts:
            for step in range(1, k.zs):
                far = lax.rem(k.z + step, k.zs)
                self.go(part, (far, k.x, k.c, k.r), part.z_in.at[step - 1], "z", step)

    def fourth(self):
        k = self.links
        self.wait()
        for part in self.parts:
            spot = (k.z, k.x, k.c, k.r, slice(None), slice(part.low, part.high))
            total = part.grad[spot].astype(F32)
            for step in range(1, k.zs):
                total = total + part.z_in[step - 1].astype(F32)
            part.mine[...] = total.astype(BF16)
            self.flying.append(k.send(part.mine, part.other, "y"))

    def drain(self):
        for copy in self.sent:
            copy.wait_send()

    def finish(self):
        k = self.links
        self.wait()
        for part in self.parts:
            cols = slice(part.low, part.high)
            part.out[part.layer_no, k.r, :, cols] = part.mine[...].astype(F32)
            part.out[part.layer_no, 1 - k.r, :, cols] = part.other[...].astype(F32)


class Total:
    def __init__(self, links, layer_no, sums, buffers):
        self.links = links
        self.place = layer_no
        self.buffers = [buffer.at[layer_no] for buffer in [sums] + buffers]
        self.sent = []

    def start(self):
        own, core_in = self.buffers[:2]
        self.sent.append(self.links.send(own, core_in, "c"))

    def second(self):
        own, core_in, one, x_in = self.buffers[:4]
        self.sent[-1].wait_recv()
        one[...] = own[...] + core_in[...]
        self.sent.append(self.links.send(one, x_in, "x"))

    def third(self):
        one, x_in, two, y_in = self.buffers[2:6]
        self.sent[-1].wait_recv()
        two[...] = one[...] + x_in[...]
        self.sent.append(self.links.send(two, y_in, "y"))

    def fourth(self):
        k = self.links
        two, y_in, three, z_in = self.buffers[4:]
        self.sent[-1].wait_recv()
        three[...] = two[...] + y_in[...]
        z_in[k.z] = three[...]
        self.last = [k.send(three, z_in.at[k.z], "z", far) for far in range(1, k.zs)]
        self.sent += self.last

    def finish(self, out):
        z_in = self.buffers[-1]
        for step in self.last:
            step.wait_recv()
        total = z_in[0]
        for zi in range(1, self.links.zs):
            total = total + z_in[zi]
        out[self.place] = total

    def drain(self):
        for copy in self.sent:
            copy.wait_send()


def pad_keys(values):
    return jnp.concatenate([values, jnp.zeros((PAD - KEYS, values.shape[1]), values.dtype)], axis=0)


def attend_windows(packed, bias_of, probs, context, first, last):
    lanes = head_lanes(BF16)
    lanes_f32 = head_lanes(F32)

    def window(w, carry):
        for group in range(GROUPS):
            low = group * LANES
            wide_query = spread(packed[w, :, low : low + LANES], lanes)
            keys = packed[w, :, C + low : C + low + LANES]
            values = packed[w, :, 2 * C + low : 2 * C + low + LANES]
            scores = dot_nt(keys, wide_query)[:KEYS] + bias_of(w, group)
            weights = jnp.exp(scores - jnp.max(scores, axis=0, keepdims=True))
            part = weights * (1.0 / jnp.sum(weights, axis=0, keepdims=True))
            probs[w * GROUPS + group] = part
            wide = dot_tn(pad_keys(part).astype(BF16), values)
            context[w, :, low : low + LANES] = gather_heads(wide, lanes_f32).astype(BF16)
        return carry

    lax.fori_loop(first, last, window, 0)


def attend_windows_back(packed, probs, grad_context, grad_packed, table, sums, first, last):
    lanes = head_lanes(BF16)
    lanes_f32 = head_lanes(F32)
    scale = HEAD_DIM ** (-0.5)
    if first == 0:
        sums[2:4, :] = jnp.zeros((2, C), F32)
        table[...] = jnp.zeros(table.shape, F32)

    def window(w, carry):
        for group in range(GROUPS):
            low = group * LANES
            wide_query = spread(packed[w, :, low : low + LANES], lanes)
            keys = packed[w, :, C + low : C + low + LANES]
            values = packed[w, :, 2 * C + low : 2 * C + low + LANES]
            wide_grad = spread(grad_context[w, :, low : low + LANES], lanes)
            part = probs[w * GROUPS + group]
            grad_probs = dot_nt(values, wide_grad)[:KEYS]
            product_sum = jnp.sum(part * grad_probs, axis=0, keepdims=True)
            grad_scores = part * (grad_probs - product_sum)
            table[2 * group] += grad_scores[:, :LANES]
            table[2 * group + 1] += grad_scores[:, LANES:]
            part_bf = pad_keys(part).astype(BF16)
            scores_bf = pad_keys(grad_scores).astype(BF16)
            grad_values = jnp.dot(part_bf, wide_grad, preferred_element_type=F32)
            grad_keys = jnp.dot(scores_bf, wide_query, preferred_element_type=F32)
            grad_query = gather_heads(dot_tn(scores_bf, keys), lanes_f32) * scale
            grad_packed[w, :, low : low + LANES] = grad_query.astype(BF16)
            grad_packed[w, :, C + low : C + low + LANES] = grad_keys.astype(BF16)
            grad_packed[w, :, 2 * C + low : 2 * C + low + LANES] = grad_values.astype(BF16)
            sums[2:3, low : low + LANES] += jnp.sum(grad_query, axis=0, keepdims=True)
            sums[3:4, low : low + LANES] += jnp.sum(
                grad_values, axis=0, keepdims=True
            )
        return carry

    lax.fori_loop(first, last, window, 0)


def table_sums(tables, index, sums):
    entry = lax.broadcasted_iota(jnp.int32, (TABLE_COLS, LANES), 0)
    lane = lax.broadcasted_iota(jnp.int32, (8, LANES), 1)
    first = (lane < PAD).astype(F32)

    def eight(block, total):
        low = pl.multiple_of(block * 8, 8)
        tiles = [table[:, pl.ds(low, 8), :] for table in tables]
        spots = index[pl.ds(low, 8), :]
        for j in range(8):
            rows = []
            for tile in tiles:
                one = tile[:, j, :]
                rows += [one * first, one * (1.0 - first)]
            rows = jnp.concatenate(rows, axis=0)
            high = rows.astype(BF16)
            rest = (rows - high.astype(F32)).astype(BF16)
            onehot = (entry == spots[j : j + 1, :]).astype(F32).astype(BF16)
            total = total + dot_nt(jnp.concatenate([high, rest], axis=0), onehot)
        return total

    count = len(tables) * 16
    total = lax.fori_loop(0, KEYS // 8, eight, jnp.zeros((2 * count, TABLE_COLS), F32))
    total = total[:count] + total[count:]
    sums[TABLE_ROW : TABLE_ROW + 8, :TABLE_COLS] = total[:8]
    sums[TABLE_ROW : TABLE_ROW + 8, TABLE_COLS:] = total[8:]


def place_vectors(refs, first_rows, owner, owners, rows):
    rows[...] = jnp.zeros(rows.shape, F32)
    for ref, first in zip(refs, first_rows):
        width = ref.shape[1]
        spot = owner * width
        column = lax.broadcasted_iota(jnp.int32, (width, C), 1)
        place = lax.broadcasted_iota(jnp.int32, (width, C), 0) + lax.rem(spot, C)
        line = jnp.dot(ref[...].astype(F32), (column == place).astype(F32))
        for row in range(owners * width // C):
            here = (spot // C == row).astype(F32)
            for layer_no in range(LAYERS):
                to = layer_no * 12 + first + row
                rows[to : to + 1, :] = line[layer_no : layer_no + 1] * here


def take_vectors(totals, first_rows, owner, owners, outs):
    for out, first in zip(outs, first_rows):
        width = out.shape[1]
        spot = owner * width
        for layer_no in range(LAYERS):
            line = totals[layer_no, pl.ds(first + spot // C, 1), :]
            line = jnp.broadcast_to(line, (8, C))
            line = pltpu.roll(line, lax.rem(C - lax.rem(spot, C), C), 1)
            out[layer_no : layer_no + 1, :] = line[:1, :width]


def make_bias(entries, index, bias):
    entry = lax.broadcasted_iota(jnp.int32, (TABLE_COLS, LANES), 0)
    first = lax.broadcasted_iota(jnp.int32, (entries.shape[0] // 2, LANES), 1) < PAD
    whole_entries = entries[...]
    high = whole_entries.astype(BF16)
    rest = whole_entries - high.astype(F32)
    middle = rest.astype(BF16)
    low_term = (rest - middle.astype(F32)).astype(BF16)
    terms = jnp.concatenate([high, middle, low_term], axis=0)
    count = entries.shape[0]

    def eight(block, carry):
        low = pl.multiple_of(block * 8, 8)
        spots = index[pl.ds(low, 8), :]
        for j in range(8):
            onehot = (entry == spots[j : j + 1, :]).astype(F32).astype(BF16)
            value = jnp.dot(terms, onehot, preferred_element_type=F32)
            value = value[:count] + value[count : 2 * count] + value[2 * count :]
            line = jnp.where(first, value[: count // 2], value[count // 2 :])
            bias[:, pl.ds(low + j, 1), :] = line[:, None, :]
        return carry

    lax.fori_loop(0, KEYS // 8, eight, 0)


def make_masks(label_rows, label_columns, half, masks):
    key = lax.broadcasted_iota(jnp.int32, (KEYS, LANES), 0)
    masks[0] = jnp.where(lax.rem(key, SIDE) < WIN, 0.0, NEG)
    for w in range(2):
        same = label_columns[2 * half + w] == label_rows[2 * half + w]
        masks[1 + w] = jnp.where(same, 0.0, NEG)


def token_rows(ref):
    value = ref[...]
    return value.reshape(-1, value.shape[-1])


def whole(ref, low, high):
    value = ref[:, :, :, :, :, low:high]
    return value.reshape(-1, high - low)


def training_kernel(depth_z, *refs):
    refs = iter(refs)

    def take(count):
        return [next(refs) for _ in range(count)]

    x_ref, cot_ref = take(2)
    shards = take(4)
    vec_refs = take(8)
    entries_ref, index_ref, label_rows, label_columns, perm_ref = take(5)
    final_ref, input_grad_ref = take(2)
    grad_outs = take(4)
    vec_outs = take(8)
    table_out = next(refs)
    weights = [take(4) for _ in range(LAYERS)]
    top_grads = take(4)
    xhat1, xhat2, scale1, scale2, inputs, packed, probs, context, hidden, slope, active = (
        take(2) for _ in range(11)
    )
    stream, grad_flow, grad_rows, rows_bf, more_bf, halo = take(6)
    grad_packed, grad_bf, tables = take(3)
    scatter_buffers = [[take(6) for _ in range(7)] for _ in range(LAYERS)]
    vecs, vec_ref, vec_core, vec_one, vec_x, vec_two, vec_z = take(7)
    bias, masks, totals = take(3)
    sums, *sum_buffers = take(8)
    send_sems, recv_sems = take(2)

    images = x_ref.shape[0]
    windows = images * 2
    tokens = windows * PAD
    ff = shards[2].shape[-1]
    links = Links(depth_z, send_sems, recv_sems)
    every = slice(None)
    mine = (links.z, links.x, links.c, links.r)

    owner = lax.axis_index("dp")
    owners = depth_z * 4
    first_rows = (0, 1, 2, 4, 5, 6, 7, 11)
    place_vectors(vec_refs, first_rows, owner, owners, vecs)
    vec_ref[...] = vecs[...].astype(BF16)
    links.greet()
    vec_sent = [
        links.send(vec_ref, vec_z.at[links.z], "z", far) for far in range(1, depth_z)
    ]
    vec_z[links.z] = vec_ref[...]
    in_parts = [(0, 0, C, 0, 1), (0, C, 3 * C, 1, 0)]
    up_parts = [(2, 0, ff // 2, 0, 1), (2, ff // 2, ff, 1, 0), (1, 0, C, 1, 0)]
    down_parts = [(3, 0, C // 2, 0, 1), (3, C // 2, C, 1, 0)]
    part_sets = (in_parts, up_parts, down_parts)

    def place_own(layer_no, which):
        weights[layer_no][which][mine + (every, every)] = shards[which][layer_no, links.r]

    def gather_of(layer_no, parts):
        return Gather(
            links,
            [
                (weights[layer_no][which], pl.ds(low, high - low), route)
                for which, low, high, route, _ in parts
            ],
        )

    gathers = [[gather_of(layer_no, parts) for parts in part_sets] for layer_no in range(LAYERS)]
    queue = [item for items in gathers for item in items]

    def pass_on(item):
        item.wait()
        spot = queue.index(item) + 1
        if spot < len(queue):
            queue[spot].start()
        item.first()

    place_own(0, 0)
    queue[0].start()
    for which in (1, 2, 3):
        place_own(0, which)
    for which in range(4):
        place_own(1, which)

    def spread_rows(source, target):
        def one(image, carry):
            for row in range(SIDE):
                for side in range(2):
                    if row < WIN:
                        line = source[image, row].astype(F32)[side * WIN : (side + 1) * WIN]
                        line = jnp.concatenate([line, jnp.zeros((1, C), F32)], axis=0)
                    else:
                        line = jnp.zeros((SIDE, C), F32)
                    target[2 * image + side, row * SIDE : (row + 1) * SIDE, :] = line
            return carry

        lax.fori_loop(0, images, one, 0)

    def join_rows(source, target):
        def one(image, carry):
            for row in range(WIN):
                low = row * SIDE
                sides = [source[2 * image + side, low : low + WIN, :] for side in range(2)]
                target[image, row] = jnp.concatenate(sides, axis=0).astype(target.dtype)
            return carry

        lax.fori_loop(0, images, one, 0)

    spread_rows(x_ref, stream)
    for step in vec_sent:
        step.wait_recv()
    total = vec_z[0].astype(F32)
    for zi in range(1, depth_z):
        total = total + vec_z[zi].astype(F32)
    vec_one[...] = total.astype(BF16)
    vec_sent.append(links.send(vec_one, vec_x, "x"))
    pass_on(gathers[0][0])
    make_bias(entries_ref, index_ref, bias)
    make_masks(label_rows, label_columns, links.r, masks)
    vec_sent[-1].wait_recv()
    vec_two[...] = vec_one[...] + vec_x[...]
    vec_sent.append(links.send(vec_two, vec_core, "c"))
    gathers[0][0].second()
    vec_sent[-1].wait_recv()
    vecs[...] = (vec_two[...] + vec_core[...]).astype(F32)

    def vec(layer_no, row):
        spot = layer_no * 12 + row
        return vecs[spot : spot + 1, :]

    def normalize(source, gain, offset, xhat, scale, target):
        def one(w, carry):
            values = source[w]
            average = jnp.mean(values, axis=-1, keepdims=True)
            centered = values - average
            variance = jnp.mean(centered * centered, axis=-1, keepdims=True)
            inverse = lax.rsqrt(variance + EPS)
            standard = centered * inverse
            xhat[w] = standard
            scale[w] = inverse
            target[w] = (standard * gain + offset).astype(BF16)
            return carry

        lax.fori_loop(0, windows, one, 0)

    def normalize_back(source, gain, xhat, scale, layer_no, row_gain):
        def one(w, carry):
            by_gain, by_offset, flow_sum = carry
            values = source[w]
            standard = xhat[w]
            scaled = values * gain
            first = jnp.mean(scaled, axis=-1, keepdims=True)
            second = jnp.mean(scaled * standard, axis=-1, keepdims=True)
            flow = grad_flow[w] + scale[w] * (scaled - first - standard * second)
            grad_flow[w] = flow
            rows_bf[w] = flow.astype(BF16)
            return (
                by_gain + jnp.sum(values * standard, axis=0, keepdims=True),
                by_offset + jnp.sum(values, axis=0, keepdims=True),
                flow_sum + jnp.sum(flow, axis=0, keepdims=True),
            )

        zero = jnp.zeros((1, C), F32)
        by_gain, by_offset, flow_sum = lax.fori_loop(0, windows, one, (zero, zero, zero))
        sums[layer_no, row_gain : row_gain + 1, :] = by_gain
        sums[layer_no, row_gain + 1 : row_gain + 2, :] = by_offset
        return flow_sum

    def enter_start(source, slot):
        return links.send(source.at[:, pl.ds(0, HALF_SEND), :], halo.at[slot], "y")

    def leave_start(source, slot, first, last):
        some = pl.ds(first, last - first)
        rows = pl.ds(HALF_SEND, HALF_SEND)
        return links.send(source.at[some, rows, :], halo.at[slot, some], "y")

    def moved(source, slot, kind, image):
        own = source[2 * image : 2 * image + 2].reshape(2 * PAD, C)
        away = halo[slot, 2 * image : 2 * image + 2].reshape(PAD, C)
        return jnp.dot(perm_ref[2 * kind], own, preferred_element_type=F32) + jnp.dot(
            perm_ref[2 * kind + 1][:, :PAD], away, preferred_element_type=F32
        )

    def move(source, slot, kind, target):
        for image in range(images):
            target[2 * image : 2 * image + 2] = (
                moved(source, slot, kind, image).astype(BF16).reshape(2, PAD, C)
            )

    def project(layer_no):
        rows = token_rows(inputs[layer_no])
        weight = weights[layer_no][0]
        query = jnp.dot(rows, whole(weight, 0, C), preferred_element_type=F32) + vec(layer_no, 2)
        query = query * HEAD_DIM ** (-0.5)
        packed[layer_no][:, :, :C] = query.astype(BF16).reshape(windows, PAD, C)
        keys = jnp.dot(rows, whole(weight, C, 2 * C), preferred_element_type=F32)
        packed[layer_no][:, :, C : 2 * C] = keys.astype(BF16).reshape(windows, PAD, C)
        values = jnp.dot(rows, whole(weight, 2 * C, 3 * C), preferred_element_type=F32)
        values = values + vec(layer_no, 3)
        packed[layer_no][:, :, 2 * C :] = values.astype(BF16).reshape(windows, PAD, C)

    def mix(layer_no):
        rows = token_rows(context[layer_no])
        out = jnp.dot(rows, whole(weights[layer_no][1], 0, C), preferred_element_type=F32)
        stream[...] = stream[...] + (out + vec(layer_no, 4)).reshape(windows, PAD, C)

    def up_columns(layer_no, j):
        cols = pl.ds(pl.multiple_of(j * C, C), C)
        return weights[layer_no][2][:, :, :, :, :, cols].reshape(C, C), cols

    def feed_up(layer_no, first, last):
        rows = token_rows(hidden[layer_no])
        base = layer_no * 12

        def one(j, carry):
            up, cols = up_columns(layer_no, j)
            pre = jnp.dot(rows, up, preferred_element_type=F32) + vecs[pl.ds(base + 7 + j, 1), :]
            half = 0.5 * (1.0 + lax.erf(pre * SQRT_HALF))
            value = (pre * half).astype(BF16)
            steep = half + pre * jnp.exp(-0.5 * pre * pre) * INV_ROOT_TAU
            active[layer_no][:, :, cols] = value.reshape(windows, PAD, C)
            slope[layer_no][:, :, cols] = steep.astype(BF16).reshape(windows, PAD, C)
            return carry

        lax.fori_loop(first, last, one, 0)

    def feed_down(layer_no):
        stream[...] = stream[...] + vec(layer_no, 11).reshape(1, 1, C)

        def one(j, carry):
            cols = pl.ds(pl.multiple_of(j * C, C), C)
            value = active[layer_no][:, :, cols].reshape(tokens, C)
            down = weights[layer_no][3][j].reshape(C, C)
            out = jnp.dot(value, down, preferred_element_type=F32)
            stream[...] = stream[...] + out.reshape(windows, PAD, C)
            return carry

        lax.fori_loop(0, depth_z, one, 0)

    halo_sent = []
    half = windows // 2
    half_z = depth_z // 2
    in0, up0, down0 = gathers[0]
    in1, up1, down1 = gathers[1]

    def bias_of(layer_no, kind_of):
        def one(w, group):
            mask = masks[kind_of(w)]
            tile = layer_no * 2 * GROUPS + 2 * group
            return jnp.concatenate([bias[tile] + mask, bias[tile + 1] + mask], axis=1)

        return one

    def attend_plain(first, last):
        attend_windows(
            packed[0], bias_of(0, lambda w: 0), probs[0], context[0], first, last
        )

    def attend_shifted(first, last):
        attend_windows(
            packed[1],
            bias_of(1, lambda w: 1 + lax.rem(w, 2)),
            probs[1],
            more_bf,
            first,
            last,
        )

    normalize(stream, vec(0, 0), vec(0, 1), xhat1[0], scale1[0], inputs[0])
    pass_on(up0)
    in0.cores()
    in0.finish()
    project(0)
    up0.second()
    pass_on(down0)
    attend_plain(0, half)
    pass_on(in1)
    down0.second()
    up0.cores()
    attend_plain(half, windows)
    up0.finish()
    mix(0)
    normalize(stream, vec(0, 5), vec(0, 6), xhat2[0], scale2[0], hidden[0])
    feed_up(0, 0, half_z)
    pass_on(up1)
    in1.second()
    down0.cores()
    feed_up(0, half_z, depth_z)
    down0.finish()
    feed_down(0)
    normalize(stream, vec(1, 0), vec(1, 1), xhat1[1], scale1[1], rows_bf)
    halo_sent.append(enter_start(rows_bf, 0))
    pass_on(down1)
    up1.second()
    in1.cores()
    halo_sent[-1].wait_recv()
    move(rows_bf, 0, 0, inputs[1])
    halo_sent[-1].wait_send()
    in1.finish()
    project(1)
    attend_shifted(0, half)
    halo_sent.append(leave_start(more_bf, 1, 0, half))
    down1.second()
    up1.cores()
    attend_shifted(half, windows)
    halo_sent.append(leave_start(more_bf, 1, half, windows))
    down1.cores()
    up1.finish()
    for step in halo_sent[-2:]:
        step.wait_recv()
    move(more_bf, 1, 1, context[1])
    for step in halo_sent[-2:]:
        step.wait_send()
    mix(1)
    normalize(stream, vec(1, 5), vec(1, 6), xhat2[1], scale2[1], hidden[1])
    feed_up(1, 0, depth_z)
    down1.finish()
    feed_down(1)

    join_rows(stream, final_ref)
    spread_rows(cot_ref, grad_flow)

    def turn(w, carry):
        rows_bf[w] = grad_flow[w].astype(BF16)
        return carry + jnp.sum(grad_flow[w], axis=0, keepdims=True)

    flow_sum = lax.fori_loop(0, windows, turn, jnp.zeros((1, C), F32))

    grads = [weights[1], top_grads]

    def scatter_of(layer_no, parts, first_buffer):
        return Scatter(
            links,
            [
                ScatterPart(
                    grads[layer_no][which],
                    low,
                    high,
                    route,
                    scatter_buffers[layer_no][first_buffer + number],
                    grad_outs[which],
                    layer_no,
                )
                for number, (which, low, high, _, route) in enumerate(parts)
            ],
        )

    scatters = [
        [scatter_of(layer_no, parts, first) for parts, first in zip(part_sets, (0, 2, 5))]
        for layer_no in range(LAYERS)
    ]

    def down_grads(layer_no):
        grad_down = grads[layer_no][3]

        def one(j, carry):
            cols = pl.ds(pl.multiple_of(j * C, C), C)
            value = active[layer_no][:, :, cols].reshape(tokens, C)
            part = dot_tn(value, token_rows(rows_bf)).astype(BF16)
            grad_down[j] = part.reshape(grad_down.shape[1:])
            return carry

        lax.fori_loop(0, depth_z, one, 0)

    def feed_back(layer_no, first, last):
        grad_up = grads[layer_no][2]
        if first == 0:
            grad_rows[...] = jnp.zeros(grad_rows.shape, F32)

        def one(j, carry):
            flow = token_rows(rows_bf)
            up, cols = up_columns(layer_no, j)
            down = weights[layer_no][3][j].reshape(C, C)
            steep = slope[layer_no][:, :, cols].reshape(tokens, C).astype(F32)
            grad_pre = dot_nt(flow, down) * steep
            sums[layer_no, pl.ds(7 + j, 1), :] = jnp.sum(grad_pre, axis=0, keepdims=True)
            grad_bf[...] = grad_pre.astype(BF16)
            up_part = dot_tn(token_rows(hidden[layer_no]), grad_bf[...]).astype(BF16)
            grad_up[:, :, :, :, :, cols] = up_part.reshape(grad_up.shape[:-1] + (C,))
            back = dot_nt(grad_bf[...], up)
            grad_rows[...] = grad_rows[...] + back.reshape(windows, PAD, C)
            return carry

        lax.fori_loop(first, last, one, 0)

    def mix_back(layer_no):
        flow = token_rows(rows_bf)
        back = dot_nt(flow, whole(weights[layer_no][1], 0, C)).astype(BF16)
        more_bf[...] = back.reshape(windows, PAD, C)

    def out_grads(layer_no):
        part = dot_tn(token_rows(context[layer_no]), token_rows(rows_bf)).astype(BF16)
        grad_out = grads[layer_no][1]
        grad_out[...] = part.reshape(grad_out.shape)

    def project_back(layer_no):
        rows = token_rows(inputs[layer_no])
        grad_in = grads[layer_no][0]
        for low in range(0, 3 * C, C):
            part = grad_packed[:, :, low : low + C].reshape(tokens, C)
            weight_part = dot_tn(rows, part).astype(BF16)
            grad_in[:, :, :, :, :, low : low + C] = weight_part.reshape(
                grad_in.shape[:-1] + (C,)
            )

    def project_rows_back(layer_no):
        total = None
        for low in range(0, 3 * C, C):
            part = grad_packed[:, :, low : low + C].reshape(tokens, C)
            back = dot_nt(part, whole(weights[layer_no][0], low, low + C))
            total = back if total is None else total + back
        grad_rows[...] = total.reshape(windows, PAD, C)

    in1, up1, down1 = scatters[1]
    in0, up0, down0 = scatters[0]

    sums[1, 11:12, :] = flow_sum
    for layer_no in range(LAYERS):
        sums[layer_no, 12:16, :] = jnp.zeros((4, C), F32)
    down_grads(1)
    down1.start()
    feed_back(1, 0, half_z)
    down1.first()
    feed_back(1, half_z, depth_z)
    sums[1, 4:5, :] = normalize_back(grad_rows, vec(1, 5), xhat2[1], scale2[1], 1, 5)
    mix_back(1)
    halo_sent.append(enter_start(more_bf, 2))
    out_grads(1)
    up1.start()
    down1.second()
    halo_sent[-1].wait_recv()
    move(more_bf, 2, 0, rows_bf)
    halo_sent[-1].wait_send()
    up1.first()

    def attend_back(layer_no, source, first, last):
        attend_windows_back(
            packed[layer_no],
            probs[layer_no],
            source,
            grad_packed,
            tables.at[layer_no],
            sums.at[layer_no],
            first,
            last,
        )

    attend_back(1, rows_bf, 0, half)
    down1.third()
    up1.second()
    attend_back(1, rows_bf, half, windows)
    down1.fourth()
    project_rows_back(1)

    def split(w, carry):
        high = grad_rows[w].astype(BF16)
        rows_bf[w] = high
        more_bf[w] = (grad_rows[w] - high.astype(F32)).astype(BF16)
        return carry

    lax.fori_loop(0, windows, split, 0)
    halo_sent.append(leave_start(rows_bf, 3, 0, windows))
    up1.third()
    project_back(1)
    in1.start()
    halo_sent[-1].wait_recv()
    for image in range(images):
        rest = more_bf[2 * image : 2 * image + 2].reshape(2 * PAD, C)
        value = moved(rows_bf, 3, 1, image) + jnp.dot(
            perm_ref[2], rest, preferred_element_type=F32
        )
        grad_rows[2 * image : 2 * image + 2] = value.reshape(2, PAD, C)
    halo_sent[-1].wait_send()
    flow_sum = normalize_back(grad_rows, vec(1, 0), xhat1[1], scale1[1], 1, 0)
    in1.first()
    down1.finish()

    for item in queue:
        item.drain()
    table_sums([tables.at[1]], index_ref, sums.at[1])
    high_sums = Total(links, 1, sums, sum_buffers)
    high_sums.start()
    sums[0, 11:12, :] = flow_sum
    down_grads(0)
    down0.start()
    up1.fourth()
    feed_back(0, 0, half_z)
    in1.second()
    down0.first()
    high_sums.second()
    feed_back(0, half_z, depth_z)
    in1.third()
    up1.finish()
    high_sums.third()
    sums[0, 4:5, :] = normalize_back(grad_rows, vec(0, 5), xhat2[0], scale2[0], 0, 5)
    out_grads(0)
    up0.start()
    mix_back(0)
    down0.second()
    high_sums.fourth()
    attend_back(0, more_bf, 0, half)
    in1.fourth()
    up0.first()
    down0.third()
    attend_back(0, more_bf, half, windows)
    high_sums.finish(totals)
    project_back(0)
    in0.start()
    up0.second()
    down0.fourth()
    project_rows_back(0)
    in1.finish()
    normalize_back(grad_rows, vec(0, 0), xhat1[0], scale1[0], 0, 0)
    table_sums([tables.at[0]], index_ref, sums.at[0])
    low_sums = Total(links, 0, sums, sum_buffers)
    low_sums.start()
    in0.first()
    down0.finish()
    up0.third()

    join_rows(grad_flow, input_grad_ref)
    low_sums.second()
    in0.second()
    low_sums.third()
    up0.fourth()
    in0.third()
    low_sums.fourth()
    up0.finish()
    in0.fourth()
    low_sums.finish(totals)
    take_vectors(totals, first_rows, owner, owners, vec_outs)
    table_out[...] = totals[:, TABLE_ROW:, :]
    in0.finish()
    for step in vec_sent:
        step.wait_send()
    for item in [high_sums, low_sums] + scatters[0] + scatters[1]:
        item.drain()


def shift_matrices():
    spots = 2 * PAD
    kinds = np.zeros((4, spots, spots), np.float32)
    for w in range(2):
        for row in range(WIN):
            for col in range(WIN):
                here = w * PAD + row * SIDE + col
                keep = WIN - SHIFT
                from_w, from_col = (w, col + SHIFT) if col < keep else (1 - w, col - keep)
                if row < keep:
                    there = from_w * PAD + (row + SHIFT) * SIDE + from_col
                    kinds[0, here, there] = 1
                    kinds[2, there, here] = 1
                else:
                    there = from_w * HALF_SEND + (row - keep) * SIDE + from_col
                    kinds[1, here, there] = 1
                    source = w * HALF_SEND + (row - keep) * SIDE + col
                    kinds[3, from_w * PAD + (row - keep) * SIDE + from_col, source] = 1
    return kinds


def hand_over(*refs):
    count = len(refs) // 2
    for source, target in zip(refs[:count], refs[count:]):
        target[...] = source[...]


def one_kernel_fits(owners, depth, down_depth, ff):
    return owners % 4 == 0 and depth % 32 == 0 and down_depth % 32 == 0 and ff == owners // 4 * C


def per_device(*args):
    attn_in_weight, mlp_in_weight, mlp_out_weight = args[2], args[4], args[5]
    sizes = (attn_in_weight.shape[1], mlp_out_weight.shape[1], mlp_in_weight.shape[2])
    if one_kernel_fits(lax.axis_size("dp"), *sizes) and lax.axis_size("rows") == 2:
        return per_device_one_kernel(*args)
    return per_device_general(*args)


def per_device_one_kernel(images, cotangent, *rest):
    shards, vectors = rest[:4], rest[4:12]
    bias_table, region_labels, table_index = rest[12:]
    owners = lax.axis_size("dp")
    depth_z = owners // 4
    owner = lax.axis_index("dp")
    widths = [member.shape[1] for member in vectors]

    def pad_window(values, fill):
        grid = values.reshape(values.shape[:-1] + (WIN, WIN))
        pads = [(0, 0)] * (values.ndim - 1) + [(0, SIDE - WIN)] * 2
        return jnp.pad(grid, pads, constant_values=fill).reshape(values.shape[:-1] + (PAD,))

    def pad_pair(values, fill):
        both = pad_window(jnp.swapaxes(pad_window(values, fill), -1, -2), fill)
        return jnp.swapaxes(both, -1, -2)

    sides = GRID // WIN
    labels = region_labels.reshape(sides, WIN, sides, WIN).transpose(0, 2, 1, 3)
    labels = pad_window(labels.reshape(sides * sides, WIN * WIN), -1)
    label_rows = jnp.tile(labels, (1, 2))[:, None]
    label_columns = jnp.broadcast_to(labels[:, :KEYS, None], labels.shape[:1] + (KEYS, LANES))
    index_keys = pad_pair(table_index, 0).T[:KEYS]
    index_wide = jnp.concatenate([index_keys, index_keys], axis=1)
    entries = jnp.pad(bias_table, ((0, 0), (0, TABLE_COLS - REL), (0, 0)))
    entries = entries.reshape(LAYERS, TABLE_COLS, 2 * GROUPS, 2).transpose(3, 0, 2, 1)
    entries = entries.reshape(-1, TABLE_COLS)
    perms = jnp.asarray(shift_matrices(), BF16)

    windows = images.shape[0] * sides
    tokens = windows * PAD
    split_shards = [shard.reshape(LAYERS, 2, shard.shape[1] // 2, -1) for shard in shards]
    shapes = [(depth_z, 2, 2, 2) + shard.shape[2:] for shard in split_shards]
    ff = shapes[2][-1]

    def rows_of(width, dtype):
        return pltpu.VMEM((windows, PAD, width), dtype)

    scratch = []
    for _ in range(LAYERS):
        scratch += [pltpu.VMEM(shape, BF16) for shape in shapes]
    scratch += [pltpu.VMEM(shape, BF16) for shape in shapes]
    scratch += [rows_of(C, F32)] * 4 + [rows_of(1, F32)] * 4
    scratch += [rows_of(C, BF16)] * 2 + [rows_of(3 * C, BF16)] * 2
    scratch += [pltpu.VMEM((windows * GROUPS, KEYS, WIDE), F32)] * 2
    scratch += [rows_of(C, BF16)] * 4 + [rows_of(ff, BF16)] * 4
    scratch += [rows_of(C, F32)] * 3 + [rows_of(C, BF16)] * 2
    scratch += [pltpu.VMEM((4, windows, HALF_SEND, C), BF16)]
    scratch += [rows_of(3 * C, BF16), pltpu.VMEM((tokens, C), BF16)]
    scratch += [pltpu.VMEM((LAYERS, 2 * GROUPS, KEYS, LANES), F32)]
    for _ in range(LAYERS):
        for which, width in (
            (0, C), (0, 2 * C), (2, ff // 2), (2, ff // 2), (1, C), (3, C // 2), (3, C // 2)
        ):
            tail = (shapes[which][-2], width)
            for lead in ((depth_z, 2, 2), (depth_z, 2), (depth_z,), (depth_z - 1,), (), ()):
                scratch.append(pltpu.VMEM(lead + tail, BF16))
    scratch += [pltpu.VMEM((VEC_ROWS, C), F32)] + [pltpu.VMEM((VEC_ROWS, C), BF16)] * 5
    scratch += [pltpu.VMEM((depth_z, VEC_ROWS, C), BF16)]
    scratch += [pltpu.VMEM((LAYERS * 2 * GROUPS, KEYS, LANES), F32)]
    scratch += [pltpu.VMEM((3, KEYS, LANES), F32), pltpu.VMEM((LAYERS, SUM_ROWS, C), F32)]
    scratch += [pltpu.VMEM((LAYERS, SUM_ROWS, C), F32)] * 7
    scratch += [pltpu.VMEM((LAYERS, depth_z, SUM_ROWS, C), F32)]
    sems = 2 * 7 * (2 * (depth_z + 2) + 1) + 3 * (depth_z + 2) + 9
    scratch += [pltpu.SemaphoreType.DMA((sems,))] * 2

    out_shape = [
        jax.ShapeDtypeStruct(images.shape, BF16),
        jax.ShapeDtypeStruct(images.shape, F32),
        *(jax.ShapeDtypeStruct(shard.shape, F32) for shard in split_shards),
        *(jax.ShapeDtypeStruct(member.shape, F32) for member in vectors),
        jax.ShapeDtypeStruct((LAYERS, SUM_ROWS - TABLE_ROW, C), F32),
    ]
    operands = (images, cotangent, *split_shards, *vectors)
    operands += (entries, index_wide, label_rows, label_columns, perms)
    results = pl.pallas_call(
        lambda *refs: training_kernel(depth_z, *refs),
        out_shape=out_shape,
        in_specs=in_vmem(len(operands)),
        out_specs=in_vmem(len(out_shape)),
        scratch_shapes=scratch,
        compiler_params=pltpu.CompilerParams(
            collective_id=0, has_side_effects=True, vmem_limit_bytes=VMEM_BYTES
        ),
    )(*operands)
    final, input_grad, *rest, table = pl.pallas_call(
        hand_over,
        out_shape=out_shape,
        in_specs=in_vmem(len(out_shape)),
        out_specs=in_vmem(len(out_shape)),
    )(*results)
    weight_grads, vector_outs = rest[:4], rest[4:]
    table = table.reshape(LAYERS, 2 * GROUPS, 2, TABLE_COLS)
    table = table.transpose(0, 3, 1, 2).reshape(LAYERS, TABLE_COLS, HEADS)[:, :REL]
    return (
        final,
        input_grad,
        *(grad.reshape(shard.shape) for grad, shard in zip(weight_grads, shards)),
        *vector_outs,
        table,
    )


def solution(mesh):
    return jax.shard_map(
        per_device,
        mesh=mesh,
        in_specs=(
            P("dp", "rows", None, None),
            P("dp", "rows", None, None),
            P(None, "dp", None),
            P(None, "dp", None),
            P(None, "dp", None),
            P(None, "dp", None),
            P(None, "dp"),
            P(None, "dp"),
            P(None, "dp"),
            P(None, "dp"),
            P(None, "dp"),
            P(None, "dp"),
            P(None, "dp"),
            P(None, "dp"),
            P(),
            P(),
            P(),
        ),
        out_specs=(
            P("dp", "rows", None, None),
            P("dp", "rows", None, None),
            P(None, "dp", None),
            P(None, "dp", None),
            P(None, "dp", None),
            P(None, "dp", None),
            P(None, "dp"),
            P(None, "dp"),
            P(None, "dp"),
            P(None, "dp"),
            P(None, "dp"),
            P(None, "dp"),
            P(None, "dp"),
            P(None, "dp"),
            P(),
        ),
        check_vma=False,
    )
```

```python
import jax
import jax.numpy as jnp
import numpy as np
from jax import lax
from jax.experimental import pallas as pl
from jax.experimental.pallas import tpu as pltpu
from jax.sharding import PartitionSpec as P

C = 512
HEADS = 16
HEAD_DIM = 32
WIN = 7
GRID = 14
SHIFT = 3
LAYERS = 2
REL = 169
SIDE = 8
PAD = SIDE * SIDE
LANES = 128
GROUP = LANES // HEAD_DIM
GROUPS = HEADS // GROUP


EPS = 1e-05
NEG = -1e30
SQRT_HALF = 0.7071067811865476
INV_ROOT_TAU = 0.3989422804014327


def swapped(array, axis, distance):
    return lax.ppermute(array, axis, [(i, i ^ 1 << distance) for i in range(lax.axis_size(axis))])


def product(spec, left, right):
    return jnp.einsum(spec, left, right, preferred_element_type=jnp.float32)


def outer(left, right):
    left_flat = left.reshape(-1, left.shape[-1])
    right_flat = right.reshape(-1, right.shape[-1])
    return lax.dot_general(
        left_flat, right_flat, (((0,), (0,)), ((), ())), preferred_element_type=jnp.float32
    )


def back_product(grad_rows, weight):
    return lax.dot_general(
        grad_rows,
        weight,
        (((grad_rows.ndim - 1,), (1,)), ((), ())),
        preferred_element_type=jnp.float32,
    )


def token_total(values):
    return jnp.sum(values.reshape(-1, values.shape[-1]), axis=0)


def to_padded(grid):
    images, _, cols, channels = grid.shape
    split = grid.reshape(images, WIN, cols // WIN, WIN, channels).transpose(0, 2, 1, 3, 4)
    padded = jnp.pad(split, ((0, 0), (0, 0), (0, SIDE - WIN), (0, SIDE - WIN), (0, 0)))
    return padded.reshape(-1, channels)


def from_padded(rows):
    channels = rows.shape[-1]
    split = rows.reshape(-1, GRID // WIN, SIDE, SIDE, channels)[:, :, :WIN, :WIN]
    return split.transpose(0, 2, 1, 3, 4).reshape(-1, WIN, GRID, channels)


def layernorm_apply(values, gain_vector, offset_vector):
    average = jnp.mean(values, axis=-1, keepdims=True)
    centered_input = values - average
    variance = jnp.mean(centered_input * centered_input, axis=-1, keepdims=True)
    inverse_deviation = lax.rsqrt(variance + EPS)
    standardized = centered_input * inverse_deviation
    return (standardized * gain_vector + offset_vector, standardized, inverse_deviation)


def layernorm_reverse(output_gradient, standardized, inverse_deviation, gain_vector):
    standardized_gradient = output_gradient * gain_vector
    input_gradient_rows = inverse_deviation * (
        standardized_gradient
        - jnp.mean(standardized_gradient, axis=-1, keepdims=True)
        - standardized * jnp.mean(standardized_gradient * standardized, axis=-1, keepdims=True)
    )
    return (
        input_gradient_rows,
        token_total(output_gradient * standardized),
        token_total(output_gradient),
    )


def gelu_value(preactivation):
    return preactivation * 0.5 * (1.0 + lax.erf(preactivation * SQRT_HALF))


def gelu_slope(preactivation):
    return (
        0.5 * (1.0 + lax.erf(preactivation * SQRT_HALF))
        + preactivation * jnp.exp(-0.5 * preactivation * preactivation) * INV_ROOT_TAU
    )


def head_lanes(dtype):
    shape = (GROUP, 1, LANES)
    head = lax.broadcasted_iota(jnp.int32, shape, 0)
    lane = lax.broadcasted_iota(jnp.int32, shape, 2)
    return (lane // HEAD_DIM == head).astype(jnp.float32).astype(dtype)


def spread(rows, lanes):
    return (rows[None] * lanes).reshape(GROUP * PAD, LANES)


def gather_heads(wide, lanes):
    return jnp.sum(wide.reshape(GROUP, PAD, LANES) * lanes, axis=0)


def dot_nt(left, right):
    return lax.dot_general(left, right, (((1,), (1,)), ((), ())), preferred_element_type=jnp.float32)


def dot_tn(left, right):
    return lax.dot_general(left, right, (((0,), (0,)), ((), ())), preferred_element_type=jnp.float32)


def window_probs(wide_query, keys, scores_bias):
    scores = dot_nt(wide_query, keys) + scores_bias
    weights = jnp.exp(scores - jnp.max(scores, axis=-1, keepdims=True))
    return weights / jnp.sum(weights, axis=-1, keepdims=True)


def attend_kernel(kinds, x_ref, w_ref, b_ref, sb_ref, packed_ref, context_ref):
    rows = x_ref[...]
    bias = b_ref[...]
    queries = jnp.dot(rows, w_ref[:, :C], preferred_element_type=jnp.float32) + bias[:, :C]
    packed_ref[:, :C] = (queries * HEAD_DIM ** (-0.5)).astype(jnp.bfloat16)
    keys = jnp.dot(rows, w_ref[:, C : 2 * C], preferred_element_type=jnp.float32)
    packed_ref[:, C : 2 * C] = keys.astype(jnp.bfloat16)
    values = jnp.dot(rows, w_ref[:, 2 * C :], preferred_element_type=jnp.float32) + bias[:, C:]
    packed_ref[:, 2 * C :] = values.astype(jnp.bfloat16)
    lanes = head_lanes(jnp.bfloat16)
    lanes_f32 = head_lanes(jnp.float32)

    def window(step, carry):
        rows = pl.ds(pl.multiple_of(step * PAD, PAD), PAD)
        kind = lax.rem(step, kinds)
        for group in range(GROUPS):
            low = group * LANES
            wide_query = spread(packed_ref[rows, low : low + LANES], lanes)
            keys = packed_ref[rows, C + low : C + low + LANES]
            values = packed_ref[rows, 2 * C + low : 2 * C + low + LANES]
            probs = window_probs(wide_query, keys, sb_ref[kind, group])
            wide = jnp.dot(
                probs.astype(jnp.bfloat16), values, preferred_element_type=jnp.float32
            )
            context_ref[rows, low : low + LANES] = gather_heads(wide, lanes_f32).astype(
                jnp.bfloat16
            )
        return carry

    lax.fori_loop(0, x_ref.shape[0] // PAD, window, 0)


def attend_back_kernel(kinds, packed_ref, dc_ref, sb_ref, dp_ref, db_ref, table_ref):
    lanes = head_lanes(jnp.bfloat16)
    lanes_f32 = head_lanes(jnp.float32)
    db_ref[...] = jnp.zeros_like(db_ref)
    table_ref[...] = jnp.zeros_like(table_ref)
    scale = HEAD_DIM ** (-0.5)

    def window(step, carry):
        rows = pl.ds(pl.multiple_of(step * PAD, PAD), PAD)
        kind = lax.rem(step, kinds)
        for group in range(GROUPS):
            low = group * LANES
            wide_query = spread(packed_ref[rows, low : low + LANES], lanes)
            keys = packed_ref[rows, C + low : C + low + LANES]
            values = packed_ref[rows, 2 * C + low : 2 * C + low + LANES]
            probs = window_probs(wide_query, keys, sb_ref[kind, group])
            wide_grad = spread(dc_ref[rows, low : low + LANES], lanes)
            grad_probs = dot_nt(wide_grad, values)
            grad_values = dot_tn(probs.astype(jnp.bfloat16), wide_grad)
            grad_scores = probs * (
                grad_probs - jnp.sum(probs * grad_probs, axis=-1, keepdims=True)
            )
            table_ref[group] += grad_scores
            scores_bf = grad_scores.astype(jnp.bfloat16)
            wide = jnp.dot(scores_bf, keys, preferred_element_type=jnp.float32)
            grad_query = gather_heads(wide, lanes_f32) * scale
            grad_keys = dot_tn(scores_bf, wide_query)
            dp_ref[rows, low : low + LANES] = grad_query.astype(jnp.bfloat16)
            dp_ref[rows, C + low : C + low + LANES] = grad_keys.astype(jnp.bfloat16)
            dp_ref[rows, 2 * C + low : 2 * C + low + LANES] = grad_values.astype(jnp.bfloat16)
            db_ref[:, low : low + LANES] += jnp.sum(grad_query, axis=0, keepdims=True)
            db_ref[:, C + low : C + low + LANES] += jnp.sum(grad_values, axis=0, keepdims=True)
        return carry

    lax.fori_loop(0, dc_ref.shape[0] // PAD, window, 0)


def in_vmem(count):
    return [pl.BlockSpec(memory_space=pltpu.VMEM)] * count


def attend(window_input, in_weight, in_bias, scores_bias):
    tokens = window_input.shape[0]
    kinds = scores_bias.shape[0]
    return pl.pallas_call(
        lambda *refs: attend_kernel(kinds, *refs),
        out_shape=(
            jax.ShapeDtypeStruct((tokens, 3 * C), jnp.bfloat16),
            jax.ShapeDtypeStruct((tokens, C), jnp.bfloat16),
        ),
        in_specs=in_vmem(4),
        out_specs=tuple(in_vmem(2)),
        cost_estimate=pl.CostEstimate(
            flops=8 * tokens * C * C, bytes_accessed=20 * 2**20, transcendentals=0
        ),
    )(window_input, in_weight, in_bias[None], scores_bias)


def attend_back(packed, grad_context, scores_bias):
    tokens = packed.shape[0]
    kinds = scores_bias.shape[0]
    return pl.pallas_call(
        lambda *refs: attend_back_kernel(kinds, *refs),
        out_shape=(
            jax.ShapeDtypeStruct((tokens, 3 * C), jnp.bfloat16),
            jax.ShapeDtypeStruct((1, 2 * C), jnp.float32),
            jax.ShapeDtypeStruct((GROUPS, GROUP * PAD, PAD), jnp.float32),
        ),
        in_specs=in_vmem(3),
        out_specs=tuple(in_vmem(3)),
        cost_estimate=pl.CostEstimate(
            flops=8 * tokens * C * C, bytes_accessed=40 * 2**20, transcendentals=0
        ),
    )(packed, grad_context, scores_bias)


def enter_grid(rows, shifted):
    if not shifted:
        return rows
    grid = from_padded(rows)
    incoming = swapped(grid[:, :SHIFT], "rows", 0)
    grid = jnp.concatenate([grid[:, SHIFT:], incoming], axis=1)
    return to_padded(jnp.roll(grid, -SHIFT, axis=2))


def leave_grid(rows, shifted):
    if not shifted:
        return rows
    grid = jnp.roll(from_padded(rows), SHIFT, axis=2)
    incoming = swapped(grid[:, WIN - SHIFT :].astype(jnp.bfloat16), "rows", 0).astype(grid.dtype)
    return to_padded(jnp.concatenate([incoming, grid[:, : WIN - SHIFT]], axis=1))


def layer_forward(stream, attn_weights, take_mlp, vectors, scores_bias, shifted, weave):
    in_weight, out_weight = attn_weights
    first_gain, first_offset, in_bias, out_bias = vectors[:4]
    second_gain, second_offset, up_bias, down_bias = vectors[4:]
    normalized, first_standardized, first_scale = layernorm_apply(stream, first_gain, first_offset)
    window_input = enter_grid(weave(normalized.astype(jnp.bfloat16)), shifted)
    window_input = weave(window_input)
    packed, context = attend(window_input, in_weight, in_bias, scores_bias)
    local_context = weave(leave_grid(weave(context), shifted))
    attended = (
        stream
        + jnp.dot(local_context, out_weight, preferred_element_type=jnp.float32)
        + out_bias
    )
    second_normalized, second_standardized, second_scale = layernorm_apply(
        attended, second_gain, second_offset
    )
    hidden = weave(second_normalized.astype(jnp.bfloat16))
    up_weight, down_weight = take_mlp()
    preactivation = jnp.dot(hidden, up_weight, preferred_element_type=jnp.float32) + up_bias
    activated = weave(gelu_value(preactivation).astype(jnp.bfloat16))
    result = (
        attended + jnp.dot(activated, down_weight, preferred_element_type=jnp.float32) + down_bias
    )
    kept = (
        first_standardized,
        first_scale,
        window_input,
        packed,
        local_context,
        second_standardized,
        second_scale,
        hidden,
        preactivation,
        activated,
    )
    return result, kept


def layer_backward(
    grad_flow, weights, vectors, scores_bias, onehot, shifted, kept, weave
):
    in_weight, out_weight, up_weight, down_weight = weights
    first_gain, second_gain = vectors[0], vectors[4]
    (
        first_standardized,
        first_scale,
        window_input,
        packed,
        local_context,
        second_standardized,
        second_scale,
        hidden,
        preactivation,
        activated,
    ) = kept
    grad_bf = grad_flow.astype(jnp.bfloat16)
    grad_down = outer(activated, grad_bf)
    grad_down_bias = token_total(grad_flow)
    grad_pre = back_product(grad_bf, down_weight) * gelu_slope(preactivation)
    grad_pre_bf = weave(grad_pre.astype(jnp.bfloat16))
    grad_up = outer(hidden, grad_pre_bf)
    grad_up_bias = token_total(grad_pre)
    attention_share, second_gain_gradient, second_offset_gradient = layernorm_reverse(
        back_product(grad_pre_bf, up_weight), second_standardized, second_scale, second_gain
    )
    attention_share = weave(attention_share)
    mlp_shards = weave.add(scatter_steps(owner_blocks((grad_up, grad_down))))
    grad_mixed = grad_flow + attention_share
    mixed_bf = grad_mixed.astype(jnp.bfloat16)
    grad_out = outer(local_context, mixed_bf)
    grad_out_bias = token_total(grad_mixed)
    grad_context = weave(back_product(mixed_bf, out_weight).astype(jnp.bfloat16))
    grad_packed, grad_in_bias, table_term = attend_back(
        packed, weave(enter_grid(grad_context, shifted)), scores_bias
    )
    grad_packed = weave(grad_packed)
    grad_in = outer(window_input, grad_packed)
    attn_shards = weave.add(scatter_steps(owner_blocks((grad_in, grad_out))))
    normalized_gradient = weave(leave_grid(weave(back_product(grad_packed, in_weight)), shifted))
    residual_share, first_gain_gradient, first_offset_gradient = layernorm_reverse(
        normalized_gradient, first_standardized, first_scale, first_gain
    )
    grad_table = lax.dot_general(
        onehot,
        table_term.reshape(HEADS, -1),
        (((0,), (1,)), ((), ())),
        precision=lax.Precision.HIGHEST,
    )
    vector_grads = (
        first_gain_gradient,
        first_offset_gradient,
        grad_in_bias.reshape(-1),
        grad_out_bias,
        second_gain_gradient,
        second_offset_gradient,
        grad_up_bias,
        grad_down_bias,
    )
    return grad_mixed + residual_share, mlp_shards, attn_shards, vector_grads, grad_table


class Chain:
    def __init__(self, steps):
        self.steps = steps
        self.state = next(steps)
        self.done = False

    def advance(self):
        following = next(self.steps, None)
        if following is None:
            self.done = True
        else:
            self.state = following

    def finish(self):
        while not self.done:
            self.advance()
        return self.state


class Weave:
    def __init__(self):
        self.chains = []

    def add(self, steps):
        chain = Chain(steps)
        self.chains.append(chain)
        return chain

    def __call__(self, value):
        live = [chain for chain in self.chains if not chain.done]
        for chain in live:
            chain.advance()
        if live:
            value, states = lax.optimization_barrier((value, [chain.state for chain in live]))
            for chain, state in zip(live, states):
                chain.state = state
        return value


def owner_blocks(grads):
    owners = lax.axis_size("dp")
    parts = []
    for grad in grads:
        grad = grad.astype(jnp.bfloat16)
        for low in range(0, grad.shape[1], C):
            parts.append(grad[:, low : low + C].reshape(owners, -1, C))
    return jnp.concatenate(parts, axis=1)


def merge(array, axis_name, bit):
    other = swapped(array, axis_name, bit)
    upper = ((lax.axis_index(axis_name) >> bit) & 1) == 1
    return jnp.where(upper, other, array), jnp.where(upper, array, other)


def double_owner(blocks, bit):
    owners, rows, _ = blocks.shape
    return jnp.stack(merge(blocks, "dp", bit), axis=1).reshape(2 * owners, rows, C)


def double_rows(blocks):
    return jnp.concatenate(merge(blocks, "rows", 0), axis=1)


def gather_steps(piece):
    bits = (lax.axis_size("dp") - 1).bit_length()
    quarters = piece.reshape(2, 2, -1, C)
    blocks = lax.dynamic_index_in_dim(quarters, lax.axis_index("rows"), 1, keepdims=False)
    blocks = blocks.reshape(1, -1, C)
    yield blocks
    for bit in range(bits - 1, 1, -1):
        blocks = double_owner(blocks, bit)
        yield blocks
    half = blocks.shape[1] // 2
    first, second = blocks[:, :half], blocks[:, half:]
    first, second = double_owner(first, 1), double_rows(second)
    yield first, second
    blocks = jnp.concatenate([double_rows(first), double_owner(second, 1)], axis=1)
    yield blocks
    yield double_owner(blocks, 0)


def piece_blocks(pieces):
    parts = []
    for piece in pieces:
        parts.extend(piece[:, low : low + C] for low in range(0, piece.shape[1], C))
    return jnp.concatenate(parts, axis=0)


def columns_of(blocks, count):
    depth = blocks.shape[1] // count
    parts = [
        blocks[:, step * depth : (step + 1) * depth].reshape(-1, C) for step in range(count)
    ]
    return jnp.concatenate(parts, axis=1)


def all_sum(values):
    for axis_name in ("dp", "rows"):
        for bit in range((lax.axis_size(axis_name) - 1).bit_length()):
            values = values + swapped(values, axis_name, bit)
    return values


def from_blocks(block, depth):
    return block.reshape(-1, depth, C).transpose(1, 0, 2).reshape(depth, -1)


def halve(array, axis_name, bit, dim):
    mine = (lax.axis_index(axis_name) >> bit) & 1
    keep = lax.dynamic_index_in_dim(array, mine, dim, keepdims=False)
    away = lax.dynamic_index_in_dim(array, 1 - mine, dim, keepdims=False)
    return add_bf(keep, swapped(away, axis_name, bit))


def add_bf(left, right):
    return (left.astype(jnp.float32) + right.astype(jnp.float32)).astype(jnp.bfloat16)


def halve_owner(blocks, bit):
    owners, rows, _ = blocks.shape
    return halve(blocks.reshape(owners // 2, 2, rows, C), "dp", bit, 1)


def halve_rows(blocks):
    owners, rows, _ = blocks.shape
    return halve(blocks.reshape(owners, 2, rows // 2, C), "rows", 0, 1)


def scatter_steps(blocks):
    bits = (lax.axis_size("dp") - 1).bit_length()
    yield blocks
    blocks = halve_owner(blocks, 0)
    yield blocks
    half = blocks.shape[1] // 2
    first, second = blocks[:, :half], blocks[:, half:]
    first, second = halve_owner(first, 1), halve_rows(second)
    yield first, second
    first, second = halve_rows(first), halve_owner(second, 1)
    both = jnp.concatenate([first, second], axis=1)
    yield both
    for bit in range(2, bits):
        both = halve_owner(both, bit)
        yield both
    low, high = merge(both[0].reshape(2, -1, C), "rows", 0)
    yield jnp.stack([low, high], axis=1).reshape(-1, C).astype(jnp.float32)


def per_device_general(
    images,
    cotangent,
    attn_in_weight,
    attn_out_weight,
    mlp_in_weight,
    mlp_out_weight,
    norm1_gain,
    norm1_bias,
    attn_in_bias,
    attn_out_bias,
    norm2_gain,
    norm2_bias,
    mlp_in_bias,
    mlp_out_bias,
    bias_table,
    region_labels,
    table_index,
):
    owners = lax.axis_size("dp")
    vector_shards = (
        norm1_gain,
        norm1_bias,
        attn_in_bias,
        attn_out_bias,
        norm2_gain,
        norm2_bias,
        mlp_in_bias,
        mlp_out_bias,
    )
    widths = [member.shape[1] for member in vector_shards]
    vector_piece = jnp.concatenate(vector_shards, axis=1).reshape(-1)
    vector_size = vector_piece.shape[0]
    vector_piece = jnp.pad(vector_piece, (0, -vector_size % (32 * C))).reshape(-1, C)
    depth = attn_in_weight.shape[1]
    up_blocks = mlp_in_weight.shape[2] // C

    def attn_piece(layer_no):
        return piece_blocks([attn_in_weight[layer_no], attn_out_weight[layer_no]])

    def mlp_piece(layer_no):
        return piece_blocks([mlp_in_weight[layer_no], mlp_out_weight[layer_no]])

    def attn_split(blocks):
        blocks = blocks[:, : 4 * depth]
        return columns_of(blocks[:, : 3 * depth], 3), blocks[:, 3 * depth :].reshape(-1, C)

    def mlp_split(blocks):
        up, down = blocks[:, : up_blocks * depth], blocks[:, up_blocks * depth :]
        return columns_of(up, up_blocks), down.reshape(-1, C)

    lead = Chain(gather_steps(jnp.concatenate([attn_piece(0), vector_piece], axis=0)))
    lead.advance()
    lead.advance()
    lead.state, first_mlp = lax.optimization_barrier((lead.state, mlp_piece(0)))
    weave = Weave()
    mlp_chains = [weave.add(gather_steps(first_mlp))]
    lead.advance()
    lead.state = weave(lead.state)
    lead.advance()
    lead.state = weave(lead.state)
    lead_blocks = lead.finish()
    vector_all = lead_blocks[:, 4 * depth :].reshape(owners, -1)[:, :vector_size]
    vector_all = vector_all.reshape(owners, LAYERS, -1).astype(jnp.float32)

    def layer_vectors(layer_no):
        start, result = 0, []
        for width in widths:
            result.append(vector_all[:, layer_no, start : start + width].reshape(-1))
            start += width
        return tuple(result)

    def pad_window(values, fill):
        grid = values.reshape(values.shape[:-1] + (WIN, WIN))
        pads = [(0, 0)] * (values.ndim - 1) + [(0, SIDE - WIN)] * 2
        return jnp.pad(grid, pads, constant_values=fill).reshape(values.shape[:-1] + (PAD,))

    def pad_pair(values, fill):
        both = pad_window(jnp.swapaxes(pad_window(values, fill), -1, -2), fill)
        return jnp.swapaxes(both, -1, -2)

    half_index = lax.axis_index("rows")
    local_labels = lax.dynamic_slice_in_dim(region_labels, half_index * WIN, WIN, 0)
    label_tiles = (
        local_labels.reshape(WIN, GRID // WIN, WIN).transpose(1, 0, 2).reshape(GRID // WIN, -1)
    )
    same = label_tiles[:, :, None] == label_tiles[:, None, :]
    real_key = pad_window(jnp.ones((WIN * WIN,), jnp.int32), 0) == 1
    allowed_pair = (
        jnp.broadcast_to(real_key[None, None, :], (1, PAD, PAD)),
        (pad_pair(same.astype(jnp.int32), 1) == 1) & real_key[None, None, :],
    )
    index_pad = pad_pair(table_index, 0)
    onehot = (index_pad.reshape(-1)[:, None] == jnp.arange(REL, dtype=jnp.int32)[None, :]).astype(
        jnp.float32
    )

    def scores_bias_of(layer_no):
        picked = lax.dot_general(
            bias_table[layer_no],
            onehot,
            (((0,), (1,)), ((), ())),
            precision=lax.Precision.HIGHEST,
            preferred_element_type=jnp.float32,
        ).reshape(HEADS, PAD, PAD)
        allowed = allowed_pair[layer_no % 2]
        masked = jnp.where(allowed[:, None], picked[None], NEG)
        return masked.reshape(-1, GROUPS, GROUP * PAD, PAD)

    stream = to_padded(images).astype(jnp.float32)
    vectors = [layer_vectors(layer_no) for layer_no in range(LAYERS)]
    score_biases = [scores_bias_of(layer_no) for layer_no in range(LAYERS)]
    kept_all = []
    attn_chains = [lead]
    weights = []
    for layer_no in range(LAYERS):
        if layer_no + 1 < LAYERS:
            attn_chains.append(weave.add(gather_steps(attn_piece(layer_no + 1))))
        attn_weights = attn_split(attn_chains[layer_no].finish())
        taken = []

        def take_mlp():
            taken.extend(mlp_split(mlp_chains[layer_no].finish()))
            if layer_no + 1 < LAYERS:
                mlp_chains.append(weave.add(gather_steps(mlp_piece(layer_no + 1))))
            return taken

        stream, kept = layer_forward(
            stream,
            attn_weights,
            take_mlp,
            vectors[layer_no],
            score_biases[layer_no],
            layer_no % 2 == 1,
            weave,
        )
        weights.append((*attn_weights, *taken))
        kept_all.append(kept)
    final_out = from_padded(stream.astype(jnp.bfloat16))
    grad_flow = to_padded(cotangent).astype(jnp.float32)
    mlp_all, attn_all, vectors_all, tables_all = ([None] * LAYERS for _ in range(4))
    for layer_no in reversed(range(LAYERS)):
        grad_flow, mlp_all[layer_no], attn_all[layer_no], grads, tables_all[layer_no] = (
            layer_backward(
                grad_flow,
                weights[layer_no],
                vectors[layer_no],
                score_biases[layer_no],
                onehot,
                layer_no % 2 == 1,
                kept_all[layer_no],
                weave,
            )
        )
        vectors_all[layer_no] = jnp.concatenate(grads)
    lengths = [width * owners for width in widths]
    small = jnp.concatenate(vectors_all + [jnp.stack(tables_all).reshape(-1)])
    total = small.shape[0]
    small = jnp.pad(small, (0, -total % (8 * LANES))).reshape(-1, LANES)
    small = all_sum(small).reshape(-1)[:total]
    mlp_all = [chain.finish() for chain in mlp_all]
    attn_all = [chain.finish() for chain in attn_all]
    vector_total = small[: LAYERS * sum(lengths)].reshape(LAYERS, -1)
    table_total = small[LAYERS * sum(lengths) :].reshape(bias_table.shape)
    vector_outs, start = [], 0
    owner = lax.axis_index("dp")
    for width, length in zip(widths, lengths):
        part = vector_total[:, start : start + length]
        vector_outs.append(lax.dynamic_slice_in_dim(part, owner * width, width, 1))
        start += length
    def stacked(blocks, low, high, rows):
        return jnp.stack([from_blocks(block[low * depth : high * depth], rows) for block in blocks])

    down_depth = mlp_out_weight.shape[1]
    grad_up = stacked(mlp_all, 0, up_blocks, depth)
    grad_down = jnp.stack([block[up_blocks * depth :].reshape(down_depth, C) for block in mlp_all])
    grad_in = stacked(attn_all, 0, 3, depth)
    grad_out = stacked(attn_all, 3, 4, depth)
    return (
        final_out,
        from_padded(grad_flow),
        grad_in,
        grad_out,
        grad_up,
        grad_down,
        *vector_outs,
        table_total,
    )


HALF_SEND = PAD // 2
KEYS = WIN * SIDE
WIDE = GROUP * PAD
VEC_ROWS = 32
SUM_ROWS = 24
TABLE_ROW = 16
TABLE_COLS = 256
MESH = pl.DeviceIdType.MESH
VMEM_BYTES = 63 * 2**20
F32 = jnp.float32
BF16 = jnp.bfloat16


class Links:
    def __init__(self, depth_z, send_sems, recv_sems):
        owner = lax.axis_index("dp")
        self.zs = depth_z
        self.r = lax.axis_index("rows")
        self.z = owner // 4
        self.x = lax.rem(owner // 2, 2)
        self.c = lax.rem(owner, 2)
        self.send_sems = send_sems
        self.recv_sems = recv_sems
        self.used = 0

    def place(self, kind, step=0):
        z, x, c, r = self.z, self.x, self.c, self.r
        if kind == "z":
            z = lax.rem(z + step, self.zs)
        elif kind == "x":
            x = 1 - x
        elif kind == "c":
            c = 1 - c
        else:
            r = 1 - r
        return (r, z * 4 + x * 2 + c)

    def greet(self):
        barrier = pltpu.get_barrier_semaphore()
        partners = [self.place("z", step) for step in range(1, self.zs)]
        partners += [self.place(kind) for kind in ("x", "c", "y")]
        for partner in partners:
            pl.semaphore_signal(barrier, inc=1, device_id=partner, device_id_type=MESH)
        pl.semaphore_wait(barrier, len(partners))

    def send(self, src, dst, kind, step=0):
        spot = self.used
        self.used += 1
        copy = pltpu.make_async_remote_copy(
            src_ref=src,
            dst_ref=dst,
            send_sem=self.send_sems.at[spot],
            recv_sem=self.recv_sems.at[spot],
            device_id=self.place(kind, step),
            device_id_type=MESH,
        )
        copy.start()
        return copy


class Gather:
    def __init__(self, links, parts):
        self.links = links
        self.parts = parts
        self.flying = []
        self.sent = []

    def wait(self):
        for copy in self.flying:
            copy.wait_recv()
        self.sent += self.flying
        self.flying = []

    def go(self, kind, pick, step=0):
        for ref, cols, route in self.parts:
            spot = pick(route)
            if spot is not None:
                view = ref.at[spot + (slice(None), cols)]
                self.flying.append(self.links.send(view, view, kind, step))

    def start(self):
        k = self.links
        for step in range(1, k.zs):
            self.go("z", lambda route: (k.z, k.x, k.c, k.r), step)

    def first(self):
        k = self.links
        self.wait()
        every = slice(None)
        self.go("x", lambda route: (every, k.x, k.c, k.r) if route == 0 else None)
        self.go("y", lambda route: (every, k.x, k.c, k.r) if route == 1 else None)

    def second(self):
        k = self.links
        self.wait()
        every = slice(None)
        self.go("y", lambda route: (every, every, k.c, k.r) if route == 0 else None)
        self.go("x", lambda route: (every, k.x, k.c, every) if route == 1 else None)

    def cores(self):
        k = self.links
        self.wait()
        every = slice(None)
        self.go("c", lambda route: (every, every, k.c, every))

    def finish(self):
        self.wait()

    def drain(self):
        for copy in self.sent:
            copy.wait_send()


def add_rows(left, right):
    return (left.astype(F32) + right.astype(F32)).astype(BF16)


class ScatterPart:
    def __init__(self, grad, low, high, route, buffers, out, layer_no):
        self.grad, self.low, self.high, self.route = grad, low, high, route
        self.core_in, self.first_in, self.second_in, self.z_in, self.mine, self.other = buffers
        self.out, self.layer_no = out, layer_no


class Scatter:
    def __init__(self, links, parts):
        self.links = links
        self.parts = parts
        self.flying = []
        self.sent = []

    def wait(self):
        for copy in self.flying:
            copy.wait_recv()
        self.sent += self.flying
        self.flying = []

    def go(self, part, spot, into, kind, step=0):
        view = part.grad.at[spot + (slice(None), pl.ds(part.low, part.high - part.low))]
        self.flying.append(self.links.send(view, into, kind, step))

    def start(self):
        k = self.links
        every = slice(None)
        for part in self.parts:
            self.go(part, (every, every, 1 - k.c, every), part.core_in, "c")

    def first(self):
        k = self.links
        every = slice(None)
        self.wait()

        def one(zi, carry):
            for part in self.parts:
                spot = (zi, every, k.c, every, every, slice(part.low, part.high))
                part.grad[spot] = add_rows(part.grad[spot], part.core_in[zi])
            return carry

        lax.fori_loop(0, k.zs, one, 0)
        for part in self.parts:
            if part.route == 0:
                self.go(part, (every, 1 - k.x, k.c, every), part.first_in, "x")
            else:
                self.go(part, (every, every, k.c, 1 - k.r), part.first_in, "y")

    def second(self):
        k = self.links
        every = slice(None)
        self.wait()

        def one(zi, carry):
            for part in self.parts:
                cols = slice(part.low, part.high)
                if part.route == 0:
                    spot = (zi, k.x, k.c, every, every, cols)
                else:
                    spot = (zi, every, k.c, k.r, every, cols)
                part.grad[spot] = add_rows(part.grad[spot], part.first_in[zi])
            return carry

        lax.fori_loop(0, k.zs, one, 0)
        for part in self.parts:
            if part.route == 0:
                self.go(part, (every, k.x, k.c, 1 - k.r), part.second_in, "y")
            else:
                self.go(part, (every, 1 - k.x, k.c, k.r), part.second_in, "x")

    def third(self):
        k = self.links
        every = slice(None)
        self.wait()

        def one(zi, carry):
            for part in self.parts:
                spot = (zi, k.x, k.c, k.r, every, slice(part.low, part.high))
                part.grad[spot] = add_rows(part.grad[spot], part.second_in[zi])
            return carry

        lax.fori_loop(0, k.zs, one, 0)
        for part in self.parts:
            for step in range(1, k.zs):
                far = lax.rem(k.z + step, k.zs)
                self.go(part, (far, k.x, k.c, k.r), part.z_in.at[step - 1], "z", step)

    def fourth(self):
        k = self.links
        self.wait()
        for part in self.parts:
            spot = (k.z, k.x, k.c, k.r, slice(None), slice(part.low, part.high))
            total = part.grad[spot].astype(F32)
            for step in range(1, k.zs):
                total = total + part.z_in[step - 1].astype(F32)
            part.mine[...] = total.astype(BF16)
            self.flying.append(k.send(part.mine, part.other, "y"))

    def drain(self):
        for copy in self.sent:
            copy.wait_send()

    def finish(self):
        k = self.links
        self.wait()
        for part in self.parts:
            cols = slice(part.low, part.high)
            part.out[part.layer_no, k.r, :, cols] = part.mine[...].astype(F32)
            part.out[part.layer_no, 1 - k.r, :, cols] = part.other[...].astype(F32)


class Total:
    def __init__(self, links, layer_no, sums, buffers):
        self.links = links
        self.place = layer_no
        self.buffers = [buffer.at[layer_no] for buffer in [sums] + buffers]
        self.sent = []

    def start(self):
        own, core_in = self.buffers[:2]
        self.sent.append(self.links.send(own, core_in, "c"))

    def second(self):
        own, core_in, one, x_in = self.buffers[:4]
        self.sent[-1].wait_recv()
        one[...] = own[...] + core_in[...]
        self.sent.append(self.links.send(one, x_in, "x"))

    def third(self):
        one, x_in, two, y_in = self.buffers[2:6]
        self.sent[-1].wait_recv()
        two[...] = one[...] + x_in[...]
        self.sent.append(self.links.send(two, y_in, "y"))

    def fourth(self):
        k = self.links
        two, y_in, three, z_in = self.buffers[4:]
        self.sent[-1].wait_recv()
        three[...] = two[...] + y_in[...]
        z_in[k.z] = three[...]
        self.last = [k.send(three, z_in.at[k.z], "z", far) for far in range(1, k.zs)]
        self.sent += self.last

    def finish(self, out):
        z_in = self.buffers[-1]
        for step in self.last:
            step.wait_recv()
        total = z_in[0]
        for zi in range(1, self.links.zs):
            total = total + z_in[zi]
        out[self.place] = total

    def drain(self):
        for copy in self.sent:
            copy.wait_send()


def pad_keys(values):
    return jnp.concatenate([values, jnp.zeros((PAD - KEYS, values.shape[1]), values.dtype)], axis=0)


def attend_windows(packed, bias_of, probs, context, first, last):
    lanes = head_lanes(BF16)
    lanes_f32 = head_lanes(F32)

    def window(w, carry):
        for group in range(GROUPS):
            low = group * LANES
            wide_query = spread(packed[w, :, low : low + LANES], lanes)
            keys = packed[w, :, C + low : C + low + LANES]
            values = packed[w, :, 2 * C + low : 2 * C + low + LANES]
            scores = dot_nt(keys, wide_query)[:KEYS] + bias_of(w, group)
            weights = jnp.exp(scores - jnp.max(scores, axis=0, keepdims=True))
            part = weights * (1.0 / jnp.sum(weights, axis=0, keepdims=True))
            probs[w * GROUPS + group] = part
            wide = dot_tn(pad_keys(part).astype(BF16), values)
            context[w, :, low : low + LANES] = gather_heads(wide, lanes_f32).astype(BF16)
        return carry

    lax.fori_loop(first, last, window, 0)


def attend_windows_back(packed, probs, grad_context, grad_packed, table, sums, first, last):
    lanes = head_lanes(BF16)
    lanes_f32 = head_lanes(F32)
    scale = HEAD_DIM ** (-0.5)
    if first == 0:
        sums[2:4, :] = jnp.zeros((2, C), F32)
        table[...] = jnp.zeros(table.shape, F32)

    def window(w, carry):
        for group in range(GROUPS):
            low = group * LANES
            wide_query = spread(packed[w, :, low : low + LANES], lanes)
            keys = packed[w, :, C + low : C + low + LANES]
            values = packed[w, :, 2 * C + low : 2 * C + low + LANES]
            wide_grad = spread(grad_context[w, :, low : low + LANES], lanes)
            part = probs[w * GROUPS + group]
            grad_probs = dot_nt(values, wide_grad)[:KEYS]
            product_sum = jnp.sum(part * grad_probs, axis=0, keepdims=True)
            grad_scores = part * (grad_probs - product_sum)
            table[2 * group] += grad_scores[:, :LANES]
            table[2 * group + 1] += grad_scores[:, LANES:]
            part_bf = pad_keys(part).astype(BF16)
            scores_bf = pad_keys(grad_scores).astype(BF16)
            grad_values = jnp.dot(part_bf, wide_grad, preferred_element_type=F32)
            grad_keys = jnp.dot(scores_bf, wide_query, preferred_element_type=F32)
            grad_query = gather_heads(dot_tn(scores_bf, keys), lanes_f32) * scale
            grad_packed[w, :, low : low + LANES] = grad_query.astype(BF16)
            grad_packed[w, :, C + low : C + low + LANES] = grad_keys.astype(BF16)
            grad_packed[w, :, 2 * C + low : 2 * C + low + LANES] = grad_values.astype(BF16)
            sums[2:3, low : low + LANES] += jnp.sum(grad_query, axis=0, keepdims=True)
            sums[3:4, low : low + LANES] += jnp.sum(
                grad_values, axis=0, keepdims=True
            )
        return carry

    lax.fori_loop(first, last, window, 0)


def table_sums(tables, index, sums):
    entry = lax.broadcasted_iota(jnp.int32, (TABLE_COLS, LANES), 0)
    lane = lax.broadcasted_iota(jnp.int32, (8, LANES), 1)
    first = (lane < PAD).astype(F32)

    def eight(block, total):
        low = pl.multiple_of(block * 8, 8)
        tiles = [table[:, pl.ds(low, 8), :] for table in tables]
        spots = index[pl.ds(low, 8), :]
        for j in range(8):
            rows = []
            for tile in tiles:
                one = tile[:, j, :]
                rows += [one * first, one * (1.0 - first)]
            rows = jnp.concatenate(rows, axis=0)
            high = rows.astype(BF16)
            rest = (rows - high.astype(F32)).astype(BF16)
            onehot = (entry == spots[j : j + 1, :]).astype(F32).astype(BF16)
            total = total + dot_nt(jnp.concatenate([high, rest], axis=0), onehot)
        return total

    count = len(tables) * 16
    total = lax.fori_loop(0, KEYS // 8, eight, jnp.zeros((2 * count, TABLE_COLS), F32))
    total = total[:count] + total[count:]
    sums[TABLE_ROW : TABLE_ROW + 8, :TABLE_COLS] = total[:8]
    sums[TABLE_ROW : TABLE_ROW + 8, TABLE_COLS:] = total[8:]


def place_vectors(refs, first_rows, owner, owners, rows):
    rows[...] = jnp.zeros(rows.shape, F32)
    for ref, first in zip(refs, first_rows):
        width = ref.shape[1]
        spot = owner * width
        column = lax.broadcasted_iota(jnp.int32, (width, C), 1)
        place = lax.broadcasted_iota(jnp.int32, (width, C), 0) + lax.rem(spot, C)
        line = jnp.dot(ref[...].astype(F32), (column == place).astype(F32))
        for row in range(owners * width // C):
            here = (spot // C == row).astype(F32)
            for layer_no in range(LAYERS):
                to = layer_no * 12 + first + row
                rows[to : to + 1, :] = line[layer_no : layer_no + 1] * here


def take_vectors(totals, first_rows, owner, owners, outs):
    for out, first in zip(outs, first_rows):
        width = out.shape[1]
        spot = owner * width
        for layer_no in range(LAYERS):
            line = totals[layer_no, pl.ds(first + spot // C, 1), :]
            line = jnp.broadcast_to(line, (8, C))
            line = pltpu.roll(line, lax.rem(C - lax.rem(spot, C), C), 1)
            out[layer_no : layer_no + 1, :] = line[:1, :width]


def make_bias(entries, index, bias):
    entry = lax.broadcasted_iota(jnp.int32, (TABLE_COLS, LANES), 0)
    first = lax.broadcasted_iota(jnp.int32, (entries.shape[0] // 2, LANES), 1) < PAD
    whole_entries = entries[...]
    high = whole_entries.astype(BF16)
    rest = whole_entries - high.astype(F32)
    middle = rest.astype(BF16)
    low_term = (rest - middle.astype(F32)).astype(BF16)
    terms = jnp.concatenate([high, middle, low_term], axis=0)
    count = entries.shape[0]

    def eight(block, carry):
        low = pl.multiple_of(block * 8, 8)
        spots = index[pl.ds(low, 8), :]
        for j in range(8):
            onehot = (entry == spots[j : j + 1, :]).astype(F32).astype(BF16)
            value = jnp.dot(terms, onehot, preferred_element_type=F32)
            value = value[:count] + value[count : 2 * count] + value[2 * count :]
            line = jnp.where(first, value[: count // 2], value[count // 2 :])
            bias[:, pl.ds(low + j, 1), :] = line[:, None, :]
        return carry

    lax.fori_loop(0, KEYS // 8, eight, 0)


def make_masks(label_rows, label_columns, half, masks):
    key = lax.broadcasted_iota(jnp.int32, (KEYS, LANES), 0)
    masks[0] = jnp.where(lax.rem(key, SIDE) < WIN, 0.0, NEG)
    for w in range(2):
        same = label_columns[2 * half + w] == label_rows[2 * half + w]
        masks[1 + w] = jnp.where(same, 0.0, NEG)


def token_rows(ref):
    value = ref[...]
    return value.reshape(-1, value.shape[-1])


def whole(ref, low, high):
    value = ref[:, :, :, :, :, low:high]
    return value.reshape(-1, high - low)


def training_kernel(depth_z, *refs):
    refs = iter(refs)

    def take(count):
        return [next(refs) for _ in range(count)]

    x_ref, cot_ref = take(2)
    shards = take(4)
    vec_refs = take(8)
    entries_ref, index_ref, label_rows, label_columns, perm_ref = take(5)
    final_ref, input_grad_ref = take(2)
    grad_outs = take(4)
    vec_outs = take(8)
    table_out = next(refs)
    weights = [take(4) for _ in range(LAYERS)]
    top_grads = take(4)
    xhat1, xhat2, scale1, scale2, inputs, packed, probs, context, hidden, slope, active = (
        take(2) for _ in range(11)
    )
    stream, grad_flow, grad_rows, rows_bf, more_bf, halo = take(6)
    grad_packed, grad_bf, tables = take(3)
    scatter_buffers = [[take(6) for _ in range(8)] for _ in range(LAYERS)]
    vecs, vec_ref, vec_core, vec_one, vec_x, vec_two, vec_z = take(7)
    bias, masks, totals = take(3)
    sums, *sum_buffers = take(8)
    send_sems, recv_sems = take(2)

    images = x_ref.shape[0]
    windows = images * 2
    tokens = windows * PAD
    ff = shards[2].shape[-1]
    links = Links(depth_z, send_sems, recv_sems)
    every = slice(None)
    mine = (links.z, links.x, links.c, links.r)

    owner = lax.axis_index("dp")
    owners = depth_z * 4
    first_rows = (0, 1, 2, 4, 5, 6, 7, 11)
    place_vectors(vec_refs, first_rows, owner, owners, vecs)
    vec_ref[...] = vecs[...].astype(BF16)
    links.greet()
    vec_sent = [
        links.send(vec_ref, vec_z.at[links.z], "z", far) for far in range(1, depth_z)
    ]
    vec_z[links.z] = vec_ref[...]
    in_parts = [(0, 0, 3 * C // 2, 0, 1), (0, 3 * C // 2, 3 * C, 1, 0)]
    up_parts = [(2, 0, ff // 2, 0, 1), (2, ff // 2, ff, 1, 0)]
    up_parts += [(1, 0, C // 2, 0, 1), (1, C // 2, C, 1, 0)]
    down_parts = [(3, 0, C // 2, 0, 1), (3, C // 2, C, 1, 0)]
    part_sets = (in_parts, up_parts, down_parts)

    def place_own(layer_no, which):
        weights[layer_no][which][mine + (every, every)] = shards[which][layer_no, links.r]

    def gather_of(layer_no, parts):
        return Gather(
            links,
            [
                (weights[layer_no][which], pl.ds(low, high - low), route)
                for which, low, high, route, _ in parts
            ],
        )

    gathers = [[gather_of(layer_no, parts) for parts in part_sets] for layer_no in range(LAYERS)]
    queue = [item for items in gathers for item in items]

    def pass_on(item):
        item.wait()
        spot = queue.index(item) + 1
        if spot < len(queue):
            queue[spot].start()
        item.first()

    place_own(0, 0)
    queue[0].start()
    for which in (1, 2, 3):
        place_own(0, which)
    for which in range(4):
        place_own(1, which)

    def spread_rows(source, target):
        def one(image, carry):
            for row in range(SIDE):
                for side in range(2):
                    if row < WIN:
                        line = source[image, row].astype(F32)[side * WIN : (side + 1) * WIN]
                        line = jnp.concatenate([line, jnp.zeros((1, C), F32)], axis=0)
                    else:
                        line = jnp.zeros((SIDE, C), F32)
                    target[2 * image + side, row * SIDE : (row + 1) * SIDE, :] = line
            return carry

        lax.fori_loop(0, images, one, 0)

    def join_rows(source, target):
        def one(image, carry):
            for row in range(WIN):
                low = row * SIDE
                sides = [source[2 * image + side, low : low + WIN, :] for side in range(2)]
                target[image, row] = jnp.concatenate(sides, axis=0).astype(target.dtype)
            return carry

        lax.fori_loop(0, images, one, 0)

    spread_rows(x_ref, stream)
    for step in vec_sent:
        step.wait_recv()
    total = vec_z[0].astype(F32)
    for zi in range(1, depth_z):
        total = total + vec_z[zi].astype(F32)
    vec_one[...] = total.astype(BF16)
    vec_sent.append(links.send(vec_one, vec_x, "x"))
    pass_on(gathers[0][0])
    make_bias(entries_ref, index_ref, bias)
    make_masks(label_rows, label_columns, links.r, masks)
    vec_sent[-1].wait_recv()
    vec_two[...] = vec_one[...] + vec_x[...]
    vec_sent.append(links.send(vec_two, vec_core, "c"))
    gathers[0][0].second()
    vec_sent[-1].wait_recv()
    vecs[...] = (vec_two[...] + vec_core[...]).astype(F32)

    def vec(layer_no, row):
        spot = layer_no * 12 + row
        return vecs[spot : spot + 1, :]

    def normalize(source, gain, offset, xhat, scale, target):
        def one(w, carry):
            values = source[w]
            average = jnp.mean(values, axis=-1, keepdims=True)
            centered = values - average
            variance = jnp.mean(centered * centered, axis=-1, keepdims=True)
            inverse = lax.rsqrt(variance + EPS)
            standard = centered * inverse
            xhat[w] = standard
            scale[w] = inverse
            target[w] = (standard * gain + offset).astype(BF16)
            return carry

        lax.fori_loop(0, windows, one, 0)

    def normalize_back(source, gain, xhat, scale, layer_no, row_gain):
        def one(w, carry):
            by_gain, by_offset, flow_sum = carry
            values = source[w]
            standard = xhat[w]
            scaled = values * gain
            first = jnp.mean(scaled, axis=-1, keepdims=True)
            second = jnp.mean(scaled * standard, axis=-1, keepdims=True)
            flow = grad_flow[w] + scale[w] * (scaled - first - standard * second)
            grad_flow[w] = flow
            rows_bf[w] = flow.astype(BF16)
            return (
                by_gain + jnp.sum(values * standard, axis=0, keepdims=True),
                by_offset + jnp.sum(values, axis=0, keepdims=True),
                flow_sum + jnp.sum(flow, axis=0, keepdims=True),
            )

        zero = jnp.zeros((1, C), F32)
        by_gain, by_offset, flow_sum = lax.fori_loop(0, windows, one, (zero, zero, zero))
        sums[layer_no, row_gain : row_gain + 1, :] = by_gain
        sums[layer_no, row_gain + 1 : row_gain + 2, :] = by_offset
        return flow_sum

    def enter_start(source, slot):
        return links.send(source.at[:, pl.ds(0, HALF_SEND), :], halo.at[slot], "y")

    def leave_start(source, slot, first, last):
        some = pl.ds(first, last - first)
        rows = pl.ds(HALF_SEND, HALF_SEND)
        return links.send(source.at[some, rows, :], halo.at[slot, some], "y")

    def moved(source, slot, kind, image):
        own = source[2 * image : 2 * image + 2].reshape(2 * PAD, C)
        away = halo[slot, 2 * image : 2 * image + 2].reshape(PAD, C)
        return jnp.dot(perm_ref[2 * kind], own, preferred_element_type=F32) + jnp.dot(
            perm_ref[2 * kind + 1][:, :PAD], away, preferred_element_type=F32
        )

    def move(source, slot, kind, target):
        for image in range(images):
            target[2 * image : 2 * image + 2] = (
                moved(source, slot, kind, image).astype(BF16).reshape(2, PAD, C)
            )

    def project(layer_no):
        rows = token_rows(inputs[layer_no])
        weight = weights[layer_no][0]
        query = jnp.dot(rows, whole(weight, 0, C), preferred_element_type=F32) + vec(layer_no, 2)
        query = query * HEAD_DIM ** (-0.5)
        packed[layer_no][:, :, :C] = query.astype(BF16).reshape(windows, PAD, C)
        keys = jnp.dot(rows, whole(weight, C, 2 * C), preferred_element_type=F32)
        packed[layer_no][:, :, C : 2 * C] = keys.astype(BF16).reshape(windows, PAD, C)
        values = jnp.dot(rows, whole(weight, 2 * C, 3 * C), preferred_element_type=F32)
        values = values + vec(layer_no, 3)
        packed[layer_no][:, :, 2 * C :] = values.astype(BF16).reshape(windows, PAD, C)

    def mix(layer_no):
        rows = token_rows(context[layer_no])
        out = jnp.dot(rows, whole(weights[layer_no][1], 0, C), preferred_element_type=F32)
        stream[...] = stream[...] + (out + vec(layer_no, 4)).reshape(windows, PAD, C)

    def up_columns(layer_no, j):
        cols = pl.ds(pl.multiple_of(j * C, C), C)
        return weights[layer_no][2][:, :, :, :, :, cols].reshape(C, C), cols

    def feed_up(layer_no, first, last):
        rows = token_rows(hidden[layer_no])
        base = layer_no * 12

        def one(j, carry):
            up, cols = up_columns(layer_no, j)
            pre = jnp.dot(rows, up, preferred_element_type=F32) + vecs[pl.ds(base + 7 + j, 1), :]
            half = 0.5 * (1.0 + lax.erf(pre * SQRT_HALF))
            value = (pre * half).astype(BF16)
            steep = half + pre * jnp.exp(-0.5 * pre * pre) * INV_ROOT_TAU
            active[layer_no][:, :, cols] = value.reshape(windows, PAD, C)
            slope[layer_no][:, :, cols] = steep.astype(BF16).reshape(windows, PAD, C)
            return carry

        lax.fori_loop(first, last, one, 0)

    def feed_down(layer_no):
        stream[...] = stream[...] + vec(layer_no, 11).reshape(1, 1, C)

        def one(j, carry):
            cols = pl.ds(pl.multiple_of(j * C, C), C)
            value = active[layer_no][:, :, cols].reshape(tokens, C)
            down = weights[layer_no][3][j].reshape(C, C)
            out = jnp.dot(value, down, preferred_element_type=F32)
            stream[...] = stream[...] + out.reshape(windows, PAD, C)
            return carry

        lax.fori_loop(0, depth_z, one, 0)

    halo_sent = []
    half = windows // 2
    half_z = depth_z // 2
    in0, up0, down0 = gathers[0]
    in1, up1, down1 = gathers[1]

    def bias_of(layer_no, kind_of):
        def one(w, group):
            mask = masks[kind_of(w)]
            tile = layer_no * 2 * GROUPS + 2 * group
            return jnp.concatenate([bias[tile] + mask, bias[tile + 1] + mask], axis=1)

        return one

    def attend_plain(first, last):
        attend_windows(
            packed[0], bias_of(0, lambda w: 0), probs[0], context[0], first, last
        )

    def attend_shifted(first, last):
        attend_windows(
            packed[1],
            bias_of(1, lambda w: 1 + lax.rem(w, 2)),
            probs[1],
            more_bf,
            first,
            last,
        )

    normalize(stream, vec(0, 0), vec(0, 1), xhat1[0], scale1[0], inputs[0])
    pass_on(up0)
    in0.cores()
    in0.finish()
    project(0)
    up0.second()
    pass_on(down0)
    attend_plain(0, half)
    pass_on(in1)
    down0.second()
    up0.cores()
    attend_plain(half, windows)
    up0.finish()
    mix(0)
    normalize(stream, vec(0, 5), vec(0, 6), xhat2[0], scale2[0], hidden[0])
    down0.cores()
    in1.second()
    pass_on(up1)
    feed_up(0, 0, depth_z)
    down0.finish()
    feed_down(0)
    normalize(stream, vec(1, 0), vec(1, 1), xhat1[1], scale1[1], rows_bf)
    halo_sent.append(enter_start(rows_bf, 0))
    pass_on(down1)
    up1.second()
    in1.cores()
    halo_sent[-1].wait_recv()
    move(rows_bf, 0, 0, inputs[1])
    halo_sent[-1].wait_send()
    in1.finish()
    project(1)
    attend_shifted(0, half)
    halo_sent.append(leave_start(more_bf, 1, 0, half))
    down1.second()
    up1.cores()
    attend_shifted(half, windows)
    halo_sent.append(leave_start(more_bf, 1, half, windows))
    down1.cores()
    up1.finish()
    for step in halo_sent[-2:]:
        step.wait_recv()
    move(more_bf, 1, 1, context[1])
    for step in halo_sent[-2:]:
        step.wait_send()
    mix(1)
    normalize(stream, vec(1, 5), vec(1, 6), xhat2[1], scale2[1], hidden[1])
    feed_up(1, 0, depth_z)
    down1.finish()
    feed_down(1)

    join_rows(stream, final_ref)
    spread_rows(cot_ref, grad_flow)

    def turn(w, carry):
        rows_bf[w] = grad_flow[w].astype(BF16)
        return carry + jnp.sum(grad_flow[w], axis=0, keepdims=True)

    flow_sum = lax.fori_loop(0, windows, turn, jnp.zeros((1, C), F32))

    grads = [weights[1], top_grads]

    def scatter_of(layer_no, parts, first_buffer):
        return Scatter(
            links,
            [
                ScatterPart(
                    grads[layer_no][which],
                    low,
                    high,
                    route,
                    scatter_buffers[layer_no][first_buffer + number],
                    grad_outs[which],
                    layer_no,
                )
                for number, (which, low, high, _, route) in enumerate(parts)
            ],
        )

    scatters = [
        [scatter_of(layer_no, parts, first) for parts, first in zip(part_sets, (0, 2, 6))]
        for layer_no in range(LAYERS)
    ]

    def down_grads(layer_no):
        grad_down = grads[layer_no][3]

        def one(j, carry):
            cols = pl.ds(pl.multiple_of(j * C, C), C)
            value = active[layer_no][:, :, cols].reshape(tokens, C)
            part = dot_tn(value, token_rows(rows_bf)).astype(BF16)
            grad_down[j] = part.reshape(grad_down.shape[1:])
            return carry

        lax.fori_loop(0, depth_z, one, 0)

    def feed_back(layer_no, first, last):
        grad_up = grads[layer_no][2]
        if first == 0:
            grad_rows[...] = jnp.zeros(grad_rows.shape, F32)

        def one(j, carry):
            flow = token_rows(rows_bf)
            up, cols = up_columns(layer_no, j)
            down = weights[layer_no][3][j].reshape(C, C)
            steep = slope[layer_no][:, :, cols].reshape(tokens, C).astype(F32)
            grad_pre = dot_nt(flow, down) * steep
            sums[layer_no, pl.ds(7 + j, 1), :] = jnp.sum(grad_pre, axis=0, keepdims=True)
            grad_bf[...] = grad_pre.astype(BF16)
            up_part = dot_tn(token_rows(hidden[layer_no]), grad_bf[...]).astype(BF16)
            grad_up[:, :, :, :, :, cols] = up_part.reshape(grad_up.shape[:-1] + (C,))
            back = dot_nt(grad_bf[...], up)
            grad_rows[...] = grad_rows[...] + back.reshape(windows, PAD, C)
            return carry

        lax.fori_loop(first, last, one, 0)

    def mix_back(layer_no):
        flow = token_rows(rows_bf)
        back = dot_nt(flow, whole(weights[layer_no][1], 0, C)).astype(BF16)
        more_bf[...] = back.reshape(windows, PAD, C)

    def out_grads(layer_no):
        part = dot_tn(token_rows(context[layer_no]), token_rows(rows_bf)).astype(BF16)
        grad_out = grads[layer_no][1]
        grad_out[...] = part.reshape(grad_out.shape)

    def project_back(layer_no):
        rows = token_rows(inputs[layer_no])
        grad_in = grads[layer_no][0]
        for low in range(0, 3 * C, C):
            part = grad_packed[:, :, low : low + C].reshape(tokens, C)
            weight_part = dot_tn(rows, part).astype(BF16)
            grad_in[:, :, :, :, :, low : low + C] = weight_part.reshape(
                grad_in.shape[:-1] + (C,)
            )

    def project_rows_back(layer_no):
        total = None
        for low in range(0, 3 * C, C):
            part = grad_packed[:, :, low : low + C].reshape(tokens, C)
            back = dot_nt(part, whole(weights[layer_no][0], low, low + C))
            total = back if total is None else total + back
        grad_rows[...] = total.reshape(windows, PAD, C)

    in1, up1, down1 = scatters[1]
    in0, up0, down0 = scatters[0]

    sums[1, 11:12, :] = flow_sum
    for layer_no in range(LAYERS):
        sums[layer_no, 12:16, :] = jnp.zeros((4, C), F32)
    down_grads(1)
    down1.start()
    feed_back(1, 0, depth_z)
    down1.first()
    sums[1, 4:5, :] = normalize_back(grad_rows, vec(1, 5), xhat2[1], scale2[1], 1, 5)
    mix_back(1)
    halo_sent.append(enter_start(more_bf, 2))
    out_grads(1)
    up1.start()
    down1.second()
    halo_sent[-1].wait_recv()
    move(more_bf, 2, 0, rows_bf)
    halo_sent[-1].wait_send()
    up1.first()

    def attend_back(layer_no, source, first, last):
        attend_windows_back(
            packed[layer_no],
            probs[layer_no],
            source,
            grad_packed,
            tables.at[layer_no],
            sums.at[layer_no],
            first,
            last,
        )

    attend_back(1, rows_bf, 0, half)
    down1.third()
    up1.second()
    attend_back(1, rows_bf, half, windows)
    down1.fourth()
    project_rows_back(1)

    def split(w, carry):
        high = grad_rows[w].astype(BF16)
        rows_bf[w] = high
        more_bf[w] = (grad_rows[w] - high.astype(F32)).astype(BF16)
        return carry

    lax.fori_loop(0, windows, split, 0)
    halo_sent.append(leave_start(rows_bf, 3, 0, windows))
    up1.third()
    project_back(1)
    in1.start()
    halo_sent[-1].wait_recv()
    for image in range(images):
        rest = more_bf[2 * image : 2 * image + 2].reshape(2 * PAD, C)
        value = moved(rows_bf, 3, 1, image) + jnp.dot(
            perm_ref[2], rest, preferred_element_type=F32
        )
        grad_rows[2 * image : 2 * image + 2] = value.reshape(2, PAD, C)
    halo_sent[-1].wait_send()
    flow_sum = normalize_back(grad_rows, vec(1, 0), xhat1[1], scale1[1], 1, 0)
    in1.first()
    down1.finish()

    for item in queue:
        item.drain()
    table_sums([tables.at[1]], index_ref, sums.at[1])
    high_sums = Total(links, 1, sums, sum_buffers)
    high_sums.start()
    sums[0, 11:12, :] = flow_sum
    down_grads(0)
    down0.start()
    up1.fourth()
    feed_back(0, 0, half_z)
    in1.second()
    high_sums.second()
    feed_back(0, half_z, depth_z)
    down0.first()
    in1.third()
    up1.finish()
    high_sums.third()
    sums[0, 4:5, :] = normalize_back(grad_rows, vec(0, 5), xhat2[0], scale2[0], 0, 5)
    out_grads(0)
    up0.start()
    mix_back(0)
    down0.second()
    high_sums.fourth()
    attend_back(0, more_bf, 0, half)
    in1.fourth()
    up0.first()
    down0.third()
    attend_back(0, more_bf, half, windows)
    high_sums.finish(totals)
    project_back(0)
    in0.start()
    up0.second()
    down0.fourth()
    project_rows_back(0)
    in1.finish()
    normalize_back(grad_rows, vec(0, 0), xhat1[0], scale1[0], 0, 0)
    table_sums([tables.at[0]], index_ref, sums.at[0])
    low_sums = Total(links, 0, sums, sum_buffers)
    low_sums.start()
    in0.first()
    down0.finish()
    up0.third()

    join_rows(grad_flow, input_grad_ref)
    low_sums.second()
    in0.second()
    low_sums.third()
    up0.fourth()
    in0.third()
    low_sums.fourth()
    up0.finish()
    in0.fourth()
    low_sums.finish(totals)
    take_vectors(totals, first_rows, owner, owners, vec_outs)
    table_out[...] = totals[:, TABLE_ROW:, :]
    in0.finish()
    for step in vec_sent:
        step.wait_send()
    for item in [high_sums, low_sums] + scatters[0] + scatters[1]:
        item.drain()


def shift_matrices():
    spots = 2 * PAD
    kinds = np.zeros((4, spots, spots), np.float32)
    for w in range(2):
        for row in range(WIN):
            for col in range(WIN):
                here = w * PAD + row * SIDE + col
                keep = WIN - SHIFT
                from_w, from_col = (w, col + SHIFT) if col < keep else (1 - w, col - keep)
                if row < keep:
                    there = from_w * PAD + (row + SHIFT) * SIDE + from_col
                    kinds[0, here, there] = 1
                    kinds[2, there, here] = 1
                else:
                    there = from_w * HALF_SEND + (row - keep) * SIDE + from_col
                    kinds[1, here, there] = 1
                    source = w * HALF_SEND + (row - keep) * SIDE + col
                    kinds[3, from_w * PAD + (row - keep) * SIDE + from_col, source] = 1
    return kinds


def hand_over(*refs):
    count = len(refs) // 2
    for source, target in zip(refs[:count], refs[count:]):
        target[...] = source[...]


def one_kernel_fits(owners, depth, down_depth, ff):
    return owners % 4 == 0 and depth % 32 == 0 and down_depth % 32 == 0 and ff == owners // 4 * C


def per_device(*args):
    attn_in_weight, mlp_in_weight, mlp_out_weight = args[2], args[4], args[5]
    sizes = (attn_in_weight.shape[1], mlp_out_weight.shape[1], mlp_in_weight.shape[2])
    if one_kernel_fits(lax.axis_size("dp"), *sizes) and lax.axis_size("rows") == 2:
        return per_device_one_kernel(*args)
    return per_device_general(*args)


def per_device_one_kernel(images, cotangent, *rest):
    shards, vectors = rest[:4], rest[4:12]
    bias_table, region_labels, table_index = rest[12:]
    owners = lax.axis_size("dp")
    depth_z = owners // 4
    owner = lax.axis_index("dp")
    widths = [member.shape[1] for member in vectors]

    def pad_window(values, fill):
        grid = values.reshape(values.shape[:-1] + (WIN, WIN))
        pads = [(0, 0)] * (values.ndim - 1) + [(0, SIDE - WIN)] * 2
        return jnp.pad(grid, pads, constant_values=fill).reshape(values.shape[:-1] + (PAD,))

    def pad_pair(values, fill):
        both = pad_window(jnp.swapaxes(pad_window(values, fill), -1, -2), fill)
        return jnp.swapaxes(both, -1, -2)

    sides = GRID // WIN
    labels = region_labels.reshape(sides, WIN, sides, WIN).transpose(0, 2, 1, 3)
    labels = pad_window(labels.reshape(sides * sides, WIN * WIN), -1)
    label_rows = jnp.tile(labels, (1, 2))[:, None]
    label_columns = jnp.broadcast_to(labels[:, :KEYS, None], labels.shape[:1] + (KEYS, LANES))
    index_keys = pad_pair(table_index, 0).T[:KEYS]
    index_wide = jnp.concatenate([index_keys, index_keys], axis=1)
    entries = jnp.pad(bias_table, ((0, 0), (0, TABLE_COLS - REL), (0, 0)))
    entries = entries.reshape(LAYERS, TABLE_COLS, 2 * GROUPS, 2).transpose(3, 0, 2, 1)
    entries = entries.reshape(-1, TABLE_COLS)
    perms = jnp.asarray(shift_matrices(), BF16)

    windows = images.shape[0] * sides
    tokens = windows * PAD
    split_shards = [shard.reshape(LAYERS, 2, shard.shape[1] // 2, -1) for shard in shards]
    shapes = [(depth_z, 2, 2, 2) + shard.shape[2:] for shard in split_shards]
    ff = shapes[2][-1]

    def rows_of(width, dtype):
        return pltpu.VMEM((windows, PAD, width), dtype)

    scratch = []
    for _ in range(LAYERS):
        scratch += [pltpu.VMEM(shape, BF16) for shape in shapes]
    scratch += [pltpu.VMEM(shape, BF16) for shape in shapes]
    scratch += [rows_of(C, F32)] * 4 + [rows_of(1, F32)] * 4
    scratch += [rows_of(C, BF16)] * 2 + [rows_of(3 * C, BF16)] * 2
    scratch += [pltpu.VMEM((windows * GROUPS, KEYS, WIDE), F32)] * 2
    scratch += [rows_of(C, BF16)] * 4 + [rows_of(ff, BF16)] * 4
    scratch += [rows_of(C, F32)] * 3 + [rows_of(C, BF16)] * 2
    scratch += [pltpu.VMEM((4, windows, HALF_SEND, C), BF16)]
    scratch += [rows_of(3 * C, BF16), pltpu.VMEM((tokens, C), BF16)]
    scratch += [pltpu.VMEM((LAYERS, 2 * GROUPS, KEYS, LANES), F32)]
    for _ in range(LAYERS):
        for which, width in ((0, 3 * C), (2, ff), (1, C), (3, C)):
            width = width // 2
            tail = (shapes[which][-2], width)
            leads = [(depth_z, 2, 2), (depth_z, 2), (depth_z,), (depth_z - 1,), (), ()]
            scratch += [pltpu.VMEM(lead + tail, BF16) for lead in leads * 2]
    scratch += [pltpu.VMEM((VEC_ROWS, C), F32)] + [pltpu.VMEM((VEC_ROWS, C), BF16)] * 5
    scratch += [pltpu.VMEM((depth_z, VEC_ROWS, C), BF16)]
    scratch += [pltpu.VMEM((LAYERS * 2 * GROUPS, KEYS, LANES), F32)]
    scratch += [pltpu.VMEM((3, KEYS, LANES), F32), pltpu.VMEM((LAYERS, SUM_ROWS, C), F32)]
    scratch += [pltpu.VMEM((LAYERS, SUM_ROWS, C), F32)] * 7
    scratch += [pltpu.VMEM((LAYERS, depth_z, SUM_ROWS, C), F32)]
    sems = 2 * 8 * (2 * (depth_z + 2) + 1) + 3 * (depth_z + 2) + 9
    scratch += [pltpu.SemaphoreType.DMA((sems,))] * 2

    out_shape = [
        jax.ShapeDtypeStruct(images.shape, BF16),
        jax.ShapeDtypeStruct(images.shape, F32),
        *(jax.ShapeDtypeStruct(shard.shape, F32) for shard in split_shards),
        *(jax.ShapeDtypeStruct(member.shape, F32) for member in vectors),
        jax.ShapeDtypeStruct((LAYERS, SUM_ROWS - TABLE_ROW, C), F32),
    ]
    operands = (images, cotangent, *split_shards, *vectors)
    operands += (entries, index_wide, label_rows, label_columns, perms)
    results = pl.pallas_call(
        lambda *refs: training_kernel(depth_z, *refs),
        out_shape=out_shape,
        in_specs=in_vmem(len(operands)),
        out_specs=in_vmem(len(out_shape)),
        scratch_shapes=scratch,
        compiler_params=pltpu.CompilerParams(
            collective_id=0, has_side_effects=True, vmem_limit_bytes=VMEM_BYTES
        ),
    )(*operands)
    final, input_grad, *rest, table = pl.pallas_call(
        hand_over,
        out_shape=out_shape,
        in_specs=in_vmem(len(out_shape)),
        out_specs=in_vmem(len(out_shape)),
    )(*results)
    weight_grads, vector_outs = rest[:4], rest[4:]
    table = table.reshape(LAYERS, 2 * GROUPS, 2, TABLE_COLS)
    table = table.transpose(0, 3, 1, 2).reshape(LAYERS, TABLE_COLS, HEADS)[:, :REL]
    return (
        final,
        input_grad,
        *(grad.reshape(shard.shape) for grad, shard in zip(weight_grads, shards)),
        *vector_outs,
        table,
    )


def solution(mesh):
    return jax.shard_map(
        per_device,
        mesh=mesh,
        in_specs=(
            P("dp", "rows", None, None),
            P("dp", "rows", None, None),
            P(None, "dp", None),
            P(None, "dp", None),
            P(None, "dp", None),
            P(None, "dp", None),
            P(None, "dp"),
            P(None, "dp"),
            P(None, "dp"),
            P(None, "dp"),
            P(None, "dp"),
            P(None, "dp"),
            P(None, "dp"),
            P(None, "dp"),
            P(),
            P(),
            P(),
        ),
        out_specs=(
            P("dp", "rows", None, None),
            P("dp", "rows", None, None),
            P(None, "dp", None),
            P(None, "dp", None),
            P(None, "dp", None),
            P(None, "dp", None),
            P(None, "dp"),
            P(None, "dp"),
            P(None, "dp"),
            P(None, "dp"),
            P(None, "dp"),
            P(None, "dp"),
            P(None, "dp"),
            P(None, "dp"),
            P(),
        ),
        check_vma=False,
    )
```

```python
import jax
import jax.numpy as jnp
import numpy as np
from jax import lax
from jax.experimental import pallas as pl
from jax.experimental.pallas import tpu as pltpu
from jax.sharding import PartitionSpec as P

C = 512
HEADS = 16
HEAD_DIM = 32
WIN = 7
GRID = 14
SHIFT = 3
LAYERS = 2
REL = 169
SIDE = 8
PAD = SIDE * SIDE
LANES = 128
GROUP = LANES // HEAD_DIM
GROUPS = HEADS // GROUP


EPS = 1e-05
NEG = -1e30
SQRT_HALF = 0.7071067811865476
INV_ROOT_TAU = 0.3989422804014327


def swapped(array, axis, distance):
    return lax.ppermute(array, axis, [(i, i ^ 1 << distance) for i in range(lax.axis_size(axis))])


def product(spec, left, right):
    return jnp.einsum(spec, left, right, preferred_element_type=jnp.float32)


def outer(left, right):
    left_flat = left.reshape(-1, left.shape[-1])
    right_flat = right.reshape(-1, right.shape[-1])
    return lax.dot_general(
        left_flat, right_flat, (((0,), (0,)), ((), ())), preferred_element_type=jnp.float32
    )


def back_product(grad_rows, weight):
    return lax.dot_general(
        grad_rows,
        weight,
        (((grad_rows.ndim - 1,), (1,)), ((), ())),
        preferred_element_type=jnp.float32,
    )


def token_total(values):
    return jnp.sum(values.reshape(-1, values.shape[-1]), axis=0)


def to_padded(grid):
    images, _, cols, channels = grid.shape
    split = grid.reshape(images, WIN, cols // WIN, WIN, channels).transpose(0, 2, 1, 3, 4)
    padded = jnp.pad(split, ((0, 0), (0, 0), (0, SIDE - WIN), (0, SIDE - WIN), (0, 0)))
    return padded.reshape(-1, channels)


def from_padded(rows):
    channels = rows.shape[-1]
    split = rows.reshape(-1, GRID // WIN, SIDE, SIDE, channels)[:, :, :WIN, :WIN]
    return split.transpose(0, 2, 1, 3, 4).reshape(-1, WIN, GRID, channels)


def layernorm_apply(values, gain_vector, offset_vector):
    average = jnp.mean(values, axis=-1, keepdims=True)
    centered_input = values - average
    variance = jnp.mean(centered_input * centered_input, axis=-1, keepdims=True)
    inverse_deviation = lax.rsqrt(variance + EPS)
    standardized = centered_input * inverse_deviation
    return (standardized * gain_vector + offset_vector, standardized, inverse_deviation)


def layernorm_reverse(output_gradient, standardized, inverse_deviation, gain_vector):
    standardized_gradient = output_gradient * gain_vector
    input_gradient_rows = inverse_deviation * (
        standardized_gradient
        - jnp.mean(standardized_gradient, axis=-1, keepdims=True)
        - standardized * jnp.mean(standardized_gradient * standardized, axis=-1, keepdims=True)
    )
    return (
        input_gradient_rows,
        token_total(output_gradient * standardized),
        token_total(output_gradient),
    )


def gelu_value(preactivation):
    return preactivation * 0.5 * (1.0 + lax.erf(preactivation * SQRT_HALF))


def gelu_slope(preactivation):
    return (
        0.5 * (1.0 + lax.erf(preactivation * SQRT_HALF))
        + preactivation * jnp.exp(-0.5 * preactivation * preactivation) * INV_ROOT_TAU
    )


def head_lanes(dtype):
    shape = (GROUP, 1, LANES)
    head = lax.broadcasted_iota(jnp.int32, shape, 0)
    lane = lax.broadcasted_iota(jnp.int32, shape, 2)
    return (lane // HEAD_DIM == head).astype(jnp.float32).astype(dtype)


def spread(rows, lanes):
    return (rows[None] * lanes).reshape(GROUP * PAD, LANES)


def gather_heads(wide, lanes):
    return jnp.sum(wide.reshape(GROUP, PAD, LANES) * lanes, axis=0)


def dot_nt(left, right):
    return lax.dot_general(left, right, (((1,), (1,)), ((), ())), preferred_element_type=jnp.float32)


def dot_tn(left, right):
    return lax.dot_general(left, right, (((0,), (0,)), ((), ())), preferred_element_type=jnp.float32)


def window_probs(wide_query, keys, scores_bias):
    scores = dot_nt(wide_query, keys) + scores_bias
    weights = jnp.exp(scores - jnp.max(scores, axis=-1, keepdims=True))
    return weights / jnp.sum(weights, axis=-1, keepdims=True)


def attend_kernel(kinds, x_ref, w_ref, b_ref, sb_ref, packed_ref, context_ref):
    rows = x_ref[...]
    bias = b_ref[...]
    queries = jnp.dot(rows, w_ref[:, :C], preferred_element_type=jnp.float32) + bias[:, :C]
    packed_ref[:, :C] = (queries * HEAD_DIM ** (-0.5)).astype(jnp.bfloat16)
    keys = jnp.dot(rows, w_ref[:, C : 2 * C], preferred_element_type=jnp.float32)
    packed_ref[:, C : 2 * C] = keys.astype(jnp.bfloat16)
    values = jnp.dot(rows, w_ref[:, 2 * C :], preferred_element_type=jnp.float32) + bias[:, C:]
    packed_ref[:, 2 * C :] = values.astype(jnp.bfloat16)
    lanes = head_lanes(jnp.bfloat16)
    lanes_f32 = head_lanes(jnp.float32)

    def window(step, carry):
        rows = pl.ds(pl.multiple_of(step * PAD, PAD), PAD)
        kind = lax.rem(step, kinds)
        for group in range(GROUPS):
            low = group * LANES
            wide_query = spread(packed_ref[rows, low : low + LANES], lanes)
            keys = packed_ref[rows, C + low : C + low + LANES]
            values = packed_ref[rows, 2 * C + low : 2 * C + low + LANES]
            probs = window_probs(wide_query, keys, sb_ref[kind, group])
            wide = jnp.dot(
                probs.astype(jnp.bfloat16), values, preferred_element_type=jnp.float32
            )
            context_ref[rows, low : low + LANES] = gather_heads(wide, lanes_f32).astype(
                jnp.bfloat16
            )
        return carry

    lax.fori_loop(0, x_ref.shape[0] // PAD, window, 0)


def attend_back_kernel(kinds, packed_ref, dc_ref, sb_ref, dp_ref, db_ref, table_ref):
    lanes = head_lanes(jnp.bfloat16)
    lanes_f32 = head_lanes(jnp.float32)
    db_ref[...] = jnp.zeros_like(db_ref)
    table_ref[...] = jnp.zeros_like(table_ref)
    scale = HEAD_DIM ** (-0.5)

    def window(step, carry):
        rows = pl.ds(pl.multiple_of(step * PAD, PAD), PAD)
        kind = lax.rem(step, kinds)
        for group in range(GROUPS):
            low = group * LANES
            wide_query = spread(packed_ref[rows, low : low + LANES], lanes)
            keys = packed_ref[rows, C + low : C + low + LANES]
            values = packed_ref[rows, 2 * C + low : 2 * C + low + LANES]
            probs = window_probs(wide_query, keys, sb_ref[kind, group])
            wide_grad = spread(dc_ref[rows, low : low + LANES], lanes)
            grad_probs = dot_nt(wide_grad, values)
            grad_values = dot_tn(probs.astype(jnp.bfloat16), wide_grad)
            grad_scores = probs * (
                grad_probs - jnp.sum(probs * grad_probs, axis=-1, keepdims=True)
            )
            table_ref[group] += grad_scores
            scores_bf = grad_scores.astype(jnp.bfloat16)
            wide = jnp.dot(scores_bf, keys, preferred_element_type=jnp.float32)
            grad_query = gather_heads(wide, lanes_f32) * scale
            grad_keys = dot_tn(scores_bf, wide_query)
            dp_ref[rows, low : low + LANES] = grad_query.astype(jnp.bfloat16)
            dp_ref[rows, C + low : C + low + LANES] = grad_keys.astype(jnp.bfloat16)
            dp_ref[rows, 2 * C + low : 2 * C + low + LANES] = grad_values.astype(jnp.bfloat16)
            db_ref[:, low : low + LANES] += jnp.sum(grad_query, axis=0, keepdims=True)
            db_ref[:, C + low : C + low + LANES] += jnp.sum(grad_values, axis=0, keepdims=True)
        return carry

    lax.fori_loop(0, dc_ref.shape[0] // PAD, window, 0)


def in_vmem(count):
    return [pl.BlockSpec(memory_space=pltpu.VMEM)] * count


def attend(window_input, in_weight, in_bias, scores_bias):
    tokens = window_input.shape[0]
    kinds = scores_bias.shape[0]
    return pl.pallas_call(
        lambda *refs: attend_kernel(kinds, *refs),
        out_shape=(
            jax.ShapeDtypeStruct((tokens, 3 * C), jnp.bfloat16),
            jax.ShapeDtypeStruct((tokens, C), jnp.bfloat16),
        ),
        in_specs=in_vmem(4),
        out_specs=tuple(in_vmem(2)),
        cost_estimate=pl.CostEstimate(
            flops=8 * tokens * C * C, bytes_accessed=20 * 2**20, transcendentals=0
        ),
    )(window_input, in_weight, in_bias[None], scores_bias)


def attend_back(packed, grad_context, scores_bias):
    tokens = packed.shape[0]
    kinds = scores_bias.shape[0]
    return pl.pallas_call(
        lambda *refs: attend_back_kernel(kinds, *refs),
        out_shape=(
            jax.ShapeDtypeStruct((tokens, 3 * C), jnp.bfloat16),
            jax.ShapeDtypeStruct((1, 2 * C), jnp.float32),
            jax.ShapeDtypeStruct((GROUPS, GROUP * PAD, PAD), jnp.float32),
        ),
        in_specs=in_vmem(3),
        out_specs=tuple(in_vmem(3)),
        cost_estimate=pl.CostEstimate(
            flops=8 * tokens * C * C, bytes_accessed=40 * 2**20, transcendentals=0
        ),
    )(packed, grad_context, scores_bias)


def enter_grid(rows, shifted):
    if not shifted:
        return rows
    grid = from_padded(rows)
    incoming = swapped(grid[:, :SHIFT], "rows", 0)
    grid = jnp.concatenate([grid[:, SHIFT:], incoming], axis=1)
    return to_padded(jnp.roll(grid, -SHIFT, axis=2))


def leave_grid(rows, shifted):
    if not shifted:
        return rows
    grid = jnp.roll(from_padded(rows), SHIFT, axis=2)
    incoming = swapped(grid[:, WIN - SHIFT :].astype(jnp.bfloat16), "rows", 0).astype(grid.dtype)
    return to_padded(jnp.concatenate([incoming, grid[:, : WIN - SHIFT]], axis=1))


def layer_forward(stream, attn_weights, take_mlp, vectors, scores_bias, shifted, weave):
    in_weight, out_weight = attn_weights
    first_gain, first_offset, in_bias, out_bias = vectors[:4]
    second_gain, second_offset, up_bias, down_bias = vectors[4:]
    normalized, first_standardized, first_scale = layernorm_apply(stream, first_gain, first_offset)
    window_input = enter_grid(weave(normalized.astype(jnp.bfloat16)), shifted)
    window_input = weave(window_input)
    packed, context = attend(window_input, in_weight, in_bias, scores_bias)
    local_context = weave(leave_grid(weave(context), shifted))
    attended = (
        stream
        + jnp.dot(local_context, out_weight, preferred_element_type=jnp.float32)
        + out_bias
    )
    second_normalized, second_standardized, second_scale = layernorm_apply(
        attended, second_gain, second_offset
    )
    hidden = weave(second_normalized.astype(jnp.bfloat16))
    up_weight, down_weight = take_mlp()
    preactivation = jnp.dot(hidden, up_weight, preferred_element_type=jnp.float32) + up_bias
    activated = weave(gelu_value(preactivation).astype(jnp.bfloat16))
    result = (
        attended + jnp.dot(activated, down_weight, preferred_element_type=jnp.float32) + down_bias
    )
    kept = (
        first_standardized,
        first_scale,
        window_input,
        packed,
        local_context,
        second_standardized,
        second_scale,
        hidden,
        preactivation,
        activated,
    )
    return result, kept


def layer_backward(
    grad_flow, weights, vectors, scores_bias, onehot, shifted, kept, weave
):
    in_weight, out_weight, up_weight, down_weight = weights
    first_gain, second_gain = vectors[0], vectors[4]
    (
        first_standardized,
        first_scale,
        window_input,
        packed,
        local_context,
        second_standardized,
        second_scale,
        hidden,
        preactivation,
        activated,
    ) = kept
    grad_bf = grad_flow.astype(jnp.bfloat16)
    grad_down = outer(activated, grad_bf)
    grad_down_bias = token_total(grad_flow)
    grad_pre = back_product(grad_bf, down_weight) * gelu_slope(preactivation)
    grad_pre_bf = weave(grad_pre.astype(jnp.bfloat16))
    grad_up = outer(hidden, grad_pre_bf)
    grad_up_bias = token_total(grad_pre)
    attention_share, second_gain_gradient, second_offset_gradient = layernorm_reverse(
        back_product(grad_pre_bf, up_weight), second_standardized, second_scale, second_gain
    )
    attention_share = weave(attention_share)
    mlp_shards = weave.add(scatter_steps(owner_blocks((grad_up, grad_down))))
    grad_mixed = grad_flow + attention_share
    mixed_bf = grad_mixed.astype(jnp.bfloat16)
    grad_out = outer(local_context, mixed_bf)
    grad_out_bias = token_total(grad_mixed)
    grad_context = weave(back_product(mixed_bf, out_weight).astype(jnp.bfloat16))
    grad_packed, grad_in_bias, table_term = attend_back(
        packed, weave(enter_grid(grad_context, shifted)), scores_bias
    )
    grad_packed = weave(grad_packed)
    grad_in = outer(window_input, grad_packed)
    attn_shards = weave.add(scatter_steps(owner_blocks((grad_in, grad_out))))
    normalized_gradient = weave(leave_grid(weave(back_product(grad_packed, in_weight)), shifted))
    residual_share, first_gain_gradient, first_offset_gradient = layernorm_reverse(
        normalized_gradient, first_standardized, first_scale, first_gain
    )
    grad_table = lax.dot_general(
        onehot,
        table_term.reshape(HEADS, -1),
        (((0,), (1,)), ((), ())),
        precision=lax.Precision.HIGHEST,
    )
    vector_grads = (
        first_gain_gradient,
        first_offset_gradient,
        grad_in_bias.reshape(-1),
        grad_out_bias,
        second_gain_gradient,
        second_offset_gradient,
        grad_up_bias,
        grad_down_bias,
    )
    return grad_mixed + residual_share, mlp_shards, attn_shards, vector_grads, grad_table


class Chain:
    def __init__(self, steps):
        self.steps = steps
        self.state = next(steps)
        self.done = False

    def advance(self):
        following = next(self.steps, None)
        if following is None:
            self.done = True
        else:
            self.state = following

    def finish(self):
        while not self.done:
            self.advance()
        return self.state


class Weave:
    def __init__(self):
        self.chains = []

    def add(self, steps):
        chain = Chain(steps)
        self.chains.append(chain)
        return chain

    def __call__(self, value):
        live = [chain for chain in self.chains if not chain.done]
        for chain in live:
            chain.advance()
        if live:
            value, states = lax.optimization_barrier((value, [chain.state for chain in live]))
            for chain, state in zip(live, states):
                chain.state = state
        return value


def owner_blocks(grads):
    owners = lax.axis_size("dp")
    parts = []
    for grad in grads:
        grad = grad.astype(jnp.bfloat16)
        for low in range(0, grad.shape[1], C):
            parts.append(grad[:, low : low + C].reshape(owners, -1, C))
    return jnp.concatenate(parts, axis=1)


def merge(array, axis_name, bit):
    other = swapped(array, axis_name, bit)
    upper = ((lax.axis_index(axis_name) >> bit) & 1) == 1
    return jnp.where(upper, other, array), jnp.where(upper, array, other)


def double_owner(blocks, bit):
    owners, rows, _ = blocks.shape
    return jnp.stack(merge(blocks, "dp", bit), axis=1).reshape(2 * owners, rows, C)


def double_rows(blocks):
    return jnp.concatenate(merge(blocks, "rows", 0), axis=1)


def gather_steps(piece):
    bits = (lax.axis_size("dp") - 1).bit_length()
    quarters = piece.reshape(2, 2, -1, C)
    blocks = lax.dynamic_index_in_dim(quarters, lax.axis_index("rows"), 1, keepdims=False)
    blocks = blocks.reshape(1, -1, C)
    yield blocks
    for bit in range(bits - 1, 1, -1):
        blocks = double_owner(blocks, bit)
        yield blocks
    half = blocks.shape[1] // 2
    first, second = blocks[:, :half], blocks[:, half:]
    first, second = double_owner(first, 1), double_rows(second)
    yield first, second
    blocks = jnp.concatenate([double_rows(first), double_owner(second, 1)], axis=1)
    yield blocks
    yield double_owner(blocks, 0)


def piece_blocks(pieces):
    parts = []
    for piece in pieces:
        parts.extend(piece[:, low : low + C] for low in range(0, piece.shape[1], C))
    return jnp.concatenate(parts, axis=0)


def columns_of(blocks, count):
    depth = blocks.shape[1] // count
    parts = [
        blocks[:, step * depth : (step + 1) * depth].reshape(-1, C) for step in range(count)
    ]
    return jnp.concatenate(parts, axis=1)


def all_sum(values):
    for axis_name in ("dp", "rows"):
        for bit in range((lax.axis_size(axis_name) - 1).bit_length()):
            values = values + swapped(values, axis_name, bit)
    return values


def from_blocks(block, depth):
    return block.reshape(-1, depth, C).transpose(1, 0, 2).reshape(depth, -1)


def halve(array, axis_name, bit, dim):
    mine = (lax.axis_index(axis_name) >> bit) & 1
    keep = lax.dynamic_index_in_dim(array, mine, dim, keepdims=False)
    away = lax.dynamic_index_in_dim(array, 1 - mine, dim, keepdims=False)
    return add_bf(keep, swapped(away, axis_name, bit))


def add_bf(left, right):
    return (left.astype(jnp.float32) + right.astype(jnp.float32)).astype(jnp.bfloat16)


def halve_owner(blocks, bit):
    owners, rows, _ = blocks.shape
    return halve(blocks.reshape(owners // 2, 2, rows, C), "dp", bit, 1)


def halve_rows(blocks):
    owners, rows, _ = blocks.shape
    return halve(blocks.reshape(owners, 2, rows // 2, C), "rows", 0, 1)


def scatter_steps(blocks):
    bits = (lax.axis_size("dp") - 1).bit_length()
    yield blocks
    blocks = halve_owner(blocks, 0)
    yield blocks
    half = blocks.shape[1] // 2
    first, second = blocks[:, :half], blocks[:, half:]
    first, second = halve_owner(first, 1), halve_rows(second)
    yield first, second
    first, second = halve_rows(first), halve_owner(second, 1)
    both = jnp.concatenate([first, second], axis=1)
    yield both
    for bit in range(2, bits):
        both = halve_owner(both, bit)
        yield both
    low, high = merge(both[0].reshape(2, -1, C), "rows", 0)
    yield jnp.stack([low, high], axis=1).reshape(-1, C).astype(jnp.float32)


def per_device_general(
    images,
    cotangent,
    attn_in_weight,
    attn_out_weight,
    mlp_in_weight,
    mlp_out_weight,
    norm1_gain,
    norm1_bias,
    attn_in_bias,
    attn_out_bias,
    norm2_gain,
    norm2_bias,
    mlp_in_bias,
    mlp_out_bias,
    bias_table,
    region_labels,
    table_index,
):
    owners = lax.axis_size("dp")
    vector_shards = (
        norm1_gain,
        norm1_bias,
        attn_in_bias,
        attn_out_bias,
        norm2_gain,
        norm2_bias,
        mlp_in_bias,
        mlp_out_bias,
    )
    widths = [member.shape[1] for member in vector_shards]
    vector_piece = jnp.concatenate(vector_shards, axis=1).reshape(-1)
    vector_size = vector_piece.shape[0]
    vector_piece = jnp.pad(vector_piece, (0, -vector_size % (32 * C))).reshape(-1, C)
    depth = attn_in_weight.shape[1]
    up_blocks = mlp_in_weight.shape[2] // C

    def attn_piece(layer_no):
        return piece_blocks([attn_in_weight[layer_no], attn_out_weight[layer_no]])

    def mlp_piece(layer_no):
        return piece_blocks([mlp_in_weight[layer_no], mlp_out_weight[layer_no]])

    def attn_split(blocks):
        blocks = blocks[:, : 4 * depth]
        return columns_of(blocks[:, : 3 * depth], 3), blocks[:, 3 * depth :].reshape(-1, C)

    def mlp_split(blocks):
        up, down = blocks[:, : up_blocks * depth], blocks[:, up_blocks * depth :]
        return columns_of(up, up_blocks), down.reshape(-1, C)

    lead = Chain(gather_steps(jnp.concatenate([attn_piece(0), vector_piece], axis=0)))
    lead.advance()
    lead.advance()
    lead.state, first_mlp = lax.optimization_barrier((lead.state, mlp_piece(0)))
    weave = Weave()
    mlp_chains = [weave.add(gather_steps(first_mlp))]
    lead.advance()
    lead.state = weave(lead.state)
    lead.advance()
    lead.state = weave(lead.state)
    lead_blocks = lead.finish()
    vector_all = lead_blocks[:, 4 * depth :].reshape(owners, -1)[:, :vector_size]
    vector_all = vector_all.reshape(owners, LAYERS, -1).astype(jnp.float32)

    def layer_vectors(layer_no):
        start, result = 0, []
        for width in widths:
            result.append(vector_all[:, layer_no, start : start + width].reshape(-1))
            start += width
        return tuple(result)

    def pad_window(values, fill):
        grid = values.reshape(values.shape[:-1] + (WIN, WIN))
        pads = [(0, 0)] * (values.ndim - 1) + [(0, SIDE - WIN)] * 2
        return jnp.pad(grid, pads, constant_values=fill).reshape(values.shape[:-1] + (PAD,))

    def pad_pair(values, fill):
        both = pad_window(jnp.swapaxes(pad_window(values, fill), -1, -2), fill)
        return jnp.swapaxes(both, -1, -2)

    half_index = lax.axis_index("rows")
    local_labels = lax.dynamic_slice_in_dim(region_labels, half_index * WIN, WIN, 0)
    label_tiles = (
        local_labels.reshape(WIN, GRID // WIN, WIN).transpose(1, 0, 2).reshape(GRID // WIN, -1)
    )
    same = label_tiles[:, :, None] == label_tiles[:, None, :]
    real_key = pad_window(jnp.ones((WIN * WIN,), jnp.int32), 0) == 1
    allowed_pair = (
        jnp.broadcast_to(real_key[None, None, :], (1, PAD, PAD)),
        (pad_pair(same.astype(jnp.int32), 1) == 1) & real_key[None, None, :],
    )
    index_pad = pad_pair(table_index, 0)
    onehot = (index_pad.reshape(-1)[:, None] == jnp.arange(REL, dtype=jnp.int32)[None, :]).astype(
        jnp.float32
    )

    def scores_bias_of(layer_no):
        picked = lax.dot_general(
            bias_table[layer_no],
            onehot,
            (((0,), (1,)), ((), ())),
            precision=lax.Precision.HIGHEST,
            preferred_element_type=jnp.float32,
        ).reshape(HEADS, PAD, PAD)
        allowed = allowed_pair[layer_no % 2]
        masked = jnp.where(allowed[:, None], picked[None], NEG)
        return masked.reshape(-1, GROUPS, GROUP * PAD, PAD)

    stream = to_padded(images).astype(jnp.float32)
    vectors = [layer_vectors(layer_no) for layer_no in range(LAYERS)]
    score_biases = [scores_bias_of(layer_no) for layer_no in range(LAYERS)]
    kept_all = []
    attn_chains = [lead]
    weights = []
    for layer_no in range(LAYERS):
        if layer_no + 1 < LAYERS:
            attn_chains.append(weave.add(gather_steps(attn_piece(layer_no + 1))))
        attn_weights = attn_split(attn_chains[layer_no].finish())
        taken = []

        def take_mlp():
            taken.extend(mlp_split(mlp_chains[layer_no].finish()))
            if layer_no + 1 < LAYERS:
                mlp_chains.append(weave.add(gather_steps(mlp_piece(layer_no + 1))))
            return taken

        stream, kept = layer_forward(
            stream,
            attn_weights,
            take_mlp,
            vectors[layer_no],
            score_biases[layer_no],
            layer_no % 2 == 1,
            weave,
        )
        weights.append((*attn_weights, *taken))
        kept_all.append(kept)
    final_out = from_padded(stream.astype(jnp.bfloat16))
    grad_flow = to_padded(cotangent).astype(jnp.float32)
    mlp_all, attn_all, vectors_all, tables_all = ([None] * LAYERS for _ in range(4))
    for layer_no in reversed(range(LAYERS)):
        grad_flow, mlp_all[layer_no], attn_all[layer_no], grads, tables_all[layer_no] = (
            layer_backward(
                grad_flow,
                weights[layer_no],
                vectors[layer_no],
                score_biases[layer_no],
                onehot,
                layer_no % 2 == 1,
                kept_all[layer_no],
                weave,
            )
        )
        vectors_all[layer_no] = jnp.concatenate(grads)
    lengths = [width * owners for width in widths]
    small = jnp.concatenate(vectors_all + [jnp.stack(tables_all).reshape(-1)])
    total = small.shape[0]
    small = jnp.pad(small, (0, -total % (8 * LANES))).reshape(-1, LANES)
    small = all_sum(small).reshape(-1)[:total]
    mlp_all = [chain.finish() for chain in mlp_all]
    attn_all = [chain.finish() for chain in attn_all]
    vector_total = small[: LAYERS * sum(lengths)].reshape(LAYERS, -1)
    table_total = small[LAYERS * sum(lengths) :].reshape(bias_table.shape)
    vector_outs, start = [], 0
    owner = lax.axis_index("dp")
    for width, length in zip(widths, lengths):
        part = vector_total[:, start : start + length]
        vector_outs.append(lax.dynamic_slice_in_dim(part, owner * width, width, 1))
        start += length
    def stacked(blocks, low, high, rows):
        return jnp.stack([from_blocks(block[low * depth : high * depth], rows) for block in blocks])

    down_depth = mlp_out_weight.shape[1]
    grad_up = stacked(mlp_all, 0, up_blocks, depth)
    grad_down = jnp.stack([block[up_blocks * depth :].reshape(down_depth, C) for block in mlp_all])
    grad_in = stacked(attn_all, 0, 3, depth)
    grad_out = stacked(attn_all, 3, 4, depth)
    return (
        final_out,
        from_padded(grad_flow),
        grad_in,
        grad_out,
        grad_up,
        grad_down,
        *vector_outs,
        table_total,
    )


HALF_SEND = PAD // 2
KEYS = WIN * SIDE
WIDE = GROUP * PAD
VEC_ROWS = 32
SUM_ROWS = 24
TABLE_ROW = 16
TABLE_COLS = 256
MESH = pl.DeviceIdType.MESH
VMEM_BYTES = 63 * 2**20
F32 = jnp.float32
BF16 = jnp.bfloat16


class Links:
    def __init__(self, depth_z, send_sems, recv_sems):
        owner = lax.axis_index("dp")
        self.zs = depth_z
        self.r = lax.axis_index("rows")
        self.z = owner // 4
        self.x = lax.rem(owner // 2, 2)
        self.c = lax.rem(owner, 2)
        self.send_sems = send_sems
        self.recv_sems = recv_sems
        self.used = 0

    def place(self, kind, step=0):
        z, x, c, r = self.z, self.x, self.c, self.r
        if kind == "z":
            z = lax.rem(z + step, self.zs)
        elif kind == "x":
            x = 1 - x
        elif kind == "c":
            c = 1 - c
        else:
            r = 1 - r
        return (r, z * 4 + x * 2 + c)

    def greet(self):
        barrier = pltpu.get_barrier_semaphore()
        partners = [self.place("z", step) for step in range(1, self.zs)]
        partners += [self.place(kind) for kind in ("x", "c", "y")]
        for partner in partners:
            pl.semaphore_signal(barrier, inc=1, device_id=partner, device_id_type=MESH)
        pl.semaphore_wait(barrier, len(partners))

    def send(self, src, dst, kind, step=0):
        spot = self.used
        self.used += 1
        copy = pltpu.make_async_remote_copy(
            src_ref=src,
            dst_ref=dst,
            send_sem=self.send_sems.at[spot],
            recv_sem=self.recv_sems.at[spot],
            device_id=self.place(kind, step),
            device_id_type=MESH,
        )
        copy.start()
        return copy


class Gather:
    def __init__(self, links, parts):
        self.links = links
        self.parts = parts
        self.flying = []
        self.sent = []

    def wait(self):
        for copy in self.flying:
            copy.wait_recv()
        self.sent += self.flying
        self.flying = []

    def go(self, kind, pick, step=0):
        for ref, cols, route in self.parts:
            spot = pick(route)
            if spot is not None:
                view = ref.at[spot + (slice(None), cols)]
                self.flying.append(self.links.send(view, view, kind, step))

    def start(self):
        k = self.links
        for step in range(1, k.zs):
            self.go("z", lambda route: (k.z, k.x, k.c, k.r), step)

    def first(self):
        k = self.links
        self.wait()
        every = slice(None)
        self.go("x", lambda route: (every, k.x, k.c, k.r) if route == 0 else None)
        self.go("y", lambda route: (every, k.x, k.c, k.r) if route == 1 else None)

    def second(self):
        k = self.links
        self.wait()
        every = slice(None)
        self.go("y", lambda route: (every, every, k.c, k.r) if route == 0 else None)
        self.go("x", lambda route: (every, k.x, k.c, every) if route == 1 else None)

    def cores(self):
        k = self.links
        self.wait()
        every = slice(None)
        self.go("c", lambda route: (every, every, k.c, every))

    def finish(self):
        self.wait()

    def drain(self):
        for copy in self.sent:
            copy.wait_send()


def add_rows(left, right):
    return (left.astype(F32) + right.astype(F32)).astype(BF16)


class ScatterPart:
    def __init__(self, grad, low, high, route, buffers, out, layer_no):
        self.grad, self.low, self.high, self.route = grad, low, high, route
        self.core_in, self.first_in, self.second_in, self.z_in, self.mine, self.other = buffers
        self.out, self.layer_no = out, layer_no


class Scatter:
    def __init__(self, links, parts):
        self.links = links
        self.parts = parts
        self.flying = []
        self.sent = []

    def wait(self):
        for copy in self.flying:
            copy.wait_recv()
        self.sent += self.flying
        self.flying = []

    def go(self, part, spot, into, kind, step=0):
        view = part.grad.at[spot + (slice(None), pl.ds(part.low, part.high - part.low))]
        self.flying.append(self.links.send(view, into, kind, step))

    def start(self):
        k = self.links
        every = slice(None)
        for part in self.parts:
            self.go(part, (every, every, 1 - k.c, every), part.core_in, "c")

    def first(self):
        k = self.links
        every = slice(None)
        self.wait()

        def one(zi, carry):
            for part in self.parts:
                spot = (zi, every, k.c, every, every, slice(part.low, part.high))
                part.grad[spot] = add_rows(part.grad[spot], part.core_in[zi])
            return carry

        lax.fori_loop(0, k.zs, one, 0)
        for part in self.parts:
            if part.route == 0:
                self.go(part, (every, 1 - k.x, k.c, every), part.first_in, "x")
            else:
                self.go(part, (every, every, k.c, 1 - k.r), part.first_in, "y")

    def second(self):
        k = self.links
        every = slice(None)
        self.wait()

        def one(zi, carry):
            for part in self.parts:
                cols = slice(part.low, part.high)
                if part.route == 0:
                    spot = (zi, k.x, k.c, every, every, cols)
                else:
                    spot = (zi, every, k.c, k.r, every, cols)
                part.grad[spot] = add_rows(part.grad[spot], part.first_in[zi])
            return carry

        lax.fori_loop(0, k.zs, one, 0)
        for part in self.parts:
            if part.route == 0:
                self.go(part, (every, k.x, k.c, 1 - k.r), part.second_in, "y")
            else:
                self.go(part, (every, 1 - k.x, k.c, k.r), part.second_in, "x")

    def third(self):
        k = self.links
        every = slice(None)
        self.wait()

        def one(zi, carry):
            for part in self.parts:
                spot = (zi, k.x, k.c, k.r, every, slice(part.low, part.high))
                part.grad[spot] = add_rows(part.grad[spot], part.second_in[zi])
            return carry

        lax.fori_loop(0, k.zs, one, 0)
        for part in self.parts:
            for step in range(1, k.zs):
                far = lax.rem(k.z + step, k.zs)
                self.go(part, (far, k.x, k.c, k.r), part.z_in.at[step - 1], "z", step)

    def fourth(self):
        k = self.links
        self.wait()
        for part in self.parts:
            spot = (k.z, k.x, k.c, k.r, slice(None), slice(part.low, part.high))
            total = part.grad[spot].astype(F32)
            for step in range(1, k.zs):
                total = total + part.z_in[step - 1].astype(F32)
            part.mine[...] = total.astype(BF16)
            self.flying.append(k.send(part.mine, part.other, "y"))

    def drain(self):
        for copy in self.sent:
            copy.wait_send()

    def finish(self):
        k = self.links
        self.wait()
        for part in self.parts:
            cols = slice(part.low, part.high)
            part.out[part.layer_no, k.r, :, cols] = part.mine[...].astype(F32)
            part.out[part.layer_no, 1 - k.r, :, cols] = part.other[...].astype(F32)


class Total:
    def __init__(self, links, layer_no, sums, buffers):
        self.links = links
        self.place = layer_no
        self.buffers = [buffer.at[layer_no] for buffer in [sums] + buffers]
        self.sent = []

    def start(self):
        own, core_in = self.buffers[:2]
        self.sent.append(self.links.send(own, core_in, "c"))

    def second(self):
        own, core_in, one, x_in = self.buffers[:4]
        self.sent[-1].wait_recv()
        one[...] = own[...] + core_in[...]
        self.sent.append(self.links.send(one, x_in, "x"))

    def third(self):
        one, x_in, two, y_in = self.buffers[2:6]
        self.sent[-1].wait_recv()
        two[...] = one[...] + x_in[...]
        self.sent.append(self.links.send(two, y_in, "y"))

    def fourth(self):
        k = self.links
        two, y_in, three, z_in = self.buffers[4:]
        self.sent[-1].wait_recv()
        three[...] = two[...] + y_in[...]
        z_in[k.z] = three[...]
        self.last = [k.send(three, z_in.at[k.z], "z", far) for far in range(1, k.zs)]
        self.sent += self.last

    def finish(self, out):
        z_in = self.buffers[-1]
        for step in self.last:
            step.wait_recv()
        total = z_in[0]
        for zi in range(1, self.links.zs):
            total = total + z_in[zi]
        out[self.place] = total

    def drain(self):
        for copy in self.sent:
            copy.wait_send()


def pad_keys(values):
    return jnp.concatenate([values, jnp.zeros((PAD - KEYS, values.shape[1]), values.dtype)], axis=0)


def attend_windows(packed, bias_of, probs, context, first, last):
    lanes = head_lanes(BF16)
    lanes_f32 = head_lanes(F32)

    def window(w, carry):
        for group in range(GROUPS):
            low = group * LANES
            wide_query = spread(packed[w, :, low : low + LANES], lanes)
            keys = packed[w, :, C + low : C + low + LANES]
            values = packed[w, :, 2 * C + low : 2 * C + low + LANES]
            scores = dot_nt(keys, wide_query)[:KEYS] + bias_of(w, group)
            weights = jnp.exp(scores - jnp.max(scores, axis=0, keepdims=True))
            part = weights * (1.0 / jnp.sum(weights, axis=0, keepdims=True))
            probs[w * GROUPS + group] = part
            wide = dot_tn(pad_keys(part).astype(BF16), values)
            context[w, :, low : low + LANES] = gather_heads(wide, lanes_f32).astype(BF16)
        return carry

    lax.fori_loop(first, last, window, 0)


def attend_windows_back(packed, probs, grad_context, grad_packed, table, sums, first, last):
    lanes = head_lanes(BF16)
    lanes_f32 = head_lanes(F32)
    scale = HEAD_DIM ** (-0.5)
    if first == 0:
        sums[2:4, :] = jnp.zeros((2, C), F32)
        table[...] = jnp.zeros(table.shape, F32)

    def window(w, carry):
        for group in range(GROUPS):
            low = group * LANES
            wide_query = spread(packed[w, :, low : low + LANES], lanes)
            keys = packed[w, :, C + low : C + low + LANES]
            values = packed[w, :, 2 * C + low : 2 * C + low + LANES]
            wide_grad = spread(grad_context[w, :, low : low + LANES], lanes)
            part = probs[w * GROUPS + group]
            grad_probs = dot_nt(values, wide_grad)[:KEYS]
            product_sum = jnp.sum(part * grad_probs, axis=0, keepdims=True)
            grad_scores = part * (grad_probs - product_sum)
            table[2 * group] += grad_scores[:, :LANES]
            table[2 * group + 1] += grad_scores[:, LANES:]
            part_bf = pad_keys(part).astype(BF16)
            scores_bf = pad_keys(grad_scores).astype(BF16)
            grad_values = jnp.dot(part_bf, wide_grad, preferred_element_type=F32)
            grad_keys = jnp.dot(scores_bf, wide_query, preferred_element_type=F32)
            grad_query = gather_heads(dot_tn(scores_bf, keys), lanes_f32) * scale
            grad_packed[w, :, low : low + LANES] = grad_query.astype(BF16)
            grad_packed[w, :, C + low : C + low + LANES] = grad_keys.astype(BF16)
            grad_packed[w, :, 2 * C + low : 2 * C + low + LANES] = grad_values.astype(BF16)
            sums[2:3, low : low + LANES] += jnp.sum(grad_query, axis=0, keepdims=True)
            sums[3:4, low : low + LANES] += jnp.sum(
                grad_values, axis=0, keepdims=True
            )
        return carry

    lax.fori_loop(first, last, window, 0)


def table_sums(tables, index, sums):
    entry = lax.broadcasted_iota(jnp.int32, (TABLE_COLS, LANES), 0)
    lane = lax.broadcasted_iota(jnp.int32, (8, LANES), 1)
    first = (lane < PAD).astype(F32)

    def eight(block, total):
        low = pl.multiple_of(block * 8, 8)
        tiles = [table[:, pl.ds(low, 8), :] for table in tables]
        spots = index[pl.ds(low, 8), :]
        spots = jnp.concatenate([spots, spots], axis=1)
        for j in range(8):
            rows = []
            for tile in tiles:
                one = tile[:, j, :]
                rows += [one * first, one * (1.0 - first)]
            rows = jnp.concatenate(rows, axis=0)
            high = rows.astype(BF16)
            rest = (rows - high.astype(F32)).astype(BF16)
            onehot = (entry == spots[j : j + 1, :]).astype(F32).astype(BF16)
            total = total + dot_nt(jnp.concatenate([high, rest], axis=0), onehot)
        return total

    count = len(tables) * 16
    total = lax.fori_loop(0, KEYS // 8, eight, jnp.zeros((2 * count, TABLE_COLS), F32))
    total = total[:count] + total[count:]
    sums[TABLE_ROW : TABLE_ROW + 8, :TABLE_COLS] = total[:8]
    sums[TABLE_ROW : TABLE_ROW + 8, TABLE_COLS:] = total[8:]


def place_vectors(refs, first_rows, owner, owners, rows):
    rows[...] = jnp.zeros(rows.shape, F32)
    for ref, first in zip(refs, first_rows):
        width = ref.shape[1]
        spot = owner * width
        column = lax.broadcasted_iota(jnp.int32, (width, C), 1)
        place = lax.broadcasted_iota(jnp.int32, (width, C), 0) + lax.rem(spot, C)
        line = jnp.dot(ref[...].astype(F32), (column == place).astype(F32))
        for row in range(owners * width // C):
            here = (spot // C == row).astype(F32)
            for layer_no in range(LAYERS):
                to = layer_no * 12 + first + row
                rows[to : to + 1, :] = line[layer_no : layer_no + 1] * here


def take_vectors(totals, first_rows, owner, owners, outs):
    for out, first in zip(outs, first_rows):
        width = out.shape[1]
        spot = owner * width
        for layer_no in range(LAYERS):
            line = totals[layer_no, pl.ds(first + spot // C, 1), :]
            line = jnp.broadcast_to(line, (8, C))
            line = pltpu.roll(line, lax.rem(C - lax.rem(spot, C), C), 1)
            out[layer_no : layer_no + 1, :] = line[:1, :width]


def make_bias(entries, index, bias):
    entry = lax.broadcasted_iota(jnp.int32, (TABLE_COLS, LANES), 0)
    first = lax.broadcasted_iota(jnp.int32, (entries.shape[0] // 2, LANES), 1) < PAD
    whole_entries = entries[...]
    high = whole_entries.astype(BF16)
    rest = whole_entries - high.astype(F32)
    middle = rest.astype(BF16)
    low_term = (rest - middle.astype(F32)).astype(BF16)
    terms = jnp.concatenate([high, middle, low_term], axis=0)
    count = entries.shape[0]

    def eight(block, carry):
        low = pl.multiple_of(block * 8, 8)
        spots = index[pl.ds(low, 8), :]
        spots = jnp.concatenate([spots, spots], axis=1)
        for j in range(8):
            onehot = (entry == spots[j : j + 1, :]).astype(F32).astype(BF16)
            value = jnp.dot(terms, onehot, preferred_element_type=F32)
            value = value[:count] + value[count : 2 * count] + value[2 * count :]
            line = jnp.where(first, value[: count // 2], value[count // 2 :])
            bias[:, pl.ds(low + j, 1), :] = line[:, None, :]
        return carry

    lax.fori_loop(0, KEYS // 8, eight, 0)


def make_masks(labels, half, masks):
    key = lax.broadcasted_iota(jnp.int32, (KEYS, LANES), 0)
    masks[0] = jnp.where(lax.rem(key, SIDE) < WIN, 0.0, NEG)
    rows = labels[...].astype(F32)
    rows = jnp.concatenate([rows, rows], axis=1)
    columns = rows.T
    for w in range(2):
        row = jnp.where(half == 0, rows[w : w + 1], rows[2 + w : 3 + w])
        column = jnp.where(half == 0, columns[:KEYS, w : w + 1], columns[:KEYS, 2 + w : 3 + w])
        masks[1 + w] = jnp.where(column == row, 0.0, NEG)


def token_rows(ref):
    value = ref[...]
    return value.reshape(-1, value.shape[-1])


def whole(ref, low, high):
    value = ref[:, :, :, :, :, low:high]
    return value.reshape(-1, high - low)


def training_kernel(depth_z, *refs):
    refs = iter(refs)

    def take(count):
        return [next(refs) for _ in range(count)]

    x_ref, cot_ref = take(2)
    shards = take(4)
    vec_refs = take(8)
    entries_ref, index_ref, label_ref, perm_ref = take(4)
    final_ref, input_grad_ref = take(2)
    grad_outs = take(4)
    vec_outs = take(8)
    table_out = next(refs)
    weights = [take(4) for _ in range(LAYERS)]
    top_grads = take(4)
    xhat1, xhat2, scale1, scale2, inputs, packed, probs, context, hidden, slope, active = (
        take(2) for _ in range(11)
    )
    stream, grad_flow, grad_rows, rows_bf, more_bf, halo = take(6)
    grad_packed, grad_bf, tables = take(3)
    scatter_buffers = [[take(6) for _ in range(8)] for _ in range(LAYERS)]
    vecs, vec_ref, vec_core, vec_one, vec_x, vec_two, vec_z = take(7)
    bias, masks, totals = take(3)
    sums, *sum_buffers = take(8)
    send_sems, recv_sems = take(2)

    images = x_ref.shape[0]
    windows = images * 2
    tokens = windows * PAD
    ff = shards[2].shape[-1]
    links = Links(depth_z, send_sems, recv_sems)
    every = slice(None)
    mine = (links.z, links.x, links.c, links.r)

    owner = lax.axis_index("dp")
    owners = depth_z * 4
    first_rows = (0, 1, 2, 4, 5, 6, 7, 11)
    place_vectors(vec_refs, first_rows, owner, owners, vecs)
    vec_ref[...] = vecs[...].astype(BF16)
    links.greet()
    vec_sent = [
        links.send(vec_ref, vec_z.at[links.z], "z", far) for far in range(1, depth_z)
    ]
    vec_z[links.z] = vec_ref[...]
    in_parts = [(0, 0, 3 * C // 2, 0, 1), (0, 3 * C // 2, 3 * C, 1, 0)]
    up_parts = [(2, 0, ff // 2, 0, 1), (2, ff // 2, ff, 1, 0)]
    up_parts += [(1, 0, C // 2, 0, 1), (1, C // 2, C, 1, 0)]
    down_parts = [(3, 0, C // 2, 0, 1), (3, C // 2, C, 1, 0)]
    part_sets = (in_parts, up_parts, down_parts)

    def place_own(layer_no, which):
        weights[layer_no][which][mine + (every, every)] = shards[which][layer_no, links.r]

    def gather_of(layer_no, parts):
        return Gather(
            links,
            [
                (weights[layer_no][which], pl.ds(low, high - low), route)
                for which, low, high, route, _ in parts
            ],
        )

    gathers = [[gather_of(layer_no, parts) for parts in part_sets] for layer_no in range(LAYERS)]
    queue = [item for items in gathers for item in items]

    def pass_on(item):
        item.wait()
        spot = queue.index(item) + 1
        if spot < len(queue):
            queue[spot].start()
        item.first()

    place_own(0, 0)
    queue[0].start()
    for which in (1, 2, 3):
        place_own(0, which)
    for which in range(4):
        place_own(1, which)

    def spread_rows(source, target):
        def one(image, carry):
            for row in range(SIDE):
                for side in range(2):
                    if row < WIN:
                        line = source[image, row].astype(F32)[side * WIN : (side + 1) * WIN]
                        line = jnp.concatenate([line, jnp.zeros((1, C), F32)], axis=0)
                    else:
                        line = jnp.zeros((SIDE, C), F32)
                    target[2 * image + side, row * SIDE : (row + 1) * SIDE, :] = line
            return carry

        lax.fori_loop(0, images, one, 0)

    def join_rows(source, target):
        def one(image, carry):
            for row in range(WIN):
                low = row * SIDE
                sides = [source[2 * image + side, low : low + WIN, :] for side in range(2)]
                target[image, row] = jnp.concatenate(sides, axis=0).astype(target.dtype)
            return carry

        lax.fori_loop(0, images, one, 0)

    spread_rows(x_ref, stream)
    for step in vec_sent:
        step.wait_recv()
    total = vec_z[0].astype(F32)
    for zi in range(1, depth_z):
        total = total + vec_z[zi].astype(F32)
    vec_one[...] = total.astype(BF16)
    vec_sent.append(links.send(vec_one, vec_x, "x"))
    pass_on(gathers[0][0])
    make_bias(entries_ref, index_ref, bias)
    make_masks(label_ref, links.r, masks)
    vec_sent[-1].wait_recv()
    vec_two[...] = vec_one[...] + vec_x[...]
    vec_sent.append(links.send(vec_two, vec_core, "c"))
    gathers[0][0].second()
    vec_sent[-1].wait_recv()
    vecs[...] = (vec_two[...] + vec_core[...]).astype(F32)

    def vec(layer_no, row):
        spot = layer_no * 12 + row
        return vecs[spot : spot + 1, :]

    def normalize(source, gain, offset, xhat, scale, target):
        def one(w, carry):
            values = source[w]
            average = jnp.mean(values, axis=-1, keepdims=True)
            centered = values - average
            variance = jnp.mean(centered * centered, axis=-1, keepdims=True)
            inverse = lax.rsqrt(variance + EPS)
            standard = centered * inverse
            xhat[w] = standard
            scale[w] = inverse
            target[w] = (standard * gain + offset).astype(BF16)
            return carry

        lax.fori_loop(0, windows, one, 0)

    def normalize_back(source, gain, xhat, scale, layer_no, row_gain):
        def one(w, carry):
            by_gain, by_offset, flow_sum = carry
            values = source[w]
            standard = xhat[w]
            scaled = values * gain
            first = jnp.mean(scaled, axis=-1, keepdims=True)
            second = jnp.mean(scaled * standard, axis=-1, keepdims=True)
            flow = grad_flow[w] + scale[w] * (scaled - first - standard * second)
            grad_flow[w] = flow
            rows_bf[w] = flow.astype(BF16)
            return (
                by_gain + jnp.sum(values * standard, axis=0, keepdims=True),
                by_offset + jnp.sum(values, axis=0, keepdims=True),
                flow_sum + jnp.sum(flow, axis=0, keepdims=True),
            )

        zero = jnp.zeros((1, C), F32)
        by_gain, by_offset, flow_sum = lax.fori_loop(0, windows, one, (zero, zero, zero))
        sums[layer_no, row_gain : row_gain + 1, :] = by_gain
        sums[layer_no, row_gain + 1 : row_gain + 2, :] = by_offset
        return flow_sum

    def enter_start(source, slot):
        return links.send(source.at[:, pl.ds(0, HALF_SEND), :], halo.at[slot], "y")

    def leave_start(source, slot, first, last):
        some = pl.ds(first, last - first)
        rows = pl.ds(HALF_SEND, HALF_SEND)
        return links.send(source.at[some, rows, :], halo.at[slot, some], "y")

    def moved(source, slot, kind, image):
        own = source[2 * image : 2 * image + 2].reshape(2 * PAD, C)
        away = halo[slot, 2 * image : 2 * image + 2].reshape(PAD, C)
        return jnp.dot(perm_ref[2 * kind], own, preferred_element_type=F32) + jnp.dot(
            perm_ref[2 * kind + 1][:, :PAD], away, preferred_element_type=F32
        )

    def move(source, slot, kind, target):
        for image in range(images):
            target[2 * image : 2 * image + 2] = (
                moved(source, slot, kind, image).astype(BF16).reshape(2, PAD, C)
            )

    def project(layer_no):
        rows = token_rows(inputs[layer_no])
        weight = weights[layer_no][0]
        query = jnp.dot(rows, whole(weight, 0, C), preferred_element_type=F32) + vec(layer_no, 2)
        query = query * HEAD_DIM ** (-0.5)
        packed[layer_no][:, :, :C] = query.astype(BF16).reshape(windows, PAD, C)
        keys = jnp.dot(rows, whole(weight, C, 2 * C), preferred_element_type=F32)
        packed[layer_no][:, :, C : 2 * C] = keys.astype(BF16).reshape(windows, PAD, C)
        values = jnp.dot(rows, whole(weight, 2 * C, 3 * C), preferred_element_type=F32)
        values = values + vec(layer_no, 3)
        packed[layer_no][:, :, 2 * C :] = values.astype(BF16).reshape(windows, PAD, C)

    def mix(layer_no):
        rows = token_rows(context[layer_no])
        out = jnp.dot(rows, whole(weights[layer_no][1], 0, C), preferred_element_type=F32)
        stream[...] = stream[...] + (out + vec(layer_no, 4)).reshape(windows, PAD, C)

    def up_columns(layer_no, j):
        cols = pl.ds(pl.multiple_of(j * C, C), C)
        return weights[layer_no][2][:, :, :, :, :, cols].reshape(C, C), cols

    def feed_up(layer_no, first, last):
        rows = token_rows(hidden[layer_no])
        base = layer_no * 12

        def one(j, carry):
            up, cols = up_columns(layer_no, j)
            pre = jnp.dot(rows, up, preferred_element_type=F32) + vecs[pl.ds(base + 7 + j, 1), :]
            half = 0.5 * (1.0 + lax.erf(pre * SQRT_HALF))
            value = (pre * half).astype(BF16)
            steep = half + pre * jnp.exp(-0.5 * pre * pre) * INV_ROOT_TAU
            active[layer_no][:, :, cols] = value.reshape(windows, PAD, C)
            slope[layer_no][:, :, cols] = steep.astype(BF16).reshape(windows, PAD, C)
            return carry

        lax.fori_loop(first, last, one, 0)

    def feed_down(layer_no):
        stream[...] = stream[...] + vec(layer_no, 11).reshape(1, 1, C)

        def one(j, carry):
            cols = pl.ds(pl.multiple_of(j * C, C), C)
            value = active[layer_no][:, :, cols].reshape(tokens, C)
            down = weights[layer_no][3][j].reshape(C, C)
            out = jnp.dot(value, down, preferred_element_type=F32)
            stream[...] = stream[...] + out.reshape(windows, PAD, C)
            return carry

        lax.fori_loop(0, depth_z, one, 0)

    halo_sent = []
    half = windows // 2
    half_z = depth_z // 2
    in0, up0, down0 = gathers[0]
    in1, up1, down1 = gathers[1]

    def bias_of(layer_no, kind_of):
        def one(w, group):
            mask = masks[kind_of(w)]
            tile = layer_no * 2 * GROUPS + 2 * group
            return jnp.concatenate([bias[tile] + mask, bias[tile + 1] + mask], axis=1)

        return one

    def attend_plain(first, last):
        attend_windows(
            packed[0], bias_of(0, lambda w: 0), probs[0], context[0], first, last
        )

    def attend_shifted(first, last):
        attend_windows(
            packed[1],
            bias_of(1, lambda w: 1 + lax.rem(w, 2)),
            probs[1],
            more_bf,
            first,
            last,
        )

    normalize(stream, vec(0, 0), vec(0, 1), xhat1[0], scale1[0], inputs[0])
    pass_on(up0)
    in0.cores()
    in0.finish()
    project(0)
    up0.second()
    pass_on(down0)
    attend_plain(0, half)
    pass_on(in1)
    down0.second()
    up0.cores()
    attend_plain(half, windows)
    up0.finish()
    mix(0)
    normalize(stream, vec(0, 5), vec(0, 6), xhat2[0], scale2[0], hidden[0])
    down0.cores()
    in1.second()
    pass_on(up1)
    feed_up(0, 0, depth_z)
    down0.finish()
    feed_down(0)
    normalize(stream, vec(1, 0), vec(1, 1), xhat1[1], scale1[1], rows_bf)
    halo_sent.append(enter_start(rows_bf, 0))
    pass_on(down1)
    up1.second()
    in1.cores()
    halo_sent[-1].wait_recv()
    move(rows_bf, 0, 0, inputs[1])
    halo_sent[-1].wait_send()
    in1.finish()
    project(1)
    attend_shifted(0, half)
    halo_sent.append(leave_start(more_bf, 1, 0, half))
    down1.second()
    up1.cores()
    attend_shifted(half, windows)
    halo_sent.append(leave_start(more_bf, 1, half, windows))
    down1.cores()
    up1.finish()
    for step in halo_sent[-2:]:
        step.wait_recv()
    move(more_bf, 1, 1, context[1])
    for step in halo_sent[-2:]:
        step.wait_send()
    mix(1)
    normalize(stream, vec(1, 5), vec(1, 6), xhat2[1], scale2[1], hidden[1])
    feed_up(1, 0, depth_z)
    down1.finish()
    feed_down(1)

    join_rows(stream, final_ref)
    spread_rows(cot_ref, grad_flow)

    def turn(w, carry):
        rows_bf[w] = grad_flow[w].astype(BF16)
        return carry + jnp.sum(grad_flow[w], axis=0, keepdims=True)

    flow_sum = lax.fori_loop(0, windows, turn, jnp.zeros((1, C), F32))

    grads = [weights[1], top_grads]

    def scatter_of(layer_no, parts, first_buffer):
        return Scatter(
            links,
            [
                ScatterPart(
                    grads[layer_no][which],
                    low,
                    high,
                    route,
                    scatter_buffers[layer_no][first_buffer + number],
                    grad_outs[which],
                    layer_no,
                )
                for number, (which, low, high, _, route) in enumerate(parts)
            ],
        )

    scatters = [
        [scatter_of(layer_no, parts, first) for parts, first in zip(part_sets, (0, 2, 6))]
        for layer_no in range(LAYERS)
    ]

    def down_grads(layer_no):
        grad_down = grads[layer_no][3]

        def one(j, carry):
            cols = pl.ds(pl.multiple_of(j * C, C), C)
            value = active[layer_no][:, :, cols].reshape(tokens, C)
            part = dot_tn(value, token_rows(rows_bf)).astype(BF16)
            grad_down[j] = part.reshape(grad_down.shape[1:])
            return carry

        lax.fori_loop(0, depth_z, one, 0)

    def feed_back(layer_no, first, last):
        grad_up = grads[layer_no][2]
        if first == 0:
            grad_rows[...] = jnp.zeros(grad_rows.shape, F32)

        def one(j, carry):
            flow = token_rows(rows_bf)
            up, cols = up_columns(layer_no, j)
            down = weights[layer_no][3][j].reshape(C, C)
            steep = slope[layer_no][:, :, cols].reshape(tokens, C).astype(F32)
            grad_pre = dot_nt(flow, down) * steep
            sums[layer_no, pl.ds(7 + j, 1), :] = jnp.sum(grad_pre, axis=0, keepdims=True)
            grad_bf[...] = grad_pre.astype(BF16)
            up_part = dot_tn(token_rows(hidden[layer_no]), grad_bf[...]).astype(BF16)
            grad_up[:, :, :, :, :, cols] = up_part.reshape(grad_up.shape[:-1] + (C,))
            back = dot_nt(grad_bf[...], up)
            grad_rows[...] = grad_rows[...] + back.reshape(windows, PAD, C)
            return carry

        lax.fori_loop(first, last, one, 0)

    def mix_back(layer_no):
        flow = token_rows(rows_bf)
        back = dot_nt(flow, whole(weights[layer_no][1], 0, C)).astype(BF16)
        more_bf[...] = back.reshape(windows, PAD, C)

    def out_grads(layer_no):
        part = dot_tn(token_rows(context[layer_no]), token_rows(rows_bf)).astype(BF16)
        grad_out = grads[layer_no][1]
        grad_out[...] = part.reshape(grad_out.shape)

    def project_back(layer_no):
        rows = token_rows(inputs[layer_no])
        grad_in = grads[layer_no][0]
        for low in range(0, 3 * C, C):
            part = grad_packed[:, :, low : low + C].reshape(tokens, C)
            weight_part = dot_tn(rows, part).astype(BF16)
            grad_in[:, :, :, :, :, low : low + C] = weight_part.reshape(
                grad_in.shape[:-1] + (C,)
            )

    def project_rows_back(layer_no):
        total = None
        for low in range(0, 3 * C, C):
            part = grad_packed[:, :, low : low + C].reshape(tokens, C)
            back = dot_nt(part, whole(weights[layer_no][0], low, low + C))
            total = back if total is None else total + back
        grad_rows[...] = total.reshape(windows, PAD, C)

    in1, up1, down1 = scatters[1]
    in0, up0, down0 = scatters[0]

    sums[1, 11:12, :] = flow_sum
    for layer_no in range(LAYERS):
        sums[layer_no, 12:16, :] = jnp.zeros((4, C), F32)
    down_grads(1)
    down1.start()
    feed_back(1, 0, depth_z)
    down1.first()
    sums[1, 4:5, :] = normalize_back(grad_rows, vec(1, 5), xhat2[1], scale2[1], 1, 5)
    mix_back(1)
    halo_sent.append(enter_start(more_bf, 2))
    out_grads(1)
    up1.start()
    down1.second()
    halo_sent[-1].wait_recv()
    move(more_bf, 2, 0, rows_bf)
    halo_sent[-1].wait_send()
    up1.first()

    def attend_back(layer_no, source, first, last):
        attend_windows_back(
            packed[layer_no],
            probs[layer_no],
            source,
            grad_packed,
            tables.at[layer_no],
            sums.at[layer_no],
            first,
            last,
        )

    attend_back(1, rows_bf, 0, half)
    down1.third()
    up1.second()
    attend_back(1, rows_bf, half, windows)
    down1.fourth()
    project_rows_back(1)

    def split(w, carry):
        high = grad_rows[w].astype(BF16)
        rows_bf[w] = high
        more_bf[w] = (grad_rows[w] - high.astype(F32)).astype(BF16)
        return carry

    lax.fori_loop(0, windows, split, 0)
    halo_sent.append(leave_start(rows_bf, 3, 0, windows))
    up1.third()
    project_back(1)
    in1.start()
    halo_sent[-1].wait_recv()
    for image in range(images):
        rest = more_bf[2 * image : 2 * image + 2].reshape(2 * PAD, C)
        value = moved(rows_bf, 3, 1, image) + jnp.dot(
            perm_ref[2], rest, preferred_element_type=F32
        )
        grad_rows[2 * image : 2 * image + 2] = value.reshape(2, PAD, C)
    halo_sent[-1].wait_send()
    flow_sum = normalize_back(grad_rows, vec(1, 0), xhat1[1], scale1[1], 1, 0)
    in1.first()
    down1.finish()

    for item in queue:
        item.drain()
    table_sums([tables.at[1]], index_ref, sums.at[1])
    high_sums = Total(links, 1, sums, sum_buffers)
    high_sums.start()
    sums[0, 11:12, :] = flow_sum
    down_grads(0)
    down0.start()
    up1.fourth()
    feed_back(0, 0, half_z)
    in1.second()
    high_sums.second()
    feed_back(0, half_z, depth_z)
    down0.first()
    in1.third()
    up1.finish()
    high_sums.third()
    sums[0, 4:5, :] = normalize_back(grad_rows, vec(0, 5), xhat2[0], scale2[0], 0, 5)
    out_grads(0)
    up0.start()
    mix_back(0)
    down0.second()
    high_sums.fourth()
    attend_back(0, more_bf, 0, half)
    in1.fourth()
    up0.first()
    down0.third()
    attend_back(0, more_bf, half, windows)
    high_sums.finish(totals)
    project_back(0)
    in0.start()
    up0.second()
    down0.fourth()
    project_rows_back(0)
    in1.finish()
    normalize_back(grad_rows, vec(0, 0), xhat1[0], scale1[0], 0, 0)
    table_sums([tables.at[0]], index_ref, sums.at[0])
    low_sums = Total(links, 0, sums, sum_buffers)
    low_sums.start()
    in0.first()
    down0.finish()
    up0.third()

    join_rows(grad_flow, input_grad_ref)
    low_sums.second()
    in0.second()
    low_sums.third()
    up0.fourth()
    in0.third()
    low_sums.fourth()
    up0.finish()
    in0.fourth()
    low_sums.finish(totals)
    take_vectors(totals, first_rows, owner, owners, vec_outs)
    table_out[...] = totals[:, TABLE_ROW:, :]
    in0.finish()
    for step in vec_sent:
        step.wait_send()
    for item in [high_sums, low_sums] + scatters[0] + scatters[1]:
        item.drain()


def shift_matrices():
    spots = 2 * PAD
    kinds = np.zeros((4, spots, spots), np.float32)
    for w in range(2):
        for row in range(WIN):
            for col in range(WIN):
                here = w * PAD + row * SIDE + col
                keep = WIN - SHIFT
                from_w, from_col = (w, col + SHIFT) if col < keep else (1 - w, col - keep)
                if row < keep:
                    there = from_w * PAD + (row + SHIFT) * SIDE + from_col
                    kinds[0, here, there] = 1
                    kinds[2, there, here] = 1
                else:
                    there = from_w * HALF_SEND + (row - keep) * SIDE + from_col
                    kinds[1, here, there] = 1
                    source = w * HALF_SEND + (row - keep) * SIDE + col
                    kinds[3, from_w * PAD + (row - keep) * SIDE + from_col, source] = 1
    return kinds


def hand_over(*refs):
    count = len(refs) // 2
    for source, target in zip(refs[:count], refs[count:]):
        target[...] = source[...]


def one_kernel_fits(owners, depth, down_depth, ff):
    return owners % 4 == 0 and depth % 32 == 0 and down_depth % 32 == 0 and ff == owners // 4 * C


def per_device(*args):
    attn_in_weight, mlp_in_weight, mlp_out_weight = args[2], args[4], args[5]
    sizes = (attn_in_weight.shape[1], mlp_out_weight.shape[1], mlp_in_weight.shape[2])
    if one_kernel_fits(lax.axis_size("dp"), *sizes) and lax.axis_size("rows") == 2:
        return per_device_one_kernel(*args)
    return per_device_general(*args)


def per_device_one_kernel(images, cotangent, *rest):
    shards, vectors = rest[:4], rest[4:12]
    bias_table, region_labels, table_index = rest[12:]
    owners = lax.axis_size("dp")
    depth_z = owners // 4
    owner = lax.axis_index("dp")
    widths = [member.shape[1] for member in vectors]

    def pad_window(values, fill):
        grid = values.reshape(values.shape[:-1] + (WIN, WIN))
        pads = [(0, 0)] * (values.ndim - 1) + [(0, SIDE - WIN)] * 2
        return jnp.pad(grid, pads, constant_values=fill).reshape(values.shape[:-1] + (PAD,))

    def pad_pair(values, fill):
        both = pad_window(jnp.swapaxes(pad_window(values, fill), -1, -2), fill)
        return jnp.swapaxes(both, -1, -2)

    sides = GRID // WIN
    labels = region_labels.reshape(sides, WIN, sides, WIN).transpose(0, 2, 1, 3)
    labels = pad_window(labels.reshape(sides * sides, WIN * WIN), -1)
    labels = jnp.pad(labels, ((0, 8 - labels.shape[0]), (0, 0)), constant_values=-1)
    index_keys = pad_pair(table_index, 0).T[:KEYS]
    entries = jnp.pad(bias_table, ((0, 0), (0, TABLE_COLS - REL), (0, 0)))
    entries = entries.reshape(LAYERS, TABLE_COLS, 2 * GROUPS, 2).transpose(3, 0, 2, 1)
    entries = entries.reshape(-1, TABLE_COLS)
    perms = jnp.asarray(shift_matrices(), BF16)

    windows = images.shape[0] * sides
    tokens = windows * PAD
    split_shards = [shard.reshape(LAYERS, 2, shard.shape[1] // 2, -1) for shard in shards]
    shapes = [(depth_z, 2, 2, 2) + shard.shape[2:] for shard in split_shards]
    ff = shapes[2][-1]

    def rows_of(width, dtype):
        return pltpu.VMEM((windows, PAD, width), dtype)

    scratch = []
    for _ in range(LAYERS):
        scratch += [pltpu.VMEM(shape, BF16) for shape in shapes]
    scratch += [pltpu.VMEM(shape, BF16) for shape in shapes]
    scratch += [rows_of(C, F32)] * 4 + [rows_of(1, F32)] * 4
    scratch += [rows_of(C, BF16)] * 2 + [rows_of(3 * C, BF16)] * 2
    scratch += [pltpu.VMEM((windows * GROUPS, KEYS, WIDE), F32)] * 2
    scratch += [rows_of(C, BF16)] * 4 + [rows_of(ff, BF16)] * 4
    scratch += [rows_of(C, F32)] * 3 + [rows_of(C, BF16)] * 2
    scratch += [pltpu.VMEM((4, windows, HALF_SEND, C), BF16)]
    scratch += [rows_of(3 * C, BF16), pltpu.VMEM((tokens, C), BF16)]
    scratch += [pltpu.VMEM((LAYERS, 2 * GROUPS, KEYS, LANES), F32)]
    for _ in range(LAYERS):
        for which, width in ((0, 3 * C), (2, ff), (1, C), (3, C)):
            width = width // 2
            tail = (shapes[which][-2], width)
            leads = [(depth_z, 2, 2), (depth_z, 2), (depth_z,), (depth_z - 1,), (), ()]
            scratch += [pltpu.VMEM(lead + tail, BF16) for lead in leads * 2]
    scratch += [pltpu.VMEM((VEC_ROWS, C), F32)] + [pltpu.VMEM((VEC_ROWS, C), BF16)] * 5
    scratch += [pltpu.VMEM((depth_z, VEC_ROWS, C), BF16)]
    scratch += [pltpu.VMEM((LAYERS * 2 * GROUPS, KEYS, LANES), F32)]
    scratch += [pltpu.VMEM((3, KEYS, LANES), F32), pltpu.VMEM((LAYERS, SUM_ROWS, C), F32)]
    scratch += [pltpu.VMEM((LAYERS, SUM_ROWS, C), F32)] * 7
    scratch += [pltpu.VMEM((LAYERS, depth_z, SUM_ROWS, C), F32)]
    sems = 2 * 8 * (2 * (depth_z + 2) + 1) + 3 * (depth_z + 2) + 9
    scratch += [pltpu.SemaphoreType.DMA((sems,))] * 2

    out_shape = [
        jax.ShapeDtypeStruct(images.shape, BF16),
        jax.ShapeDtypeStruct(images.shape, F32),
        *(jax.ShapeDtypeStruct(shard.shape, F32) for shard in split_shards),
        *(jax.ShapeDtypeStruct(member.shape, F32) for member in vectors),
        jax.ShapeDtypeStruct((LAYERS, SUM_ROWS - TABLE_ROW, C), F32),
    ]
    operands = (images, cotangent, *split_shards, *vectors)
    operands += (entries, index_keys, labels, perms)
    results = pl.pallas_call(
        lambda *refs: training_kernel(depth_z, *refs),
        out_shape=out_shape,
        in_specs=in_vmem(len(operands)),
        out_specs=in_vmem(len(out_shape)),
        scratch_shapes=scratch,
        compiler_params=pltpu.CompilerParams(
            collective_id=0, has_side_effects=True, vmem_limit_bytes=VMEM_BYTES
        ),
    )(*operands)
    final, input_grad, *rest, table = pl.pallas_call(
        hand_over,
        out_shape=out_shape,
        in_specs=in_vmem(len(out_shape)),
        out_specs=in_vmem(len(out_shape)),
    )(*results)
    weight_grads, vector_outs = rest[:4], rest[4:]
    table = table.reshape(LAYERS, 2 * GROUPS, 2, TABLE_COLS)
    table = table.transpose(0, 3, 1, 2).reshape(LAYERS, TABLE_COLS, HEADS)[:, :REL]
    return (
        final,
        input_grad,
        *(grad.reshape(shard.shape) for grad, shard in zip(weight_grads, shards)),
        *vector_outs,
        table,
    )


def solution(mesh):
    return jax.shard_map(
        per_device,
        mesh=mesh,
        in_specs=(
            P("dp", "rows", None, None),
            P("dp", "rows", None, None),
            P(None, "dp", None),
            P(None, "dp", None),
            P(None, "dp", None),
            P(None, "dp", None),
            P(None, "dp"),
            P(None, "dp"),
            P(None, "dp"),
            P(None, "dp"),
            P(None, "dp"),
            P(None, "dp"),
            P(None, "dp"),
            P(None, "dp"),
            P(),
            P(),
            P(),
        ),
        out_specs=(
            P("dp", "rows", None, None),
            P("dp", "rows", None, None),
            P(None, "dp", None),
            P(None, "dp", None),
            P(None, "dp", None),
            P(None, "dp", None),
            P(None, "dp"),
            P(None, "dp"),
            P(None, "dp"),
            P(None, "dp"),
            P(None, "dp"),
            P(None, "dp"),
            P(None, "dp"),
            P(None, "dp"),
            P(),
        ),
        check_vma=False,
    )
```
